32 devices in a mesh: fsdp: 8 (over y, x, core), seq: 4 (over z).
Axes of the slice: x: 2, y: 2, z: 4, core: 2. Of those that a mesh axis runs over, the one named last changes fastest.
Arguments:
- tokens: bfloat16 [12288, 1024], P(('fsdp', 'seq')), may hold values from -6 to 6
- segment_ids: int32 [12288], P(('fsdp', 'seq')), may hold values from -1 to 1, as said below
- ln1_gain: bfloat16 [1024], P('fsdp'), may hold values from 0.099609375 to 1.8984375
- ln1_bias: bfloat16 [1024], P('fsdp'), may hold values from -3 to 3
- w_qkv: bfloat16 [1024, 3072], P('fsdp'), may hold values from -0.1875 to 0.1875
- q_bias: bfloat16 [1024], P('fsdp'), may hold values from -3 to 3
- v_bias: bfloat16 [1024], P('fsdp'), may hold values from -3 to 3
- w_out: bfloat16 [1024, 1024], P('fsdp'), may hold values from -0.75 to 0.75
- out_bias: bfloat16 [1024], P('fsdp'), may hold values from -3 to 3
- ln2_gain: bfloat16 [1024], P('fsdp'), may hold values from 0.099609375 to 1.8984375
- ln2_bias: bfloat16 [1024], P('fsdp'), may hold values from -3 to 3
- w_fc1: bfloat16 [1024, 4096], P('fsdp'), may hold values from -0.1875 to 0.1875
- fc1_bias: bfloat16 [4096], P('fsdp'), may hold values from -3 to 3
- w_fc2: bfloat16 [4096, 1024], P('fsdp'), may hold values from -0.09375 to 0.09375
- fc2_bias: bfloat16 [1024], P('fsdp'), may hold values from -3 to 3
- cotangent: bfloat16 [12288, 1024], P(('fsdp', 'seq')), may hold values from -6 to 6
Outputs:
- layer_output: bfloat16 [12288, 1024], P(('fsdp', 'seq'))
- tokens_grad: float32 [12288, 1024], P(('fsdp', 'seq'))
- ln1_gain_grad: float32 [1024], P(('fsdp', 'seq'))
- ln1_bias_grad: float32 [1024], P(('fsdp', 'seq'))
- w_qkv_grad: float32 [1024, 3072], P('fsdp', 'seq')
- q_bias_grad: float32 [1024], P(('fsdp', 'seq'))
- v_bias_grad: float32 [1024], P(('fsdp', 'seq'))
- w_out_grad: float32 [1024, 1024], P('fsdp', 'seq')
- out_bias_grad: float32 [1024], P(('fsdp', 'seq'))
- ln2_gain_grad: float32 [1024], P(('fsdp', 'seq'))
- ln2_bias_grad: float32 [1024], P(('fsdp', 'seq'))
- w_fc1_grad: float32 [1024, 4096], P('fsdp', 'seq')
- fc1_bias_grad: float32 [4096], P(('fsdp', 'seq'))
- w_fc2_grad: float32 [4096, 1024], P('fsdp', 'seq')
- fc2_bias_grad: float32 [1024], P(('fsdp', 'seq'))
The draws below stay inside these ranges and needn't reach their ends.
Inputs may be any that keep to these rules, and one draw needn't show every extreme that they name: `segment_ids`: each span of 1536 slots (one index of fsdp) holds whole images of 577 slots from its first slot on, numbered 0, 1, 2, ... within the span, then padding slots marked -1; every span holds at least half of 2 images and some span holds 2.
All inputs are finite; a program needn't handle non-finite values.
Results may differ from the reference program's by a relative error of at most 0.019.
Values may be sent and summed in bfloat16 or wider, within the bound.
No kernel may reach another device: no remote copies, remote signals or barrier semaphores. Data moves between devices by JAX's collectives and lax.ppermute only.
A program may use at most 192 MiB of HBM per device.

```python
import jax
import jax.numpy as jnp
from jax import lax

D = 1024
HEADS = 16
HD = 64
FF = 4096
LEN = 577
SPAN = 1536
SPANS = 8
TOKENS = 12288
IMG_MAX = 2


def draw_segment_ids(key, part):
    count_key = jax.random.fold_in(key, 11)
    fullest_key = jax.random.fold_in(key, 23)
    counts = jax.random.randint(count_key, (SPANS,), (IMG_MAX + 1) // 2, IMG_MAX + 1)
    fullest = jax.random.randint(fullest_key, (), 0, SPANS)
    counts = jnp.where(jnp.arange(SPANS) == fullest, IMG_MAX, counts)
    places = jnp.arange(SPAN)
    labels = jnp.where(places[None, :] < (counts * LEN)[:, None], places[None, :] // LEN, -1)
    return labels.reshape(SPAN * SPANS).astype(jnp.int32)


def level_of(own_key, dims, pieces, low, top_value):
    def one(position, parts):
        draws = jax.random.uniform(jax.random.fold_in(jax.random.fold_in(own_key, 6), position), (parts,), jnp.float32, low / len(pieces), top_value / len(pieces))
        return jnp.repeat(jnp.exp(draws), dims[position] // parts).reshape((-1,) + (1,) * (len(dims) - position - 1))

    factor_of = one(*pieces[0])
    for cut in pieces[1:]:
        factor_of = factor_of * one(*cut)
    return factor_of


def gaussian(own_key, shape, scale, most, shards=(), held_as=jnp.bfloat16):
    drawn = jax.random.normal(own_key, shape, jnp.float32) * scale
    if len(shards) > 0:
        drawn = level_of(own_key, shape, shards, -0.22, 0.18) * drawn
    return jnp.clip(drawn, min=-most, max=most).astype(held_as)


def setup_inputs(seed: int = 0) -> dict:
    seeds = jax.random.split(jax.random.key(seed), 17)
    return {
        "tokens": gaussian(seeds[0], (TOKENS, D), 1.0, 6.0, ((0, 32),)),
        "segment_ids": draw_segment_ids(jax.random.fold_in(seeds[16], 71), 0),
        "ln1_gain": jnp.clip(1.0 + 0.18 * jax.random.normal(seeds[2], (D,), jnp.float32), 0.099609375, 1.8984375).astype(jnp.bfloat16),
        "ln1_bias": gaussian(seeds[3], (D,), 0.5, 3.0, ((0, 8),)),
        "w_qkv": gaussian(seeds[4], (D, 3 * D), D ** -0.5, 0.1875, ((0, 8),)),
        "q_bias": gaussian(seeds[5], (D,), 0.5, 3.0, ((0, 8),)),
        "v_bias": gaussian(seeds[6], (D,), 0.5, 3.0, ((0, 8),)),
        "w_out": gaussian(seeds[7], (D, D), (D // 16) ** -0.5, 0.75, ((0, 8),)),
        "out_bias": gaussian(seeds[8], (D,), 0.4, 3.0, ((0, 8),)),
        "ln2_gain": jnp.clip(1.0 + 0.18 * jax.random.normal(seeds[9], (D,), jnp.float32), 0.099609375, 1.8984375).astype(jnp.bfloat16),
        "ln2_bias": gaussian(seeds[10], (D,), 0.5, 3.0, ((0, 8),)),
        "w_fc1": gaussian(seeds[11], (D, FF), D ** -0.5, 0.1875, ((0, 8),)),
        "fc1_bias": gaussian(seeds[12], (FF,), 0.5, 3.0, ((0, 8),)),
        "w_fc2": gaussian(seeds[13], (FF, D), FF ** -0.5, 0.09375, ((0, 8),)),
        "fc2_bias": gaussian(seeds[14], (D,), 0.4, 3.0, ((0, 8),)),
        "cotangent": gaussian(seeds[15], (TOKENS, D), 1.0, 6.0, ((0, 32),)),
    }


norm_eps = 1e-06
masked_score = -1000000000.0
highest = lax.Precision.HIGHEST

@jax.custom_vjp
def low(v):
    return lax.optimization_barrier(v.astype(jnp.bfloat16)).astype(jnp.float32)

@jax.custom_vjp
def low_back(v):
    return v

def low_keep(v):
    return (low(v), None)

def low_pass(kept, grad):
    return (grad,)

def back_keep(v):
    return (v, None)

def back_low(kept, grad):
    return (low(grad),)
low.defvjp(low_keep, low_pass)
low_back.defvjp(back_keep, back_low)

def matmul(left, right):
    return jnp.dot(left, right, precision=highest)

def normalize(values, gain, shift):
    row_mean = lax.optimization_barrier(jnp.mean(values, axis=-1, keepdims=True))
    centered = values - row_mean
    variance = lax.optimization_barrier(jnp.mean(centered * centered, axis=-1, keepdims=True))
    return centered * lax.rsqrt(variance + norm_eps) * gain + shift

def attend_one(packed):
    queries, key_rows, values, labels = packed
    scaled = jnp.dot(queries, key_rows.T, precision=highest) * HD ** (-0.5)
    same_image = labels[:, None] == labels[None, :]
    scores = low_back(jnp.where(same_image, scaled, masked_score))
    attn_probs = low(jax.nn.softmax(scores, axis=-1))
    return low_back(low(jnp.dot(attn_probs, values, precision=highest)))

def split_heads(matrix):
    return matrix.reshape(SPANS, SPAN, HEADS, HD).transpose(0, 2, 1, 3).reshape(SPANS * HEADS, SPAN, HD)

def merge_heads(stacked):
    return stacked.reshape(SPANS, HEADS, SPAN, HD).transpose(0, 2, 1, 3).reshape(TOKENS, D)

def forward(inputs, segment_ids, ln1_gain, ln1_bias, w_qkv, q_bias, v_bias, w_out, out_bias, ln2_gain, ln2_bias, w_fc1, fc1_bias, w_fc2, fc2_bias):
    first_norm = low(normalize(inputs, ln1_gain, ln1_bias))
    projected = matmul(first_norm, w_qkv)
    queries = low_back(low(projected[:, :D] + q_bias))
    key_rows = low_back(low(projected[:, D:2 * D]))
    values = low_back(low(projected[:, 2 * D:] + v_bias))
    labels = jnp.repeat(segment_ids.reshape(SPANS, SPAN), HEADS, axis=0)
    attended = lax.map(jax.checkpoint(attend_one), (split_heads(queries), split_heads(key_rows), split_heads(values), labels))
    attended = merge_heads(attended)
    mixed = low_back(matmul(attended, w_out) + out_bias)
    middle = inputs + mixed
    second_norm = low(normalize(middle, ln2_gain, ln2_bias))
    hidden = low_back(matmul(second_norm, w_fc1) + fc1_bias)
    activated = low(jax.nn.gelu(hidden, approximate=False))
    branch = low_back(matmul(activated, w_fc2) + fc2_bias)
    valid = (segment_ids >= 0).astype(jnp.float32)[:, None]
    return valid * (middle + branch)

def reference(tokens, segment_ids, ln1_gain, ln1_bias, w_qkv, q_bias, v_bias, w_out, out_bias, ln2_gain, ln2_bias, w_fc1, fc1_bias, w_fc2, fc2_bias, cotangent):
    params = [p.astype(jnp.float32) for p in (ln1_gain, ln1_bias, w_qkv, q_bias, v_bias, w_out, out_bias, ln2_gain, ln2_bias, w_fc1, fc1_bias, w_fc2, fc2_bias)]

    def apply(inputs, *weights):
        return forward(inputs, segment_ids, *weights)
    result, pullback = jax.vjp(apply, tokens.astype(jnp.float32), *params)
    grads = pullback(cotangent.astype(jnp.float32))
    return (result.astype(jnp.bfloat16), grads[0], grads[1], grads[2], grads[3], grads[4], grads[5], grads[6], grads[7], grads[8], grads[9], grads[10], grads[11], grads[12], grads[13])
```

```python
from functools import partial

import jax
import jax.numpy as jnp
from jax import lax
from jax.experimental import pallas as pl
from jax.experimental.pallas import tpu as pltpu
from jax.sharding import PartitionSpec as P

HD = 64
LEN = 577


norm_eps = 1e-06
masked_score = -1000000000.0


def normalize(values, gain, shift):
    row_mean = jnp.mean(values, axis=-1, keepdims=True)
    centered = values - row_mean
    variance = jnp.mean(centered * centered, axis=-1, keepdims=True)
    return centered * lax.rsqrt(variance + norm_eps) * gain + shift


def contract_rows(left, right):
    return lax.dot_general(
        left, right, (((0,), (0,)), ((), ())), preferred_element_type=jnp.float32
    )


def times_transposed(left, right):
    return lax.dot_general(
        left, right, (((1,), (1,)), ((), ())), preferred_element_type=jnp.float32
    )


def column_sum(values):
    return jnp.sum(values, axis=0, dtype=jnp.float32)


def shards_per_block(row_count, seq_count):
    for factor in range(1, seq_count + 1):
        if seq_count % factor == 0 and (row_count * factor >= 512 or factor == seq_count):
            return factor
    return seq_count


def add_window(total, delta, start):
    current = lax.dynamic_slice_in_dim(total, start, delta.shape[0], 0)
    return lax.dynamic_update_slice_in_dim(total, current + delta, start, 0)


def general_shards(
    tokens,
    segment_ids,
    ln1_gain,
    ln1_bias,
    w_qkv,
    q_bias,
    v_bias,
    w_out,
    out_bias,
    ln2_gain,
    ln2_bias,
    w_fc1,
    fc1_bias,
    w_fc2,
    fc2_bias,
    cotangent,
):
    row_count = tokens.shape[0]
    feature_width = tokens.shape[1]
    seq_count = lax.axis_size("seq")
    span_rows = row_count * seq_count
    local_heads = feature_width // seq_count // HD
    block_rows = row_count * shards_per_block(row_count, seq_count)
    block_count = span_rows // block_rows
    margin = LEN - 1
    window = block_rows + 2 * margin
    offsets = jnp.arange(block_count, dtype=jnp.int32) * block_rows
    scale = HD ** (-0.5)
    as_float = jnp.float32

    def weight_grad(left, right):
        return contract_rows(left, right)

    attn_set = (
        lax.all_gather(ln1_gain, "fsdp", axis=0, tiled=True),
        lax.all_gather(ln1_bias, "fsdp", axis=0, tiled=True),
        lax.all_gather(w_qkv, "fsdp", axis=0, tiled=True),
        lax.all_gather(q_bias, "fsdp", axis=0, tiled=True),
        lax.all_gather(v_bias, "fsdp", axis=0, tiled=True),
        lax.all_gather(w_out, "fsdp", axis=0, tiled=True),
        lax.all_gather(out_bias, "fsdp", axis=0, tiled=True),
    )
    span_labels = lax.all_gather(segment_ids, "seq", axis=0, tiled=True)
    inputs = tokens.astype(as_float)
    gain_one = attn_set[0].astype(as_float)
    shift_one = attn_set[1].astype(as_float)
    first_norm = normalize(inputs, gain_one, shift_one).astype(jnp.bfloat16)
    projected = jnp.dot(first_norm, attn_set[2], preferred_element_type=as_float)
    bias_all = jnp.concatenate(
        [
            attn_set[3].astype(as_float),
            jnp.zeros((feature_width,), as_float),
            attn_set[4].astype(as_float),
        ]
    )
    packed = (projected + bias_all).astype(jnp.bfloat16).reshape(row_count, 3, feature_width)
    head_rows = lax.all_to_all(packed, "seq", split_axis=2, concat_axis=0, tiled=True)
    query_heads = head_rows[:, 0, :].reshape(span_rows, local_heads, HD)
    key_heads = head_rows[:, 1, :].reshape(span_rows, local_heads, HD)
    value_heads = head_rows[:, 2, :].reshape(span_rows, local_heads, HD)
    key_padded = jnp.pad(key_heads, ((margin, margin), (0, 0), (0, 0)))
    value_padded = jnp.pad(value_heads, ((margin, margin), (0, 0), (0, 0)))
    label_padded = jnp.pad(span_labels, (margin, margin), constant_values=-2)

    def block_scores(offset):
        query_block = lax.dynamic_slice_in_dim(query_heads, offset, block_rows, 0)
        label_block = lax.dynamic_slice_in_dim(span_labels, offset, block_rows, 0)
        key_window = lax.dynamic_slice_in_dim(key_padded, offset, window, 0)
        value_window = lax.dynamic_slice_in_dim(value_padded, offset, window, 0)
        label_window = lax.dynamic_slice_in_dim(label_padded, offset, window, 0)
        scaled = (
            jnp.einsum("qhd,khd->hqk", query_block, key_window, preferred_element_type=as_float)
            * scale
        )
        same_image = label_block[:, None] == label_window[None, :]
        return (
            query_block,
            key_window,
            value_window,
            jnp.where(same_image[None], scaled, masked_score),
        )

    def block_forward(offset):
        unused_query, unused_key, value_window, scores = block_scores(offset)
        row_peak = jnp.max(scores, axis=-1, keepdims=True)
        lifted = jnp.exp(scores - row_peak)
        row_total = jnp.sum(lifted, axis=-1, keepdims=True)
        attn_probs = (lifted / row_total).astype(jnp.bfloat16)
        block_out = jnp.einsum(
            "hqk,khd->qhd", attn_probs, value_window, preferred_element_type=as_float
        ).astype(jnp.bfloat16)
        return (block_out, (row_peak + jnp.log(row_total))[..., 0])

    head_out, log_totals = lax.map(block_forward, offsets)
    head_flat = head_out.reshape(span_rows, local_heads * HD)
    attended = lax.all_to_all(head_flat, "seq", split_axis=0, concat_axis=1, tiled=True)
    mixed = jnp.dot(attended, attn_set[5], preferred_element_type=as_float) + attn_set[6].astype(
        as_float
    )
    middle = inputs + mixed
    mlp_set = (
        lax.all_gather(ln2_gain, "fsdp", axis=0, tiled=True),
        lax.all_gather(ln2_bias, "fsdp", axis=0, tiled=True),
        lax.all_gather(w_fc1, "fsdp", axis=0, tiled=True),
        lax.all_gather(fc1_bias, "fsdp", axis=0, tiled=True),
        lax.all_gather(w_fc2, "fsdp", axis=0, tiled=True),
        lax.all_gather(fc2_bias, "fsdp", axis=0, tiled=True),
    )
    gain_two = mlp_set[0].astype(as_float)
    shift_two = mlp_set[1].astype(as_float)
    second_norm = normalize(middle, gain_two, shift_two).astype(jnp.bfloat16)
    hidden = jnp.dot(second_norm, mlp_set[2], preferred_element_type=as_float) + mlp_set[3].astype(
        as_float
    )
    activated = jax.nn.gelu(hidden, approximate=False).astype(jnp.bfloat16)
    branch = jnp.dot(activated, mlp_set[4], preferred_element_type=as_float) + mlp_set[5].astype(
        as_float
    )
    valid = (segment_ids >= 0).astype(as_float)[:, None]
    layer_output = (valid * (middle + branch)).astype(jnp.bfloat16)
    grad_out = valid * cotangent.astype(as_float)
    grad_branch = grad_out.astype(jnp.bfloat16)
    fc2_bias_part = column_sum(grad_branch)
    w_fc2_part = weight_grad(activated, grad_branch)
    grad_act = times_transposed(grad_branch, mlp_set[4])
    unused_hidden, gelu_back = jax.vjp(partial(jax.nn.gelu, approximate=False), hidden)
    grad_hidden = gelu_back(grad_act)[0].astype(jnp.bfloat16)
    fc1_bias_part = column_sum(grad_hidden)
    w_fc1_part = weight_grad(second_norm, grad_hidden)
    grad_norm_two = times_transposed(grad_hidden, mlp_set[2])
    unused_two, norm_two_back = jax.vjp(
        normalize, middle, mlp_set[0].astype(as_float), mlp_set[1].astype(as_float)
    )
    grad_mid_norm, ln2_gain_part, ln2_bias_part = norm_two_back(grad_norm_two)
    grad_middle = grad_out + grad_mid_norm
    grad_mixed = grad_middle.astype(jnp.bfloat16)
    out_bias_part = column_sum(grad_mixed)
    w_out_part = weight_grad(attended, grad_mixed)
    grad_attended = times_transposed(grad_mixed, attn_set[5]).astype(jnp.bfloat16)
    grad_heads = lax.all_to_all(
        grad_attended, "seq", split_axis=1, concat_axis=0, tiled=True
    ).reshape(span_rows, local_heads, HD)

    def block_backward(running, inputs_block):
        key_total, value_total = running
        offset, log_block = inputs_block
        query_block, key_window, value_window, scores = block_scores(offset)
        grad_block = lax.dynamic_slice_in_dim(grad_heads, offset, block_rows, 0)
        probs_full = jnp.exp(scores - log_block[..., None])
        attn_probs = probs_full.astype(jnp.bfloat16)
        value_delta = jnp.einsum(
            "hqk,qhd->khd", attn_probs, grad_block, preferred_element_type=as_float
        )
        grad_probs = jnp.einsum(
            "qhd,khd->hqk", grad_block, value_window, preferred_element_type=as_float
        )
        row_inner = jnp.sum(grad_probs * probs_full, axis=-1, keepdims=True)
        grad_scores = (probs_full * (grad_probs - row_inner)).astype(jnp.bfloat16)
        grad_query = (
            jnp.einsum("hqk,khd->qhd", grad_scores, key_window, preferred_element_type=as_float)
            * scale
        )
        key_delta = (
            jnp.einsum("hqk,qhd->khd", grad_scores, query_block, preferred_element_type=as_float)
            * scale
        )
        return (
            (
                add_window(key_total, key_delta, offset),
                add_window(value_total, value_delta, offset),
            ),
            grad_query,
        )

    zero_heads = jnp.zeros((span_rows + 2 * margin, local_heads, HD), as_float)
    (key_padded_grad, value_padded_grad), query_grad = lax.scan(
        block_backward, (zero_heads, zero_heads), (offsets, log_totals)
    )
    key_grad = key_padded_grad[margin : margin + span_rows]
    value_grad = value_padded_grad[margin : margin + span_rows]
    head_grads = jnp.concatenate(
        [
            query_grad.reshape(span_rows, 1, local_heads * HD),
            key_grad.reshape(span_rows, 1, local_heads * HD),
            value_grad.reshape(span_rows, 1, local_heads * HD),
        ],
        axis=1,
    ).astype(jnp.bfloat16)
    token_grads = lax.all_to_all(
        head_grads, "seq", split_axis=0, concat_axis=2, tiled=True
    ).reshape(row_count, 3 * feature_width)
    q_bias_part = column_sum(token_grads[:, :feature_width])
    v_bias_part = column_sum(token_grads[:, 2 * feature_width :])
    w_qkv_part = weight_grad(first_norm, token_grads)
    grad_norm_one = times_transposed(token_grads, attn_set[2])
    unused_one, norm_one_back = jax.vjp(
        normalize, inputs, attn_set[0].astype(as_float), attn_set[1].astype(as_float)
    )
    grad_input_norm, ln1_gain_part, ln1_bias_part = norm_one_back(grad_norm_one)
    tokens_grad = grad_middle + grad_input_norm
    partial_sums = (
        lax.psum_scatter(
            ln1_gain_part.astype(jnp.bfloat16), "fsdp", scatter_dimension=0, tiled=True
        ).astype(jnp.float32),
        lax.psum_scatter(
            ln1_bias_part.astype(jnp.bfloat16), "fsdp", scatter_dimension=0, tiled=True
        ).astype(jnp.float32),
        lax.psum_scatter(
            w_qkv_part.astype(jnp.bfloat16), "fsdp", scatter_dimension=0, tiled=True
        ).astype(jnp.float32),
        lax.psum_scatter(
            q_bias_part.astype(jnp.bfloat16), "fsdp", scatter_dimension=0, tiled=True
        ).astype(jnp.float32),
        lax.psum_scatter(
            v_bias_part.astype(jnp.bfloat16), "fsdp", scatter_dimension=0, tiled=True
        ).astype(jnp.float32),
        lax.psum_scatter(
            w_out_part.astype(jnp.bfloat16), "fsdp", scatter_dimension=0, tiled=True
        ).astype(jnp.float32),
        lax.psum_scatter(
            out_bias_part.astype(jnp.bfloat16), "fsdp", scatter_dimension=0, tiled=True
        ).astype(jnp.float32),
        lax.psum_scatter(
            ln2_gain_part.astype(jnp.bfloat16), "fsdp", scatter_dimension=0, tiled=True
        ).astype(jnp.float32),
        lax.psum_scatter(
            ln2_bias_part.astype(jnp.bfloat16), "fsdp", scatter_dimension=0, tiled=True
        ).astype(jnp.float32),
        lax.psum_scatter(
            w_fc1_part.astype(jnp.bfloat16), "fsdp", scatter_dimension=0, tiled=True
        ).astype(jnp.float32),
        lax.psum_scatter(
            fc1_bias_part.astype(jnp.bfloat16), "fsdp", scatter_dimension=0, tiled=True
        ).astype(jnp.float32),
        lax.psum_scatter(
            w_fc2_part.astype(jnp.bfloat16), "fsdp", scatter_dimension=0, tiled=True
        ).astype(jnp.float32),
        lax.psum_scatter(
            fc2_bias_part.astype(jnp.bfloat16), "fsdp", scatter_dimension=0, tiled=True
        ).astype(jnp.float32),
    )
    summed = (
        lax.psum_scatter(
            partial_sums[0].astype(jnp.bfloat16), "seq", scatter_dimension=0, tiled=True
        ).astype(jnp.float32),
        lax.psum_scatter(
            partial_sums[1].astype(jnp.bfloat16), "seq", scatter_dimension=0, tiled=True
        ).astype(jnp.float32),
        lax.psum_scatter(
            partial_sums[2].astype(jnp.bfloat16), "seq", scatter_dimension=1, tiled=True
        ).astype(jnp.float32),
        lax.psum_scatter(
            partial_sums[3].astype(jnp.bfloat16), "seq", scatter_dimension=0, tiled=True
        ).astype(jnp.float32),
        lax.psum_scatter(
            partial_sums[4].astype(jnp.bfloat16), "seq", scatter_dimension=0, tiled=True
        ).astype(jnp.float32),
        lax.psum_scatter(
            partial_sums[5].astype(jnp.bfloat16), "seq", scatter_dimension=1, tiled=True
        ).astype(jnp.float32),
        lax.psum_scatter(
            partial_sums[6].astype(jnp.bfloat16), "seq", scatter_dimension=0, tiled=True
        ).astype(jnp.float32),
        lax.psum_scatter(
            partial_sums[7].astype(jnp.bfloat16), "seq", scatter_dimension=0, tiled=True
        ).astype(jnp.float32),
        lax.psum_scatter(
            partial_sums[8].astype(jnp.bfloat16), "seq", scatter_dimension=0, tiled=True
        ).astype(jnp.float32),
        lax.psum_scatter(
            partial_sums[9].astype(jnp.bfloat16), "seq", scatter_dimension=1, tiled=True
        ).astype(jnp.float32),
        lax.psum_scatter(
            partial_sums[10].astype(jnp.bfloat16), "seq", scatter_dimension=0, tiled=True
        ).astype(jnp.float32),
        lax.psum_scatter(
            partial_sums[11].astype(jnp.bfloat16), "seq", scatter_dimension=1, tiled=True
        ).astype(jnp.float32),
        lax.psum_scatter(
            partial_sums[12].astype(jnp.bfloat16), "seq", scatter_dimension=0, tiled=True
        ).astype(jnp.float32),
    )
    return (
        layer_output,
        tokens_grad,
        summed[0],
        summed[1],
        summed[2],
        summed[3],
        summed[4],
        summed[5],
        summed[6],
        summed[7],
        summed[8],
        summed[9],
        summed[10],
        summed[11],
        summed[12],
    )


LX = (0, 4, 2, 6, 1, 5, 3, 7)
LY = (0, 2, 4, 6, 1, 3, 5, 7)
PAIR = ((0, 1), (1, 0), (2, 3), (3, 2))
FAR = ((0, 2), (2, 0), (1, 3), (3, 1))
CROSS = ((0, 3), (3, 0), (1, 2), (2, 1))
BF = jnp.bfloat16
F32 = jnp.float32
RATE = 1e8
SMEM_SPEC = pl.BlockSpec(memory_space=pltpu.SMEM)
VMEM_SPEC = pl.BlockSpec(memory_space=pltpu.VMEM)
HALF_ROOT = 0.7071067811865476
DENSITY = 0.3989422804014327


def fshift(values, bit, name="move"):
    with jax.named_scope(name):
        return lax.ppermute(values, "fsdp", [(i, i ^ bit) for i in range(8)])


def zshift(values, pairs, name="move"):
    with jax.named_scope(name):
        return lax.ppermute(values, "seq", pairs)


def after(values, *earlier):
    return lax.optimization_barrier((values, *earlier))[0]


def cost(micros):
    return pl.CostEstimate(flops=int(micros * RATE) + 1, bytes_accessed=1, transcendentals=0)


def call(body, outs, args, scratch=(), micros=1.0, limit=12, space=pltpu.VMEM):
    single = not isinstance(outs, (list, tuple))
    shapes = [outs] if single else list(outs)
    result = pl.pallas_call(
        body,
        out_shape=shapes,
        in_specs=[SMEM_SPEC] + [pl.BlockSpec(memory_space=space)] * (len(args) - 1),
        out_specs=[VMEM_SPEC] * len(shapes),
        scratch_shapes=list(scratch),
        compiler_params=pltpu.CompilerParams(vmem_limit_bytes=limit * 2**20),
        cost_estimate=cost(micros),
    )(*args)
    return result[0] if single else result


def struct(shape, dtype):
    return jax.ShapeDtypeStruct(shape, dtype)


def lanes_low(shape):
    return lax.broadcasted_iota(jnp.int32, shape, 1) < HD


def dot_nn(a, b):
    return lax.dot_general(a, b, (((1,), (0,)), ((), ())), preferred_element_type=F32)


def dot_nt(a, b):
    return lax.dot_general(a, b, (((1,), (1,)), ((), ())), preferred_element_type=F32)


def dot_tn(a, b):
    return lax.dot_general(a, b, (((0,), (0,)), ((), ())), preferred_element_type=F32)


def offset(index, size):
    return pl.multiple_of(index * size, size)


def natural(ref, start):
    return jnp.concatenate([ref[i : i + 1, start : start + 128] for i in range(8)], axis=1)


def pick_qkv(ids, w_hbm, tokens_hbm, *refs):
    count = (len(refs) - 4) // 2
    rows_hbm, (out_ref, extra_ref, w_ref), rows, sems = refs[:count], refs[count : count + 3], refs[count + 3 : -1], refs[-1]
    cut = tokens_hbm.shape[0] // 2
    copies = [(w_hbm, w_ref), (tokens_hbm.at[pl.ds(cut, cut)], extra_ref), *zip(rows_hbm, rows)]
    copies = [pltpu.make_async_copy(source, target, sems.at[i]) for i, (source, target) in enumerate(copies)]
    for copy in copies:
        copy.start()
    for copy in copies:
        copy.wait()
    half = ids[1] % 2
    low = lanes_low((128, 128))
    for j in range(w_ref.shape[1] // 256):
        first = w_ref[:, 256 * j : 256 * j + 128].astype(F32)
        second = w_ref[:, 256 * j + 128 : 256 * j + 256].astype(F32)
        even = jnp.where(low, first, pltpu.roll(second, HD, 1))
        odd = jnp.where(low, pltpu.roll(first, HD, 1), second)
        out_ref[0:128, 128 * j : 128 * j + 128] = jnp.where(half == 0, even, odd).astype(BF)
    start = 0
    for row_ref in rows:
        size = row_ref.shape[0]
        row = row_ref[...].astype(F32)
        out_ref[128:144, start : start + size] = jnp.broadcast_to(row.reshape(1, size), (16, size)).astype(BF)
        start += size


def pick_mlp(ids, w1_hbm, w2_hbm, wo_hbm, one_ref, two_ref, out_ref, sems):
    half = ids[1] % 2
    out_hbm = wo_hbm.at[pl.ds(offset(half, 64), 64)]
    copies = [
        (w2_hbm.at[pl.ds(offset(half, 256), 256)], two_ref.at[pl.ds(0, 256)]),
        (out_hbm, out_ref),
        (out_hbm, one_ref.at[pl.ds(256, 64)]),
        (out_hbm, two_ref.at[pl.ds(256, 64)]),
    ]
    for b in range(8):
        rows, lanes = pl.ds(128 * (b // 4), 128), pl.ds(256 * (b % 4), 256)
        copies.append((w1_hbm.at[:, pl.ds(offset(2 * b + half, 256), 256)], one_ref.at[rows, lanes]))
    copies = [pltpu.make_async_copy(source, target, sems.at[i]) for i, (source, target) in enumerate(copies)]
    for copy in copies:
        copy.start()
    for copy in copies:
        copy.wait()


def stack_mlp_body(ids, one_ref, one_x_ref, two_ref, two_y_ref, out_ref, one_out, two_out, outs):
    one_out[0:256, :] = one_ref[0:256, :]
    one_out[256:512, :] = one_x_ref[0:256, :]
    two_out[0:256, :] = two_ref[0:256, :]
    two_out[256:512, :] = two_y_ref[0:256, :]
    outs[0:64, :] = one_ref[256:320, :]
    outs[64:128, :] = one_x_ref[256:320, :]
    outs[128:192, :] = two_y_ref[256:320, :]
    outs[192:256, :] = out_ref[...]


def stack_body(ids, *refs):
    out_ref = refs[-1]
    start = 0
    for ref in refs[:-1]:
        out_ref[start : start + ref.shape[0], :] = ref[...]
        start += ref.shape[0]


def stack(ids, *arrays):
    rows = sum(a.shape[0] for a in arrays)
    return call(stack_body, struct((rows, arrays[0].shape[1]), BF), (ids, *arrays), micros=0.7)


def place_rows(ids, own_ref, theirs_ref, two_ref, three_ref, out_ref):
    half = ids[1] % 2
    pair = ids[1] // 2
    own_rows = own_ref.shape[0]
    cut = two_ref.shape[0]
    tail = out_ref.shape[0] - own_rows - cut
    for value in range(2):
        first, second = (own_ref, theirs_ref) if value == 0 else (theirs_ref, own_ref)

        @pl.when(half == value)
        def _():
            out_ref[0:own_rows, :] = first[...]

        @pl.when((half == value) & (pair == 0))
        def _():
            out_ref[own_rows:, :] = second[0 : cut + tail, :]

        @pl.when((half == value) & (pair == 1))
        def _():
            out_ref[own_rows + cut :, :] = second[0:tail, :]

    @pl.when(pair == 1)
    def _():
        out_ref[own_rows : own_rows + cut, :] = two_ref[...] + three_ref[...]


def place_grad_body(ids, own_ref, theirs_ref, two_ref, three_ref, out_ref):
    place_rows(ids, own_ref, theirs_ref, two_ref, three_ref, out_ref)
    own_rows = own_ref.shape[0]
    rows = out_ref.shape[0]
    live = key_valid(ids, (rows - own_rows, 1), 0, own_rows, own_rows)
    tail = out_ref[own_rows:, :].astype(F32)
    out_ref[own_rows:, :] = jnp.where(live, tail, 0.0).astype(BF)


def parts_of(refs):
    a, x, y, d, other = refs
    parts = {0: (a, 0), 2: (x, 0), 4: (y, 0), 6: (d, 0)}
    parts.update({2 * i + 1: (other, 144 * i) for i in range(4)})
    return parts


def piece_tile(parts, k, lanes):
    ref, row = parts[k]
    return ref[row : row + 128, lanes]


def qkv_body(ids, own_ref, theirs_ref, two_ref, three_ref, *refs):
    parts = parts_of(refs[:5])
    x_ref, qkv_ref, even_ref, odd_ref, par_ref, norm_ref, bias_ref = refs[5:]
    place_rows(ids, own_ref, theirs_ref, two_ref, three_ref, x_ref)
    f = ids[0]
    half = ids[1] % 2
    rows = x_ref.shape[0]
    for k in range(8):
        ref, at = parts[k]
        par_ref[pl.ds(f ^ k, 1), :] = ref[at + 128 : at + 129, :].astype(F32)
    gain = natural(par_ref, 0)
    shift = natural(par_ref, 128)
    low = lanes_low((1, 128))
    bias_ref[...] = jnp.zeros_like(bias_ref)
    for start, place in ((768, 0), (896, 1024)):
        block = par_ref[:, start : start + 128]
        turned = pltpu.roll(block, HD, 1)
        lower = jnp.where(half == 0, block, turned)
        upper = jnp.where(half == 0, turned, block)
        for j in range(4):
            bias_ref[:, place + 128 * j : place + 128 * j + 128] = jnp.where(
                low, lower[2 * j : 2 * j + 1], upper[2 * j + 1 : 2 * j + 2]
            )

    def norm(i, carry):
        at = pl.ds(offset(i, 32), 32)
        values = x_ref[at, :].astype(F32)
        norm_ref[at, :] = normalize(values, gain, shift).astype(BF)
        return carry

    lax.fori_loop(0, rows // 32, norm, 0)
    for place, k in enumerate(LY):
        target = even_ref if place < 4 else odd_ref
        column = 128 * (place % 4)
        target[:, column : column + 128] = norm_ref[:, pl.ds(offset(f ^ k, 128), 128)]
    left = jnp.concatenate([even_ref[...], odd_ref[...]], axis=1)
    for n in range(6):
        lanes = slice(256 * n, 256 * n + 256)
        weight = jnp.concatenate([piece_tile(parts, k, lanes) for k in LY], axis=0)
        qkv_ref[:, lanes] = (dot_nn(left, weight) + bias_ref[:, lanes]).astype(BF)


def key_valid(ids, shape, axis, own_rows, first=0):
    pair = ids[1] // 2
    place = lax.broadcasted_iota(jnp.int32, shape, axis) + first
    return (place < LEN + pair) & ((place != own_rows) | (pair == 0))


def head_masked(block, head, factor=None):
    wide = block.astype(F32)
    low = lanes_low(wide.shape)
    keep = low if head == 0 else jnp.logical_not(low)
    if factor is not None:
        wide = wide * factor
    return jnp.where(keep, wide, 0.0).astype(BF)


def attend_body(own_rows, tile, ids, q_ref, k_ref, v_ref, o_ref):
    rows = q_ref.shape[0]
    value = v_ref[...]
    live = key_valid(ids, (1, rows), 1, own_rows)
    low = lanes_low((tile, 128))
    keys = [head_masked(k_ref[...], head, HD**-0.5) for head in range(2)]
    for t in range(rows // tile):
        at = slice(t * tile, t * tile + tile)
        outs = []
        for head in range(2):
            scores = jnp.where(live, dot_nt(q_ref[at, :], keys[head]), masked_score)
            peak = jnp.max(scores, axis=1, keepdims=True)
            lifted = jnp.exp(scores - peak)
            total = jnp.sum(lifted, axis=1, keepdims=True)
            outs.append(dot_nn(lifted.astype(BF), value) / total)
        o_ref[at, :] = jnp.where(low, outs[0], outs[1]).astype(BF)


def attend_back_body(own_rows, tile, ids, q_ref, k_ref, v_ref, g0_ref, g1_ref, gq_ref, gk_ref, gv_ref):
    rows = q_ref.shape[0]
    whole = jnp.concatenate([g0_ref[...], g1_ref[...]], axis=0)
    scale = HD**-0.5
    live = key_valid(ids, (rows, 1), 0, own_rows)
    low = lanes_low((rows, 128))
    grads_k = []
    grads_v = []
    for t in range(rows // tile):
        at = slice(t * tile, t * tile + tile)
        query = q_ref[at, :]
        grad = whole[at]
        grad_q = None
        for head in range(2):
            keys = head_masked(k_ref[...], head, scale)
            values = head_masked(v_ref[...], head)
            scores = jnp.where(live, dot_nt(keys, query), masked_score)
            peak = jnp.max(scores, axis=0, keepdims=True)
            lifted = jnp.exp(scores - peak)
            probs = lifted * (1.0 / jnp.sum(lifted, axis=0, keepdims=True))
            grad_p = dot_nt(values, grad)
            inner = jnp.sum(grad_p * probs, axis=0, keepdims=True)
            grad_s = (probs * (grad_p - inner)).astype(BF)
            grad_v = dot_nn(probs.astype(BF), grad)
            grad_k = dot_nn(grad_s, query) * scale
            part = dot_tn(grad_s, keys)
            grad_q = part if grad_q is None else grad_q + part
            if t == 0:
                grads_k.append(grad_k)
                grads_v.append(grad_v)
            else:
                grads_k[head] = grads_k[head] + grad_k
                grads_v[head] = grads_v[head] + grad_v
        gq_ref[at, :] = grad_q.astype(BF)
    gk_ref[...] = jnp.where(low, grads_k[0], grads_k[1]).astype(BF)
    gv_ref[...] = jnp.where(low, grads_v[0], grads_v[1]).astype(BF)


def mixed_body(ids, o_ref, even_ref, odd_ref, first_ref, second_ref, w_ref):
    f = ids[0]
    for place, k in enumerate((0, 2, 4, 6)):
        row = HD * place
        w_ref[pl.ds(offset(f ^ k, HD), HD), :] = even_ref[row : row + HD, :]
        w_ref[pl.ds(offset(f ^ k ^ 1, HD), HD), :] = odd_ref[row : row + HD, :]
    size = first_ref.shape[0]
    for n in range(4):
        lanes = slice(256 * n, 256 * n + 256)
        first_ref[:, lanes] = dot_nn(o_ref[0:size, :], w_ref[:, lanes]).astype(BF)
    for n in range(4):
        lanes = slice(256 * n, 256 * n + 256)
        second_ref[:, lanes] = dot_nn(o_ref[size:, :], w_ref[:, lanes]).astype(BF)


def mlp_body(base, ids, par_ref, x_ref, mine_ref, theirs_ref, gm_ref, one_a, one_b, two_a, two_b, *refs):
    (mid_ref, even_ref, odd_ref, act_e_ref, act_o_ref, gu_ref, gh_ref, bias_ref, norm_ref, u_ref, g_ref) = refs
    f = ids[0]
    half = ids[1] % 2
    rows = mid_ref.shape[0]
    gain = natural(par_ref, 384)
    shift = natural(par_ref, 512)
    bias = natural(par_ref, 256)

    def one_rows(place, start, size, lanes):
        ref = one_a if place < 4 else one_b
        return ref[pl.ds(256 * (place % 4) + start, size), lanes]

    def norm(i, carry):
        at = pl.ds(offset(i, 32), 32)
        middle = x_ref[pl.ds(pl.multiple_of(base + i * 32, 32), 32), :].astype(F32)
        middle = middle + (mine_ref[at, :].astype(F32) + theirs_ref[at, :].astype(F32) + bias)
        mid_ref[at, :] = middle
        norm_ref[at, :] = normalize(middle, gain, shift).astype(BF)
        return carry

    lax.fori_loop(0, rows // 32, norm, 0)
    for place, k in enumerate(LY):
        target = even_ref if place < 4 else odd_ref
        column = 128 * (place % 4)
        target[:, column : column + 128] = norm_ref[:, pl.ds(offset(f ^ k, 128), 128)]
    left = jnp.concatenate([even_ref[...], odd_ref[...]], axis=1)
    grad = gm_ref[base : base + rows, :]
    for place, k in enumerate(LX):
        block = f ^ k
        at_lanes = pl.ds(offset(block % 4, 256), 256)
        weight = jnp.concatenate([one_rows(j, offset(block // 4, 128), 128, at_lanes) for j in range(8)], axis=0)
        u_ref[...] = dot_nn(left, weight)
        two_ref = two_a if place < 4 else two_b
        g_ref[...] = dot_nt(grad, two_ref[256 * (place % 4) : 256 * (place % 4) + 256, :])
        row = par_ref[pl.ds(block, 1), pl.ds(offset(4 + half, 256), 256)]
        act_ref = act_e_ref if place < 4 else act_o_ref
        column = 256 * (place % 4)

        def gelu(i, total):
            at = pl.ds(offset(i, 32), 32)
            u = u_ref[at, :] + row
            cdf = 0.5 + 0.5 * lax.erf(u * HALF_ROOT)
            act_ref[at, column : column + 256] = (u * cdf).astype(BF)
            slope = cdf + u * (jnp.exp(-0.5 * (u * u)) * DENSITY)
            gu = (g_ref[at, :] * slope).astype(BF)
            gu_ref[at, pl.ds(offset(block, 256), 256)] = gu
            return total + jnp.sum(gu.astype(F32), axis=0, keepdims=True)

        total = lax.fori_loop(0, rows // 32, gelu, jnp.zeros((1, 256), F32))
        bias_ref[pl.ds(block, 1), :] = total
    for j in range(4):
        total = None
        for part in range(2):
            weight = jnp.concatenate(
                [one_rows(place, 128 * part, 128, slice(None)) for place in (2 * j, 2 * j + 1)], axis=0
            )
            term = dot_nt(gu_ref[:, 1024 * part : 1024 * part + 1024], weight)
            total = term if total is None else total + term
        gh_ref[:, pl.ds(offset(f ^ LY[2 * j], 128), 128)] = total[:, 0:128].astype(BF)
        gh_ref[:, pl.ds(offset(f ^ LY[2 * j + 1], 128), 128)] = total[:, 128:256].astype(BF)


def out_body(ids, e0_ref, o0_ref, e1_ref, o1_ref, two_a, two_b, keep_ref, send_ref, y_ref):
    half = ids[1] % 2
    for n in range(4):
        lanes = slice(256 * n, 256 * n + 256)
        weight = jnp.concatenate([two_a[:, lanes], two_b[:, lanes]], axis=0)
        start = 0
        for e_ref, o_ref in ((e0_ref, o0_ref), (e1_ref, o1_ref)):
            left = jnp.concatenate([e_ref[...], o_ref[...]], axis=1)
            y_ref[start : start + left.shape[0], lanes] = dot_nn(left, weight).astype(BF)
            start += left.shape[0]
    rows = keep_ref.shape[0]
    shift = y_ref.shape[0] - rows
    keep_ref[...] = y_ref[pl.ds(offset(half, shift), rows), :]
    send_ref[...] = y_ref[pl.ds(offset(1 - half, shift), rows), :]


def result_body(ids, par_ref, mid0_ref, mid1_ref, mine_ref, theirs_ref, out_ref, extra_ref):
    half = ids[1] % 2
    bias = natural(par_ref, 640)
    rows = out_ref.shape[0]
    shift = mid0_ref.shape[0] + mid1_ref.shape[0] - rows

    def step(i, carry):
        at = pl.ds(offset(i, 32), 32)
        place = half * shift + i * 32
        total = mine_ref[at, :].astype(F32) + theirs_ref[at, :].astype(F32) + bias
        size = mid0_ref.shape[0]

        @pl.when(place < size)
        def _():
            out_ref[at, :] = (total + mid0_ref[pl.ds(pl.multiple_of(place, 32), 32), :]).astype(BF)

        @pl.when(place >= size)
        def _():
            out_ref[at, :] = (total + mid1_ref[pl.ds(pl.multiple_of(place - size, 32), 32), :]).astype(BF)

        return carry

    lax.fori_loop(0, rows // 32, step, 0)
    spot = rows - shift
    extra_ref[...] = out_ref[spot : spot + extra_ref.shape[0], :]


def owner_rows_body(ids, valid_ref, full_ref, extra_ref, out_ref):
    half = ids[1] % 2
    pair = ids[1] // 2
    rows, cut = full_ref.shape[0], extra_ref.shape[0]
    tail = 2 * cut + 32 - rows
    shift = cut + tail
    spot = rows - shift
    width = full_ref.shape[1]

    def masked(at, values):
        valid = jnp.concatenate([valid_ref[at, :]] * (width // 128), axis=1)
        return jnp.where(valid > 0.0, values.astype(F32), 0.0).astype(out_ref.dtype)

    @pl.when(half == 0)
    def _():
        out_ref[...] = masked(slice(None), full_ref[...])

    @pl.when((half == 1) & (pair == 0))
    def _():
        top = slice(0, cut)
        out_ref[top, :] = masked(top, full_ref[spot : spot + cut, :])
        low = slice(cut, rows)
        border = full_ref[spot + cut : spot + cut + 1, :].astype(F32)
        first = lax.broadcasted_iota(jnp.int32, (cut, 1), 0) == 0
        out_ref[low, :] = masked(low, jnp.where(first, border, extra_ref[...].astype(F32)))

    @pl.when((half == 1) & (pair == 1))
    def _():
        top = slice(0, tail)
        out_ref[top, :] = masked(top, full_ref[spot + cut : spot + cut + tail, :])
        out_ref[tail:rows, :] = jnp.zeros((rows - tail, width), out_ref.dtype)


def rows_grad_body(step, ids, l0_ref, l1_ref, r0_ref, r1_ref, out_ref):
    rows = l0_ref.shape[0] + l1_ref.shape[0]
    left = jnp.concatenate([l0_ref[...], l1_ref[...]], axis=0)
    for n in range(out_ref.shape[1] // step):
        lanes = slice(step * n, step * n + step)
        if r0_ref.shape[0] == rows:
            right = r0_ref[:, lanes]
        else:
            right = jnp.concatenate([r0_ref[:, lanes], r1_ref[:, lanes]], axis=0)
        out_ref[:, lanes] = dot_tn(left, right).astype(BF)


def norm_back(values, grad, gain):
    center = values - jnp.mean(values, axis=-1, keepdims=True)
    scale = lax.rsqrt(jnp.mean(center * center, axis=-1, keepdims=True) + norm_eps)
    unit = center * scale
    scaled = grad * gain
    first = jnp.mean(scaled, axis=-1, keepdims=True)
    second = jnp.mean(scaled * unit, axis=-1, keepdims=True)
    return unit, scale * (scaled - first - unit * second)


def fold(values):
    total = values[0:8]
    for i in range(1, values.shape[0] // 8):
        total = total + values[8 * i : 8 * i + 8]
    return total


def spread(ref, start, partial_rows):
    row = jnp.sum(partial_rows, axis=0, keepdims=True)
    for i in range(8):
        ref[i : i + 1, start : start + 128] = row[:, 128 * i : 128 * i + 128]


def middle_back_body(base, ids, par_ref, mid_ref, gm_ref, mine_ref, theirs_ref, w_ref, gb_ref, go_ref, sums_ref):
    half = ids[1] % 2
    counts = jnp.where(half == 0, 1.0, 0.0)
    gain = natural(par_ref, 384)
    rows = mid_ref.shape[0]

    def step(i, carry):
        out_sum, gain_sum, shift_sum, last_sum = carry
        at = pl.ds(offset(i, 32), 32)
        mine = mine_ref[at, :].astype(F32)
        grad = mine + theirs_ref[at, :].astype(F32)
        unit, back = norm_back(mid_ref[at, :], grad, gain)
        gm = gm_ref[pl.ds(pl.multiple_of(base + i * 32, 32), 32), :].astype(F32)
        gb = (gm + back).astype(BF)
        gb_ref[at, :] = gb
        return (
            out_sum + fold(gb.astype(F32)),
            gain_sum + fold(mine * unit),
            shift_sum + fold(mine),
            last_sum + fold(gm),
        )

    zero = jnp.zeros((8, mid_ref.shape[1]), F32)
    sums = lax.fori_loop(0, rows // 32, step, (zero, zero, zero, zero))
    spread(sums_ref, 0, sums[0] * counts)
    spread(sums_ref, 128, sums[1])
    spread(sums_ref, 256, sums[2])
    spread(sums_ref, 384, sums[3] * counts)
    grad = gb_ref[...]
    for n in range(2):
        rows = slice(256 * n, 256 * n + 256)
        go_ref[:, rows] = dot_nt(grad, w_ref[rows, :]).astype(BF)


def out_grad_body(ids, o_ref, gb0_ref, gb1_ref, keep_ref, send_ref, grad_ref):
    f = ids[0]
    for n in range(4):
        lanes = slice(256 * n, 256 * n + 256)
        right = jnp.concatenate([gb0_ref[:, lanes], gb1_ref[:, lanes]], axis=0)
        grad_ref[:, lanes] = dot_tn(o_ref[...], right).astype(BF)
    for place, k in enumerate(LX):
        target = keep_ref if place < 4 else send_ref
        row = HD * (place % 4)
        target[row : row + HD, :] = grad_ref[pl.ds(offset(f ^ k, HD), HD), :]


def input_grad_body(ids, x_ref, par_ref, gq_ref, gk_ref, gv_ref, *refs):
    parts = parts_of(refs[:5])
    keep_ref, send_ref, sums_ref, wide_ref, gh_ref = refs[5:]
    f = ids[0]
    left = jnp.concatenate([gq_ref[...], gk_ref[...], gv_ref[...]], axis=1)
    for j in range(4):
        first, second = LY[2 * j], LY[2 * j + 1]
        weight = jnp.concatenate(
            [piece_tile(parts, first, slice(None)), piece_tile(parts, second, slice(None))], axis=0
        )
        total = dot_nt(left, weight)
        wide_ref[:, pl.ds(offset(f ^ first, 128), 128)] = total[:, 0:128]
        wide_ref[:, pl.ds(offset(f ^ second, 128), 128)] = total[:, 128:256]

    def step(i, carry):
        gain_sum, shift_sum = carry
        at = pl.ds(offset(i, 32), 32)
        grad = wide_ref[at, :]
        gh_ref[at, :] = grad.astype(BF)
        values = x_ref[at, :].astype(F32)
        center = values - jnp.mean(values, axis=-1, keepdims=True)
        unit = center * lax.rsqrt(jnp.mean(center * center, axis=-1, keepdims=True) + norm_eps)
        return gain_sum + fold(grad * unit), shift_sum + fold(grad)

    zero = jnp.zeros((8, x_ref.shape[1]), F32)
    gain_sum, shift_sum = lax.fori_loop(0, x_ref.shape[0] // 32, step, (zero, zero))
    half = ids[1] % 2
    rows = keep_ref.shape[0]
    shift = x_ref.shape[0] - rows
    keep_ref[...] = gh_ref[pl.ds(offset(half, shift), rows), :]
    send_ref[...] = gh_ref[pl.ds(offset(1 - half, shift), rows), :]
    spread(sums_ref, 0, gain_sum)
    spread(sums_ref, 128, shift_sum)


def qkv_grad_body(ids, even_ref, odd_ref, gq_ref, gk_ref, gv_ref, one_ref, mid0_ref, mid1_ref, fc0_ref, fc1_ref, *refs):
    keep_ref, send_ref, par_ref = refs
    f = ids[0]
    half = ids[1] % 2
    par_ref[:, 0:256] = one_ref[...]
    par_ref[:, 256:768] = mid0_ref[...] + mid1_ref[...]
    fc_sum = fc0_ref[...] + fc1_ref[...]
    low = lanes_low((1, 128))
    mine = low == (half == 0)
    for g_ref, place in ((gq_ref, 768), (gv_ref, 896)):
        row = jnp.sum(g_ref[...].astype(F32), axis=0, keepdims=True)
        for j in range(4):
            block = row[:, 128 * j : 128 * j + 128]
            turned = pltpu.roll(jnp.broadcast_to(block, (8, 128)), HD, 1)[0:1]
            first = jnp.where(half == 0, block, turned)
            second = jnp.where(half == 0, turned, block)
            par_ref[2 * j : 2 * j + 1, place : place + 128] = jnp.where(mine, first, 0.0)
            par_ref[2 * j + 1 : 2 * j + 2, place : place + 128] = jnp.where(mine, second, 0.0)
    zero = jnp.zeros((8, 256), F32)
    par_ref[:, 1024:1280] = jnp.where(half == 0, fc_sum, zero)
    par_ref[:, 1280:1536] = jnp.where(half == 1, fc_sum, zero)
    order_b = LY
    place_a = {k: i for i, k in enumerate(LX)}
    for j in range(4):
        source = even_ref if j < 2 else odd_ref
        left = source[:, 256 * (j % 2) : 256 * (j % 2) + 256]
        for n, g_ref in enumerate((gq_ref, gk_ref, gv_ref)):
            lanes = slice(512 * n, 512 * n + 512)
            total = dot_tn(left, g_ref[...]).astype(BF)
            for i in range(2):
                k = order_b[2 * j + i]
                target = keep_ref if place_a[k] < 4 else send_ref
                row = 64 * (place_a[k] % 4)
                target[row : row + 64, lanes] = total[128 * i : 128 * i + 64]
                row = 256 + 80 * ((2 * j + i) % 4)
                target[row : row + 64, lanes] = total[128 * i + 64 : 128 * i + 128]
    for place, k in enumerate(order_b):
        target = keep_ref if place < 4 else send_ref
        row = 320 + 80 * (place % 4)
        target[row : row + 16, :] = jnp.broadcast_to(par_ref[pl.ds(f ^ k, 1), :], (16, 1536)).astype(BF)


def input_back_body(ids, par_ref, x_ref, gb0_ref, gb1_ref, mine_ref, theirs_ref, out_ref, extra_ref, gb_ref):
    half = ids[1] % 2
    gain = natural(par_ref, 0)
    rows = out_ref.shape[0]
    shift = x_ref.shape[0] - rows
    size = gb0_ref.shape[0]
    gb_ref[0:size, :] = gb0_ref[...]
    gb_ref[size:, :] = gb1_ref[...]

    def step(i, carry):
        at = pl.ds(offset(i, 32), 32)
        place = pl.ds(pl.multiple_of(half * shift + i * 32, 32), 32)
        grad = mine_ref[at, :].astype(F32) + theirs_ref[at, :].astype(F32)
        back = norm_back(x_ref[place, :].astype(F32), grad, gain)[1]
        out_ref[at, :] = gb_ref[place, :].astype(F32) + back
        return carry

    lax.fori_loop(0, rows // 32, step, 0)
    spot = rows - shift
    extra_ref[...] = out_ref[spot : spot + extra_ref.shape[0], :].astype(BF)


def line_body(ids, ka_ref, ra_ref, kb_ref, rb_ref, *outs):
    s = ids[1]
    wide_a, wide_b = outs[4:]
    wide_a[...] = halve(ka_ref[...], ra_ref[...])
    wide_b[...] = halve(kb_ref[...], rb_ref[...])
    for turn in range(4):
        lanes = pl.ds(offset(s ^ turn, 384), 384)
        out_ref = outs[turn]
        out_ref[0:64, :] = wide_a[:, lanes]
        out_ref[64:128, :] = wide_b[0:64, lanes]
        for i in range(4):
            out_ref[128 + 16 * i : 144 + 16 * i, :] = wide_b[64:80, 384 * i : 384 * i + 384]


def line_mlp_body(ids, k2_ref, r2_ref, k1_ref, r1_ref, *outs):
    s = ids[1]
    two, one = outs[4:]
    two[...] = halve(k2_ref[...], r2_ref[...])
    one[...] = halve(k1_ref[...], r1_ref[...])
    for turn in range(4):
        t = s ^ turn
        out_ref = outs[turn]
        out_ref[0:256, :] = two[0:256, pl.ds(offset(t, 256), 256)]
        for i in range(2):
            out_ref[256 + 128 * i : 384 + 128 * i, :] = one[:, pl.ds(offset(2 * t + i, 256), 256)]
        out_ref[512:576, :] = two[256:320, pl.ds(offset(t, 256), 256)]


def merge_body(plan, ids, *refs):
    count = sum(len(group) for group in plan)
    at = 0
    for place, group in enumerate(plan):
        stay_ref, send_ref = refs[2 * count + 2 * place : 2 * count + 2 * place + 2]
        row = 0
        for start, rows in group:
            keep_ref, got_ref = refs[2 * at : 2 * at + 2]
            half = rows // 2
            stay_ref[row : row + half, :] = halve(keep_ref[start : start + half, :], got_ref[start : start + half, :])
            send_ref[row : row + half, :] = halve(
                keep_ref[start + half : start + rows, :], got_ref[start + half : start + rows, :]
            )
            row += half
            at += 1


def merge(ids, *groups):
    plan = tuple(tuple((start, rows) for _, _, start, rows in group) for group in groups)
    shapes = []
    for group in groups:
        rows = sum(g[3] for g in group) // 2
        shapes += [struct((rows, group[0][0].shape[1]), BF)] * 2
    operands = [a for group in groups for g in group for a in g[:2]]
    return call(partial(merge_body, plan), shapes, (ids, *operands), micros=1.0)


def join_mlp_body(ids, own_ref, pair_ref, far_ref, cross_ref, one_ref, two_ref, out_ref):
    half = ids[1] % 2
    other = 1 - half

    def sums(at):
        same = own_ref[at, :].astype(F32) + far_ref[at, :].astype(F32)
        return same, pair_ref[at, :].astype(F32) + cross_ref[at, :].astype(F32)

    same, rest = sums(slice(0, 256))
    two_ref[pl.ds(offset(half, 256), 256), :] = same
    two_ref[pl.ds(offset(other, 256), 256), :] = rest
    for i in range(2):
        same, rest = sums(slice(256 + 128 * i, 384 + 128 * i))
        one_ref[:, pl.ds(offset(2 * i + half, 256), 256)] = same
        one_ref[:, pl.ds(offset(2 * i + other, 256), 256)] = rest
    same, rest = sums(slice(512, 576))
    out_ref[pl.ds(offset(half, 64), 64), :] = same
    out_ref[pl.ds(offset(other, 64), 64), :] = rest


def join_body(ids, own_ref, pair_ref, far_ref, cross_ref, out_ref, sums_ref, wide_ref):
    s = ids[1]
    lower = s % 2 == 0
    low = lanes_low((128, 128))
    for j in range(3):
        lanes = slice(128 * j, 128 * j + 128)
        same = own_ref[0:128, lanes].astype(F32) + far_ref[0:128, lanes].astype(F32)
        other = pair_ref[0:128, lanes].astype(F32) + cross_ref[0:128, lanes].astype(F32)
        first = jnp.where(lower, same, other)
        second = jnp.where(lower, other, same)
        out_ref[:, 256 * j : 256 * j + 128] = jnp.where(low, first, pltpu.roll(second, HD, 1))
        out_ref[:, 256 * j + 128 : 256 * j + 256] = jnp.where(low, pltpu.roll(first, HD, 1), second)
    for i in range(4):
        at = slice(128 + 16 * i, 144 + 16 * i)
        total = own_ref[at, :].astype(F32) + far_ref[at, :].astype(F32)
        total = total + pair_ref[at, :].astype(F32) + cross_ref[at, :].astype(F32)
        for n in range(3):
            spot = 3 * i + n
            block = total[0:8, 128 * n : 128 * n + 128]
            if spot < 8:
                sums_ref[spot : spot + 1, :] = pltpu.roll(block, (128 - 32 * s) % 128, 1)[0:1]
            else:
                wide_ref[spot - 8 : spot - 7, :] = block[0:1]
    sums_ref[8:9, :] = wide_ref[pl.ds(s, 1), :]


def halve(keep, received):
    return (keep.astype(F32) + received.astype(F32)).astype(BF)


def paired_shards(
    tokens,
    segment_ids,
    ln1_gain,
    ln1_bias,
    w_qkv,
    q_bias,
    v_bias,
    w_out,
    out_bias,
    ln2_gain,
    ln2_bias,
    w_fc1,
    fc1_bias,
    w_fc2,
    fc2_bias,
    cotangent,
):
    own_rows, width = tokens.shape
    cut = own_rows // 2
    tail = 32
    rows = own_rows + cut + tail
    f = lax.axis_index("fsdp")
    s = lax.axis_index("seq")
    ids = jnp.where(lax.iota(jnp.int32, 2) == 0, f, s).astype(jnp.int32)

    def exchange(own, extra, name):
        extra = zshift(extra, ((1, 2),), name + "_extra")
        return zshift(own, PAIR, name), extra, zshift(extra, ((2, 3),), name + "_relay")

    hbm = partial(pltpu.with_memory_space_constraint, memory_space=pltpu.HBM)
    vectors = [ln1_gain, ln1_bias, out_bias, ln2_gain, ln2_bias, fc2_bias, q_bias, v_bias, fc1_bias]
    a, tokens_extra = call(
        pick_qkv,
        [struct((144, 1536), BF), struct((own_rows - cut, width), BF)],
        (ids, *[hbm(v) for v in (w_qkv, tokens, *vectors)]),
        scratch=[pltpu.VMEM(v.shape, BF) for v in (w_qkv, *vectors)] + [pltpu.SemaphoreType.DMA((11,))],
        space=pltpu.HBM, micros=2.2)
    moved_tokens = exchange(tokens, tokens_extra, "tokens")
    one, two, out = call(
        pick_mlp,
        [struct((320, 1024), BF), struct((320, 1024), BF), struct((64, 1024), BF)],
        (ids, hbm(after(w_fc1, a)), hbm(w_fc2), hbm(w_out)),
        scratch=[pltpu.SemaphoreType.DMA((12,))],
        space=pltpu.HBM, micros=1.9)
    pieces = [a, fshift(a, 2, "qkv_x"), fshift(a, 4, "qkv_y"), fshift(a, 6, "qkv_xy")]
    pieces.append(fshift(stack(ids, after(a, *moved_tokens, out), *pieces[1:]), 1, "qkv_core"))

    one_x = fshift(after(one, moved_tokens[0]), 2, "one_x")
    two_y = fshift(after(two, moved_tokens[0]), 4, "two_y")
    out_xy = fshift(after(out, *pieces[1:4]), 6, "out_xy")

    x, qkv, h1_e, h1_o, par = call(
        qkv_body,
        [
            struct((rows, width), BF),
            struct((rows, 1536), BF),
            struct((rows, 512), BF),
            struct((rows, 512), BF),
            struct((8, 1536), F32),
        ],
        (ids, tokens, *moved_tokens, *pieces),
        scratch=[pltpu.VMEM((rows, 1024), BF), pltpu.VMEM((1, 1536), F32)], micros=6.8)
    one_two, two_two, outs_even = call(
        stack_mlp_body,
        [struct((512, 1024), BF), struct((512, 1024), BF), struct((256, 1024), BF)],
        (ids, after(one, qkv), one_x, two, two_y, out_xy), micros=0.8)
    outs_odd = fshift(outs_even, 1, "out_core")
    valid = segment_ids >= 0
    gm_own = jnp.where(valid[:, None], after(cotangent, *moved_tokens), jnp.zeros_like(cotangent))
    valid_lanes = jnp.broadcast_to(valid[:, None].astype(F32), (own_rows, 128))
    moved_gm = exchange(gm_own, gm_own[cut:], "cotangent")

    def columns(base, size=rows):
        return pl.BlockSpec((size, 128), lambda j: (0, base + j))

    heads_o = pl.pallas_call(
        partial(attend_body, own_rows, rows // 2),
        grid=(4,),
        out_shape=struct((rows, 512), BF),
        in_specs=[SMEM_SPEC, columns(0), columns(4), columns(8)],
        out_specs=columns(0),
        compiler_params=pltpu.CompilerParams(vmem_limit_bytes=20 * 2**20),
        cost_estimate=cost(7.1),
    )(ids, after(qkv, one_two), qkv, qkv)
    sizes = (320, rows - 320)

    mine_0, mine_1, w_out_full = call(
        mixed_body,
        [struct((sizes[0], width), BF), struct((sizes[1], width), BF), struct((512, width), BF)],
        (ids, heads_o, outs_even, outs_odd), micros=1.4)
    theirs_0 = zshift(mine_0, PAIR, "mixed")
    theirs_1 = zshift(after(mine_1, mine_0), PAIR, "mixed")
    gm = call(place_grad_body, struct((rows, width), BF), (ids, after(gm_own, mine_1), *moved_gm), micros=1.0)
    one_even = stack(ids, after(one_two, gm), fshift(one_two, 4, "one_y"))
    two_even = stack(ids, after(two_two, gm), fshift(two_two, 2, "two_x"))
    weights = (one_even, fshift(one_even, 1, "one_core"), two_even, fshift(two_even, 1, "two_core"))

    def mlp(chunk, mine, theirs):
        part = sizes[chunk]
        return call(
            partial(mlp_body, chunk * sizes[0]),
            [
                struct((part, 1024), F32),
                struct((part, 512), BF),
                struct((part, 512), BF),
                struct((part, 1024), BF),
                struct((part, 1024), BF),
                struct((part, 2048), BF),
                struct((part, 1024), BF),
                struct((8, 256), F32),
            ],
            (ids, par, x, mine, theirs, gm, *weights),
            scratch=[pltpu.VMEM((part, 1024), BF), pltpu.VMEM((part, 256), F32), pltpu.VMEM((part, 256), F32)], micros=11.2)

    mid_0, h2_e0, h2_o0, act_e0, act_o0, gu_0, gh2_0, fc1_sums_0 = mlp(0, mine_0, theirs_0)
    gh2_theirs_0 = zshift(gh2_0, PAIR, "mlp_grad")
    mid_1, h2_e1, h2_o1, act_e1, act_o1, gu_1, gh2_1, fc1_sums_1 = mlp(1, after(mine_1, gh2_0), theirs_1)
    gh2_theirs_1 = zshift(gh2_1, PAIR, "mlp_grad")

    def row_grad(l0, l1, r0, r1, step):
        return call(
            partial(rows_grad_body, step),
            struct((l0.shape[1], r0.shape[1]), BF),
            (ids, l0, l1, r0, r1), micros=2.4)

    send_two = row_grad(after(act_o0, gh2_1), act_o1, gm, gm, 256)
    got_two = fshift(send_two, 1, "two_grad_core")
    keep_two = row_grad(after(act_e0, send_two), act_e1, gm, gm, 256)
    send_one = row_grad(after(h2_o0, keep_two), h2_o1, gu_0, gu_1, 512)
    got_one = fshift(send_one, 1, "one_grad_core")
    stay_two, send_two = merge(ids, [(after(keep_two, send_one), got_two, 0, 1024)])
    got_two = fshift(send_two, 2, "two_grad_x")
    keep_one = row_grad(after(h2_e0, stay_two), h2_e1, gu_0, gu_1, 512)
    stay_one, send_one = merge(ids, [(keep_one, got_one, 0, 512)])
    got_one = fshift(send_one, 4, "one_grad_y")

    def middle_back(chunk, mid, mine, theirs):
        part = sizes[chunk]
        return call(
            partial(middle_back_body, chunk * sizes[0]),
            [struct((part, 1024), BF), struct((part, 512), BF), struct((8, 512), F32)],
            (ids, par, mid, gm, mine, theirs, w_out_full), micros=4.0)

    gb_0, go_0, mid_sums_0 = middle_back(0, after(mid_0, stay_one), gh2_0, gh2_theirs_0)
    y_keep, y_send = call(
        out_body,
        [struct((own_rows, width), BF)] * 2,
        (ids, after(act_e0, gb_0), act_o0, act_e1, act_o1, two_even, weights[3]),
        scratch=[pltpu.VMEM((rows, width), BF)], micros=3.6)
    y_theirs = zshift(after(y_send, gh2_theirs_1), PAIR, "output")
    gb_1, go_1, mid_sums_1 = middle_back(1, after(mid_1, y_keep), gh2_1, gh2_theirs_1)
    keep_o, send_o = call(
        out_grad_body,
        [struct((256, 1024), BF)] * 2,
        (ids, heads_o, gb_0, gb_1),
        scratch=[pltpu.VMEM((512, 1024), BF)], micros=1.7)
    got_o = fshift(send_o, 1, "out_grad_core")
    gq, gk, gv = pl.pallas_call(
        partial(attend_back_body, own_rows, rows),
        grid=(4,),
        out_shape=[struct((rows, 512), BF)] * 3,
        in_specs=[SMEM_SPEC, columns(0), columns(4), columns(8), columns(0, sizes[0]), columns(0, sizes[1])],
        out_specs=[columns(0)] * 3,
        compiler_params=pltpu.CompilerParams(vmem_limit_bytes=24 * 2**20),
        cost_estimate=cost(14.0),
    )(ids, qkv, qkv, qkv, after(go_0, keep_o), go_1)
    stay_o, send_o = merge(ids, [(after(keep_o, gq), got_o, 0, 256)])
    got_o = fshift(send_o, 2, "out_grad_x")
    stay_one, send_one = merge(ids, [(after(stay_one, stay_o), got_one, 0, 256)])
    got_one = fshift(send_one, 2, "one_grad_x")
    result, result_extra = call(
        result_body,
        [struct((own_rows, width), BF), struct((cut, width), BF)],
        (ids, par, mid_0, mid_1, after(y_keep, stay_one), y_theirs), micros=1.1)
    result_extra = zshift(result_extra, ((3, 1),), "output_rows")

    gh1_keep, gh1_send, one_sums = call(
        input_grad_body,
        [struct((own_rows, 1024), BF), struct((own_rows, 1024), BF), struct((8, 256), F32)],
        (ids, x, par, gq, gk, after(gv, result), *pieces),
        scratch=[pltpu.VMEM((rows, 1024), F32), pltpu.VMEM((rows, 1024), BF)], micros=7.0)
    gh1_theirs = zshift(gh1_send, PAIR, "input_grad")
    stay_two, send_two = merge(
        ids, [(after(stay_two, gh1_send), got_two, 0, 512), (stay_o, got_o, 0, 128)]
    )
    got_two = fshift(send_two, 4, "two_grad_y")
    keep_q, send_q = call(
        qkv_grad_body,
        [struct((576, 1536), BF), struct((576, 1536), BF)],
        (ids, h1_e, h1_o, gq, gk, after(gv, stay_two), one_sums, mid_sums_0, mid_sums_1, fc1_sums_0, fc1_sums_1),
        scratch=[pltpu.VMEM((8, 1536), F32)], micros=3.3)
    got_q = fshift(send_q, 1, "qkv_grad_core")
    stay_a, send_a, stay_b, send_b = merge(ids, [(keep_q, got_q, 0, 256)], [(keep_q, got_q, 256, 320)])
    got_a = fshift(send_a, 2, "qkv_grad_x")
    got_b = fshift(send_b, 4, "qkv_grad_y")
    mlp_own, *mlp_sends = call(
        line_mlp_body,
        [struct((576, 256), BF)] * 4,
        (ids, after(stay_two, stay_a), got_two, stay_one, got_one),
        scratch=[pltpu.VMEM((320, 1024), BF), pltpu.VMEM((128, 2048), BF)], micros=1.2)
    mlp_gots = [zshift(t, p, "mlp_grad_z") for t, p in zip(mlp_sends, (PAIR, FAR, CROSS))]
    layer_output = call(
        owner_rows_body,
        struct((own_rows, width), BF),
        (ids, valid_lanes, after(result, mlp_own), result_extra), micros=1.5)
    back, back_extra = call(
        input_back_body,
        [struct((own_rows, width), F32), struct((cut, width), BF)],
        (ids, par, x, gb_0, gb_1, after(gh1_keep, layer_output), gh1_theirs),
        scratch=[pltpu.VMEM((rows, width), BF)], micros=4.0)
    back_extra = zshift(back_extra, ((3, 1),), "input_grad_rows")
    stay_a, send_a, stay_b, send_b = merge(
        ids, [(after(stay_a, back), got_a, 0, 128)], [(stay_b, got_b, 0, 160)]
    )
    got_a = fshift(send_a, 4, "qkv_grad_y")
    got_b = fshift(send_b, 2, "qkv_grad_x")
    w_fc1_grad, w_fc2_grad, w_out_grad = call(
        join_mlp_body,
        [struct((128, 1024), F32), struct((512, 256), F32), struct((128, 256), F32)],
        (ids, after(mlp_own, stay_a), *mlp_gots), micros=1.7)
    own, to_pair, to_far, to_cross = call(
        line_body,
        [struct((192, 384), BF)] * 4,
        (ids, after(stay_a, w_out_grad), got_a, stay_b, got_b),
        scratch=[pltpu.VMEM((64, 1536), BF), pltpu.VMEM((80, 1536), BF)], micros=0.8)
    got_pair = zshift(to_pair, PAIR, "qkv_grad_z")
    got_far = zshift(to_far, FAR, "qkv_grad_z")
    got_cross = zshift(to_cross, CROSS, "qkv_grad_z")
    tokens_grad = call(
        owner_rows_body,
        struct((own_rows, width), F32),
        (ids, valid_lanes, after(back, own), back_extra), micros=1.5)
    w_qkv_grad, sums = call(
        join_body,
        [struct((128, 768), F32), struct((9, 128), F32)],
        (ids, own, got_pair, got_far, got_cross),
        scratch=[pltpu.VMEM((4, 128), F32)], micros=1.4)

    def vector(spot):
        return sums[spot, 0:32]

    return (
        layer_output,
        tokens_grad,
        vector(0),
        vector(1),
        w_qkv_grad,
        vector(6),
        vector(7),
        w_out_grad,
        vector(2),
        vector(3),
        vector(4),
        w_fc1_grad,
        sums[8],
        w_fc2_grad,
        vector(5),
    )


def shards(*operands):
    tokens = operands[0]
    fits = (
        lax.axis_size("fsdp") == 8
        and lax.axis_size("seq") == 4
        and tokens.shape == (384, 1024)
        and operands[11].shape == (128, 4096)
    )
    return paired_shards(*operands) if fits else general_shards(*operands)


def solution(mesh):
    return jax.shard_map(
        shards,
        mesh=mesh,
        in_specs=(
            P(("fsdp", "seq"), None),
            P(("fsdp", "seq")),
            P("fsdp"),
            P("fsdp"),
            P("fsdp", None),
            P("fsdp"),
            P("fsdp"),
            P("fsdp", None),
            P("fsdp"),
            P("fsdp"),
            P("fsdp"),
            P("fsdp", None),
            P("fsdp"),
            P("fsdp", None),
            P("fsdp"),
            P(("fsdp", "seq"), None),
        ),
        out_specs=(
            P(("fsdp", "seq"), None),
            P(("fsdp", "seq"), None),
            P(("fsdp", "seq")),
            P(("fsdp", "seq")),
            P("fsdp", "seq"),
            P(("fsdp", "seq")),
            P(("fsdp", "seq")),
            P("fsdp", "seq"),
            P(("fsdp", "seq")),
            P(("fsdp", "seq")),
            P(("fsdp", "seq")),
            P("fsdp", "seq"),
            P(("fsdp", "seq")),
            P("fsdp", "seq"),
            P(("fsdp", "seq")),
        ),
        check_vma=False,
    )
```

```python
from functools import partial

import jax
import jax.numpy as jnp
from jax import lax
from jax.experimental import pallas as pl
from jax.experimental.pallas import tpu as pltpu
from jax.sharding import PartitionSpec as P

HD = 64
LEN = 577


norm_eps = 1e-06
masked_score = -1000000000.0


def normalize(values, gain, shift):
    row_mean = jnp.mean(values, axis=-1, keepdims=True)
    centered = values - row_mean
    variance = jnp.mean(centered * centered, axis=-1, keepdims=True)
    return centered * lax.rsqrt(variance + norm_eps) * gain + shift


def contract_rows(left, right):
    return lax.dot_general(
        left, right, (((0,), (0,)), ((), ())), preferred_element_type=jnp.float32
    )


def times_transposed(left, right):
    return lax.dot_general(
        left, right, (((1,), (1,)), ((), ())), preferred_element_type=jnp.float32
    )


def column_sum(values):
    return jnp.sum(values, axis=0, dtype=jnp.float32)


def shards_per_block(row_count, seq_count):
    for factor in range(1, seq_count + 1):
        if seq_count % factor == 0 and (row_count * factor >= 512 or factor == seq_count):
            return factor
    return seq_count


def add_window(total, delta, start):
    current = lax.dynamic_slice_in_dim(total, start, delta.shape[0], 0)
    return lax.dynamic_update_slice_in_dim(total, current + delta, start, 0)


def general_shards(
    tokens,
    segment_ids,
    ln1_gain,
    ln1_bias,
    w_qkv,
    q_bias,
    v_bias,
    w_out,
    out_bias,
    ln2_gain,
    ln2_bias,
    w_fc1,
    fc1_bias,
    w_fc2,
    fc2_bias,
    cotangent,
):
    row_count = tokens.shape[0]
    feature_width = tokens.shape[1]
    seq_count = lax.axis_size("seq")
    span_rows = row_count * seq_count
    local_heads = feature_width // seq_count // HD
    block_rows = row_count * shards_per_block(row_count, seq_count)
    block_count = span_rows // block_rows
    margin = LEN - 1
    window = block_rows + 2 * margin
    offsets = jnp.arange(block_count, dtype=jnp.int32) * block_rows
    scale = HD ** (-0.5)
    as_float = jnp.float32

    def weight_grad(left, right):
        return contract_rows(left, right)

    attn_set = (
        lax.all_gather(ln1_gain, "fsdp", axis=0, tiled=True),
        lax.all_gather(ln1_bias, "fsdp", axis=0, tiled=True),
        lax.all_gather(w_qkv, "fsdp", axis=0, tiled=True),
        lax.all_gather(q_bias, "fsdp", axis=0, tiled=True),
        lax.all_gather(v_bias, "fsdp", axis=0, tiled=True),
        lax.all_gather(w_out, "fsdp", axis=0, tiled=True),
        lax.all_gather(out_bias, "fsdp", axis=0, tiled=True),
    )
    span_labels = lax.all_gather(segment_ids, "seq", axis=0, tiled=True)
    inputs = tokens.astype(as_float)
    gain_one = attn_set[0].astype(as_float)
    shift_one = attn_set[1].astype(as_float)
    first_norm = normalize(inputs, gain_one, shift_one).astype(jnp.bfloat16)
    projected = jnp.dot(first_norm, attn_set[2], preferred_element_type=as_float)
    bias_all = jnp.concatenate(
        [
            attn_set[3].astype(as_float),
            jnp.zeros((feature_width,), as_float),
            attn_set[4].astype(as_float),
        ]
    )
    packed = (projected + bias_all).astype(jnp.bfloat16).reshape(row_count, 3, feature_width)
    head_rows = lax.all_to_all(packed, "seq", split_axis=2, concat_axis=0, tiled=True)
    query_heads = head_rows[:, 0, :].reshape(span_rows, local_heads, HD)
    key_heads = head_rows[:, 1, :].reshape(span_rows, local_heads, HD)
    value_heads = head_rows[:, 2, :].reshape(span_rows, local_heads, HD)
    key_padded = jnp.pad(key_heads, ((margin, margin), (0, 0), (0, 0)))
    value_padded = jnp.pad(value_heads, ((margin, margin), (0, 0), (0, 0)))
    label_padded = jnp.pad(span_labels, (margin, margin), constant_values=-2)

    def block_scores(offset):
        query_block = lax.dynamic_slice_in_dim(query_heads, offset, block_rows, 0)
        label_block = lax.dynamic_slice_in_dim(span_labels, offset, block_rows, 0)
        key_window = lax.dynamic_slice_in_dim(key_padded, offset, window, 0)
        value_window = lax.dynamic_slice_in_dim(value_padded, offset, window, 0)
        label_window = lax.dynamic_slice_in_dim(label_padded, offset, window, 0)
        scaled = (
            jnp.einsum("qhd,khd->hqk", query_block, key_window, preferred_element_type=as_float)
            * scale
        )
        same_image = label_block[:, None] == label_window[None, :]
        return (
            query_block,
            key_window,
            value_window,
            jnp.where(same_image[None], scaled, masked_score),
        )

    def block_forward(offset):
        unused_query, unused_key, value_window, scores = block_scores(offset)
        row_peak = jnp.max(scores, axis=-1, keepdims=True)
        lifted = jnp.exp(scores - row_peak)
        row_total = jnp.sum(lifted, axis=-1, keepdims=True)
        attn_probs = (lifted / row_total).astype(jnp.bfloat16)
        block_out = jnp.einsum(
            "hqk,khd->qhd", attn_probs, value_window, preferred_element_type=as_float
        ).astype(jnp.bfloat16)
        return (block_out, (row_peak + jnp.log(row_total))[..., 0])

    head_out, log_totals = lax.map(block_forward, offsets)
    head_flat = head_out.reshape(span_rows, local_heads * HD)
    attended = lax.all_to_all(head_flat, "seq", split_axis=0, concat_axis=1, tiled=True)
    mixed = jnp.dot(attended, attn_set[5], preferred_element_type=as_float) + attn_set[6].astype(
        as_float
    )
    middle = inputs + mixed
    mlp_set = (
        lax.all_gather(ln2_gain, "fsdp", axis=0, tiled=True),
        lax.all_gather(ln2_bias, "fsdp", axis=0, tiled=True),
        lax.all_gather(w_fc1, "fsdp", axis=0, tiled=True),
        lax.all_gather(fc1_bias, "fsdp", axis=0, tiled=True),
        lax.all_gather(w_fc2, "fsdp", axis=0, tiled=True),
        lax.all_gather(fc2_bias, "fsdp", axis=0, tiled=True),
    )
    gain_two = mlp_set[0].astype(as_float)
    shift_two = mlp_set[1].astype(as_float)
    second_norm = normalize(middle, gain_two, shift_two).astype(jnp.bfloat16)
    hidden = jnp.dot(second_norm, mlp_set[2], preferred_element_type=as_float) + mlp_set[3].astype(
        as_float
    )
    activated = jax.nn.gelu(hidden, approximate=False).astype(jnp.bfloat16)
    branch = jnp.dot(activated, mlp_set[4], preferred_element_type=as_float) + mlp_set[5].astype(
        as_float
    )
    valid = (segment_ids >= 0).astype(as_float)[:, None]
    layer_output = (valid * (middle + branch)).astype(jnp.bfloat16)
    grad_out = valid * cotangent.astype(as_float)
    grad_branch = grad_out.astype(jnp.bfloat16)
    fc2_bias_part = column_sum(grad_branch)
    w_fc2_part = weight_grad(activated, grad_branch)
    grad_act = times_transposed(grad_branch, mlp_set[4])
    unused_hidden, gelu_back = jax.vjp(partial(jax.nn.gelu, approximate=False), hidden)
    grad_hidden = gelu_back(grad_act)[0].astype(jnp.bfloat16)
    fc1_bias_part = column_sum(grad_hidden)
    w_fc1_part = weight_grad(second_norm, grad_hidden)
    grad_norm_two = times_transposed(grad_hidden, mlp_set[2])
    unused_two, norm_two_back = jax.vjp(
        normalize, middle, mlp_set[0].astype(as_float), mlp_set[1].astype(as_float)
    )
    grad_mid_norm, ln2_gain_part, ln2_bias_part = norm_two_back(grad_norm_two)
    grad_middle = grad_out + grad_mid_norm
    grad_mixed = grad_middle.astype(jnp.bfloat16)
    out_bias_part = column_sum(grad_mixed)
    w_out_part = weight_grad(attended, grad_mixed)
    grad_attended = times_transposed(grad_mixed, attn_set[5]).astype(jnp.bfloat16)
    grad_heads = lax.all_to_all(
        grad_attended, "seq", split_axis=1, concat_axis=0, tiled=True
    ).reshape(span_rows, local_heads, HD)

    def block_backward(running, inputs_block):
        key_total, value_total = running
        offset, log_block = inputs_block
        query_block, key_window, value_window, scores = block_scores(offset)
        grad_block = lax.dynamic_slice_in_dim(grad_heads, offset, block_rows, 0)
        probs_full = jnp.exp(scores - log_block[..., None])
        attn_probs = probs_full.astype(jnp.bfloat16)
        value_delta = jnp.einsum(
            "hqk,qhd->khd", attn_probs, grad_block, preferred_element_type=as_float
        )
        grad_probs = jnp.einsum(
            "qhd,khd->hqk", grad_block, value_window, preferred_element_type=as_float
        )
        row_inner = jnp.sum(grad_probs * probs_full, axis=-1, keepdims=True)
        grad_scores = (probs_full * (grad_probs - row_inner)).astype(jnp.bfloat16)
        grad_query = (
            jnp.einsum("hqk,khd->qhd", grad_scores, key_window, preferred_element_type=as_float)
            * scale
        )
        key_delta = (
            jnp.einsum("hqk,qhd->khd", grad_scores, query_block, preferred_element_type=as_float)
            * scale
        )
        return (
            (
                add_window(key_total, key_delta, offset),
                add_window(value_total, value_delta, offset),
            ),
            grad_query,
        )

    zero_heads = jnp.zeros((span_rows + 2 * margin, local_heads, HD), as_float)
    (key_padded_grad, value_padded_grad), query_grad = lax.scan(
        block_backward, (zero_heads, zero_heads), (offsets, log_totals)
    )
    key_grad = key_padded_grad[margin : margin + span_rows]
    value_grad = value_padded_grad[margin : margin + span_rows]
    head_grads = jnp.concatenate(
        [
            query_grad.reshape(span_rows, 1, local_heads * HD),
            key_grad.reshape(span_rows, 1, local_heads * HD),
            value_grad.reshape(span_rows, 1, local_heads * HD),
        ],
        axis=1,
    ).astype(jnp.bfloat16)
    token_grads = lax.all_to_all(
        head_grads, "seq", split_axis=0, concat_axis=2, tiled=True
    ).reshape(row_count, 3 * feature_width)
    q_bias_part = column_sum(token_grads[:, :feature_width])
    v_bias_part = column_sum(token_grads[:, 2 * feature_width :])
    w_qkv_part = weight_grad(first_norm, token_grads)
    grad_norm_one = times_transposed(token_grads, attn_set[2])
    unused_one, norm_one_back = jax.vjp(
        normalize, inputs, attn_set[0].astype(as_float), attn_set[1].astype(as_float)
    )
    grad_input_norm, ln1_gain_part, ln1_bias_part = norm_one_back(grad_norm_one)
    tokens_grad = grad_middle + grad_input_norm
    partial_sums = (
        lax.psum_scatter(
            ln1_gain_part.astype(jnp.bfloat16), "fsdp", scatter_dimension=0, tiled=True
        ).astype(jnp.float32),
        lax.psum_scatter(
            ln1_bias_part.astype(jnp.bfloat16), "fsdp", scatter_dimension=0, tiled=True
        ).astype(jnp.float32),
        lax.psum_scatter(
            w_qkv_part.astype(jnp.bfloat16), "fsdp", scatter_dimension=0, tiled=True
        ).astype(jnp.float32),
        lax.psum_scatter(
            q_bias_part.astype(jnp.bfloat16), "fsdp", scatter_dimension=0, tiled=True
        ).astype(jnp.float32),
        lax.psum_scatter(
            v_bias_part.astype(jnp.bfloat16), "fsdp", scatter_dimension=0, tiled=True
        ).astype(jnp.float32),
        lax.psum_scatter(
            w_out_part.astype(jnp.bfloat16), "fsdp", scatter_dimension=0, tiled=True
        ).astype(jnp.float32),
        lax.psum_scatter(
            out_bias_part.astype(jnp.bfloat16), "fsdp", scatter_dimension=0, tiled=True
        ).astype(jnp.float32),
        lax.psum_scatter(
            ln2_gain_part.astype(jnp.bfloat16), "fsdp", scatter_dimension=0, tiled=True
        ).astype(jnp.float32),
        lax.psum_scatter(
            ln2_bias_part.astype(jnp.bfloat16), "fsdp", scatter_dimension=0, tiled=True
        ).astype(jnp.float32),
        lax.psum_scatter(
            w_fc1_part.astype(jnp.bfloat16), "fsdp", scatter_dimension=0, tiled=True
        ).astype(jnp.float32),
        lax.psum_scatter(
            fc1_bias_part.astype(jnp.bfloat16), "fsdp", scatter_dimension=0, tiled=True
        ).astype(jnp.float32),
        lax.psum_scatter(
            w_fc2_part.astype(jnp.bfloat16), "fsdp", scatter_dimension=0, tiled=True
        ).astype(jnp.float32),
        lax.psum_scatter(
            fc2_bias_part.astype(jnp.bfloat16), "fsdp", scatter_dimension=0, tiled=True
        ).astype(jnp.float32),
    )
    summed = (
        lax.psum_scatter(
            partial_sums[0].astype(jnp.bfloat16), "seq", scatter_dimension=0, tiled=True
        ).astype(jnp.float32),
        lax.psum_scatter(
            partial_sums[1].astype(jnp.bfloat16), "seq", scatter_dimension=0, tiled=True
        ).astype(jnp.float32),
        lax.psum_scatter(
            partial_sums[2].astype(jnp.bfloat16), "seq", scatter_dimension=1, tiled=True
        ).astype(jnp.float32),
        lax.psum_scatter(
            partial_sums[3].astype(jnp.bfloat16), "seq", scatter_dimension=0, tiled=True
        ).astype(jnp.float32),
        lax.psum_scatter(
            partial_sums[4].astype(jnp.bfloat16), "seq", scatter_dimension=0, tiled=True
        ).astype(jnp.float32),
        lax.psum_scatter(
            partial_sums[5].astype(jnp.bfloat16), "seq", scatter_dimension=1, tiled=True
        ).astype(jnp.float32),
        lax.psum_scatter(
            partial_sums[6].astype(jnp.bfloat16), "seq", scatter_dimension=0, tiled=True
        ).astype(jnp.float32),
        lax.psum_scatter(
            partial_sums[7].astype(jnp.bfloat16), "seq", scatter_dimension=0, tiled=True
        ).astype(jnp.float32),
        lax.psum_scatter(
            partial_sums[8].astype(jnp.bfloat16), "seq", scatter_dimension=0, tiled=True
        ).astype(jnp.float32),
        lax.psum_scatter(
            partial_sums[9].astype(jnp.bfloat16), "seq", scatter_dimension=1, tiled=True
        ).astype(jnp.float32),
        lax.psum_scatter(
            partial_sums[10].astype(jnp.bfloat16), "seq", scatter_dimension=0, tiled=True
        ).astype(jnp.float32),
        lax.psum_scatter(
            partial_sums[11].astype(jnp.bfloat16), "seq", scatter_dimension=1, tiled=True
        ).astype(jnp.float32),
        lax.psum_scatter(
            partial_sums[12].astype(jnp.bfloat16), "seq", scatter_dimension=0, tiled=True
        ).astype(jnp.float32),
    )
    return (
        layer_output,
        tokens_grad,
        summed[0],
        summed[1],
        summed[2],
        summed[3],
        summed[4],
        summed[5],
        summed[6],
        summed[7],
        summed[8],
        summed[9],
        summed[10],
        summed[11],
        summed[12],
    )


LX = (0, 4, 2, 6, 1, 5, 3, 7)
LY = (0, 2, 4, 6, 1, 3, 5, 7)
PAIR = ((0, 1), (1, 0), (2, 3), (3, 2))
FAR = ((0, 2), (2, 0), (1, 3), (3, 1))
CROSS = ((0, 3), (3, 0), (1, 2), (2, 1))
BF = jnp.bfloat16
F32 = jnp.float32
RATE = 1.6e9
SMEM_SPEC = pl.BlockSpec(memory_space=pltpu.SMEM)
VMEM_SPEC = pl.BlockSpec(memory_space=pltpu.VMEM)
HALF_ROOT = 0.7071067811865476
DENSITY = 0.3989422804014327


def fshift(values, bit, name="move"):
    with jax.named_scope(name):
        return lax.ppermute(values, "fsdp", [(i, i ^ bit) for i in range(8)])


def zshift(values, pairs, name="move"):
    with jax.named_scope(name):
        return lax.ppermute(values, "seq", pairs)


def after(values, *earlier):
    return lax.optimization_barrier((values, *earlier))[0]


def cost(micros):
    return pl.CostEstimate(flops=int(micros * RATE) + 1, bytes_accessed=1, transcendentals=0)


def call(body, outs, args, scratch=(), micros=1.0, limit=12, space=pltpu.VMEM):
    single = not isinstance(outs, (list, tuple))
    shapes = [outs] if single else list(outs)
    result = pl.pallas_call(
        body,
        out_shape=shapes,
        in_specs=[SMEM_SPEC] + [pl.BlockSpec(memory_space=space)] * (len(args) - 1),
        out_specs=[VMEM_SPEC] * len(shapes),
        scratch_shapes=list(scratch),
        compiler_params=pltpu.CompilerParams(vmem_limit_bytes=limit * 2**20),
        cost_estimate=cost(micros),
    )(*args)
    return result[0] if single else result


def struct(shape, dtype):
    return jax.ShapeDtypeStruct(shape, dtype)


def lanes_low(shape):
    return lax.broadcasted_iota(jnp.int32, shape, 1) < HD


def dot_nn(a, b):
    return lax.dot_general(a, b, (((1,), (0,)), ((), ())), preferred_element_type=F32)


def dot_nt(a, b):
    return lax.dot_general(a, b, (((1,), (1,)), ((), ())), preferred_element_type=F32)


def dot_tn(a, b):
    return lax.dot_general(a, b, (((0,), (0,)), ((), ())), preferred_element_type=F32)


def offset(index, size):
    return pl.multiple_of(index * size, size)


def natural(ref, start):
    return jnp.concatenate([ref[i : i + 1, start : start + 128] for i in range(8)], axis=1)


def pick_qkv(ids, w_hbm, tokens_hbm, wo_hbm, *refs):
    count = (len(refs) - 6) // 2
    rows_hbm, rows, sems = refs[:count], refs[count + 5 : -1], refs[-1]
    out_ref, both_ref, extra_ref, w_ref, wo_ref = refs[count : count + 5]
    half = ids[1] % 2
    cut = tokens_hbm.shape[0] // 2
    copies = [(w_hbm, w_ref), (tokens_hbm.at[pl.ds(cut, cut)], extra_ref)]
    copies += [(wo_hbm.at[pl.ds(offset(half, 64), 64)], wo_ref), *zip(rows_hbm, rows)]
    copies = [pltpu.make_async_copy(source, target, sems.at[i]) for i, (source, target) in enumerate(copies)]
    for copy in copies:
        copy.start()
    for copy in copies:
        copy.wait()
    low = lanes_low((128, 128))
    for j in range(w_ref.shape[1] // 256):
        first = w_ref[:, 256 * j : 256 * j + 128].astype(F32)
        second = w_ref[:, 256 * j + 128 : 256 * j + 256].astype(F32)
        even = jnp.where(low, first, pltpu.roll(second, HD, 1))
        odd = jnp.where(low, pltpu.roll(first, HD, 1), second)
        out_ref[0:128, 128 * j : 128 * j + 128] = jnp.where(half == 0, even, odd).astype(BF)
    start = 0
    for row_ref in rows:
        size = row_ref.shape[0]
        row = row_ref[...].astype(F32)
        out_ref[128:144, start : start + size] = jnp.broadcast_to(row.reshape(1, size), (16, size)).astype(BF)
        start += size
    both_ref[0:144, :] = out_ref[...]
    pack_out(both_ref, 144, wo_ref[...])


def pick_mlp(ids, w1_hbm, w2_hbm, wo_hbm, one_ref, two_ref, sems):
    half = ids[1] % 2
    out_hbm = wo_hbm.at[pl.ds(offset(half, 64), 64)]
    copies = [
        (w2_hbm.at[pl.ds(offset(half, 256), 256)], two_ref.at[pl.ds(0, 256)]),
        (out_hbm, one_ref.at[pl.ds(256, 64)]),
        (out_hbm, two_ref.at[pl.ds(256, 64)]),
    ]
    for b in range(8):
        rows, lanes = pl.ds(128 * (b // 4), 128), pl.ds(256 * (b % 4), 256)
        copies.append((w1_hbm.at[:, pl.ds(offset(2 * b + half, 256), 256)], one_ref.at[rows, lanes]))
    copies = [pltpu.make_async_copy(source, target, sems.at[i]) for i, (source, target) in enumerate(copies)]
    for copy in copies:
        copy.start()
    for copy in copies:
        copy.wait()


def stack_mlp_body(ids, one_ref, one_x_ref, two_ref, two_y_ref, both_ref, one_out, two_out, outs):
    one_out[0:256, :] = one_ref[0:256, :]
    one_out[256:512, :] = one_x_ref[0:256, :]
    two_out[0:256, :] = two_ref[0:256, :]
    two_out[256:512, :] = two_y_ref[0:256, :]
    outs[0:64, :] = one_ref[256:320, :]
    outs[64:128, :] = one_x_ref[256:320, :]
    outs[128:192, :] = two_y_ref[256:320, :]
    for i in range(2):
        lanes = slice(512 * i, 512 * i + 512)
        outs[192:240, lanes] = both_ref[144:192, lanes]
        outs[240:256, lanes] = both_ref[144 + 16 * i : 160 + 16 * i, 1024:1536]


def stack_body(sizes, ids, *refs):
    out_ref = refs[-1]
    start = 0
    for ref, size in zip(refs[:-1], sizes):
        out_ref[start : start + size, :] = ref[0:size, :]
        start += size


def stack(ids, *arrays, sizes=None):
    sizes = sizes or tuple(a.shape[0] for a in arrays)
    shape = struct((sum(sizes), arrays[0].shape[1]), BF)
    return call(partial(stack_body, sizes), shape, (ids, *arrays), micros=0.7)


def place_rows(ids, own_ref, theirs_ref, two_ref, three_ref, out_ref):
    half = ids[1] % 2
    pair = ids[1] // 2
    own_rows = own_ref.shape[0]
    cut = two_ref.shape[0]
    tail = out_ref.shape[0] - own_rows - cut
    for value in range(2):
        first, second = (own_ref, theirs_ref) if value == 0 else (theirs_ref, own_ref)

        @pl.when(half == value)
        def _():
            out_ref[0:own_rows, :] = first[...]

        @pl.when((half == value) & (pair == 0))
        def _():
            out_ref[own_rows:, :] = second[0 : cut + tail, :]

        @pl.when((half == value) & (pair == 1))
        def _():
            out_ref[own_rows + cut :, :] = second[0:tail, :]

    @pl.when(pair == 1)
    def _():
        out_ref[own_rows : own_rows + cut, :] = two_ref[...] + three_ref[...]


def place_grad_body(ids, own_ref, theirs_ref, two_ref, three_ref, out_ref):
    place_rows(ids, own_ref, theirs_ref, two_ref, three_ref, out_ref)
    own_rows = own_ref.shape[0]
    rows = out_ref.shape[0]
    live = key_valid(ids, (rows - own_rows, 1), 0, own_rows, own_rows)
    tail = out_ref[own_rows:, :].astype(F32)
    out_ref[own_rows:, :] = jnp.where(live, tail, 0.0).astype(BF)


def parts_of(refs):
    a, x, y, d, other = refs
    parts = {0: (a, 0), 2: (x, 0), 4: (y, 0), 6: (d, 0)}
    parts.update({2 * i + 1: (other, 144 * i) for i in range(4)})
    return parts


def piece_tile(parts, k, lanes):
    ref, row = parts[k]
    return ref[row : row + 128, lanes]


def qkv_body(ids, own_ref, theirs_ref, two_ref, three_ref, *refs):
    parts = parts_of(refs[:5])
    x_ref, qkv_ref, even_ref, odd_ref, par_ref, norm_ref, bias_ref = refs[5:]
    place_rows(ids, own_ref, theirs_ref, two_ref, three_ref, x_ref)
    f = ids[0]
    half = ids[1] % 2
    rows = x_ref.shape[0]
    for k in range(8):
        ref, at = parts[k]
        par_ref[pl.ds(f ^ k, 1), :] = ref[at + 128 : at + 129, :].astype(F32)
    gain = natural(par_ref, 0)
    shift = natural(par_ref, 128)
    low = lanes_low((1, 128))
    bias_ref[...] = jnp.zeros_like(bias_ref)
    for start, place in ((768, 0), (896, 1024)):
        block = par_ref[:, start : start + 128]
        turned = pltpu.roll(block, HD, 1)
        lower = jnp.where(half == 0, block, turned)
        upper = jnp.where(half == 0, turned, block)
        for j in range(4):
            bias_ref[:, place + 128 * j : place + 128 * j + 128] = jnp.where(
                low, lower[2 * j : 2 * j + 1], upper[2 * j + 1 : 2 * j + 2]
            )

    def norm(i, carry):
        at = pl.ds(offset(i, 32), 32)
        values = x_ref[at, :].astype(F32)
        norm_ref[at, :] = normalize(values, gain, shift).astype(BF)
        return carry

    lax.fori_loop(0, rows // 32, norm, 0)
    for place, k in enumerate(LY):
        target = even_ref if place < 4 else odd_ref
        column = 128 * (place % 4)
        target[:, column : column + 128] = norm_ref[:, pl.ds(offset(f ^ k, 128), 128)]
    left = jnp.concatenate([even_ref[...], odd_ref[...]], axis=1)
    for n in range(6):
        lanes = slice(256 * n, 256 * n + 256)
        weight = jnp.concatenate([piece_tile(parts, k, lanes) for k in LY], axis=0)
        qkv_ref[:, lanes] = (dot_nn(left, weight) + bias_ref[:, lanes]).astype(BF)


def key_valid(ids, shape, axis, own_rows, first=0):
    pair = ids[1] // 2
    place = lax.broadcasted_iota(jnp.int32, shape, axis) + first
    return (place < LEN + pair) & ((place != own_rows) | (pair == 0))


def head_masked(block, head, factor=None):
    wide = block.astype(F32)
    low = lanes_low(wide.shape)
    keep = low if head == 0 else jnp.logical_not(low)
    if factor is not None:
        wide = wide * factor
    return jnp.where(keep, wide, 0.0).astype(BF)


def attend_body(own_rows, tile, ids, q_ref, k_ref, v_ref, o_ref):
    rows = q_ref.shape[0]
    value = v_ref[...]
    live = key_valid(ids, (1, rows), 1, own_rows)
    low = lanes_low((tile, 128))
    keys = [head_masked(k_ref[...], head, HD**-0.5) for head in range(2)]
    for t in range(rows // tile):
        at = slice(t * tile, t * tile + tile)
        outs = []
        for head in range(2):
            scores = jnp.where(live, dot_nt(q_ref[at, :], keys[head]), masked_score)
            peak = jnp.max(scores, axis=1, keepdims=True)
            lifted = jnp.exp(scores - peak)
            total = jnp.sum(lifted, axis=1, keepdims=True)
            outs.append(dot_nn(lifted.astype(BF), value) / total)
        o_ref[at, :] = jnp.where(low, outs[0], outs[1]).astype(BF)


def attend_back_body(own_rows, tile, ids, q_ref, k_ref, v_ref, g0_ref, g1_ref, gq_ref, gk_ref, gv_ref):
    rows = q_ref.shape[0]
    whole = jnp.concatenate([g0_ref[...], g1_ref[...]], axis=0)
    scale = HD**-0.5
    live = key_valid(ids, (rows, 1), 0, own_rows)
    low = lanes_low((rows, 128))
    grads_k = []
    grads_v = []
    for t in range(rows // tile):
        at = slice(t * tile, t * tile + tile)
        query = q_ref[at, :]
        grad = whole[at]
        grad_q = None
        for head in range(2):
            keys = head_masked(k_ref[...], head, scale)
            values = head_masked(v_ref[...], head)
            scores = jnp.where(live, dot_nt(keys, query), masked_score)
            peak = jnp.max(scores, axis=0, keepdims=True)
            lifted = jnp.exp(scores - peak)
            probs = lifted * (1.0 / jnp.sum(lifted, axis=0, keepdims=True))
            grad_p = dot_nt(values, grad)
            inner = jnp.sum(grad_p * probs, axis=0, keepdims=True)
            grad_s = (probs * (grad_p - inner)).astype(BF)
            grad_v = dot_nn(probs.astype(BF), grad)
            grad_k = dot_nn(grad_s, query) * scale
            part = dot_tn(grad_s, keys)
            grad_q = part if grad_q is None else grad_q + part
            if t == 0:
                grads_k.append(grad_k)
                grads_v.append(grad_v)
            else:
                grads_k[head] = grads_k[head] + grad_k
                grads_v[head] = grads_v[head] + grad_v
        gq_ref[at, :] = grad_q.astype(BF)
    gk_ref[...] = jnp.where(low, grads_k[0], grads_k[1]).astype(BF)
    gv_ref[...] = jnp.where(low, grads_v[0], grads_v[1]).astype(BF)


def mixed_body(ids, o_ref, even_ref, odd_ref, first_ref, second_ref, w_ref):
    f = ids[0]
    for place, k in enumerate((0, 2, 4, 6)):
        row = HD * place
        w_ref[pl.ds(offset(f ^ k, HD), HD), :] = even_ref[row : row + HD, :]
        w_ref[pl.ds(offset(f ^ k ^ 1, HD), HD), :] = odd_ref[row : row + HD, :]
    size = first_ref.shape[0]
    for n in range(4):
        lanes = slice(256 * n, 256 * n + 256)
        first_ref[:, lanes] = dot_nn(o_ref[0:size, :], w_ref[:, lanes]).astype(BF)
    for n in range(4):
        lanes = slice(256 * n, 256 * n + 256)
        second_ref[:, lanes] = dot_nn(o_ref[size:, :], w_ref[:, lanes]).astype(BF)


def middle_body(base, ids, par_ref, x_ref, mine_ref, theirs_ref, mid_ref, even_ref, odd_ref, norm_ref):
    f = ids[0]
    rows = mid_ref.shape[0]
    gain = natural(par_ref, 384)
    shift = natural(par_ref, 512)
    bias = natural(par_ref, 256)

    def norm(i, carry):
        at = pl.ds(offset(i, 32), 32)
        middle = x_ref[pl.ds(pl.multiple_of(base + i * 32, 32), 32), :].astype(F32)
        middle = middle + (mine_ref[at, :].astype(F32) + theirs_ref[at, :].astype(F32) + bias)
        mid_ref[at, :] = middle
        norm_ref[at, :] = normalize(middle, gain, shift).astype(BF)
        return carry

    lax.fori_loop(0, rows // 32, norm, 0)
    for place, k in enumerate(LY):
        target = even_ref if place < 4 else odd_ref
        column = 128 * (place % 4)
        target[:, column : column + 128] = norm_ref[:, pl.ds(offset(f ^ k, 128), 128)]


def mlp_body(base, ids, par_ref, even_ref, odd_ref, gm_ref, one_a, one_b, two_a, two_b, *refs):
    act_e_ref, act_o_ref, gu_ref, gh_ref, bias_ref, u_ref, g_ref = refs
    f = ids[0]
    half = ids[1] % 2
    rows = even_ref.shape[0]

    def one_rows(place, start, size, lanes):
        ref = one_a if place < 4 else one_b
        return ref[pl.ds(256 * (place % 4) + start, size), lanes]

    left = jnp.concatenate([even_ref[...], odd_ref[...]], axis=1)
    grad = gm_ref[base : base + rows, :]
    for place, k in enumerate(LX):
        block = f ^ k
        at_lanes = pl.ds(offset(block % 4, 256), 256)
        weight = jnp.concatenate([one_rows(j, offset(block // 4, 128), 128, at_lanes) for j in range(8)], axis=0)
        u_ref[...] = dot_nn(left, weight)
        two_ref = two_a if place < 4 else two_b
        g_ref[...] = dot_nt(grad, two_ref[256 * (place % 4) : 256 * (place % 4) + 256, :])
        row = par_ref[pl.ds(block, 1), pl.ds(offset(4 + half, 256), 256)]
        act_ref = act_e_ref if place < 4 else act_o_ref
        column = 256 * (place % 4)

        def gelu(i, total):
            at = pl.ds(offset(i, 32), 32)
            u = u_ref[at, :] + row
            cdf = 0.5 + 0.5 * lax.erf(u * HALF_ROOT)
            act_ref[at, column : column + 256] = (u * cdf).astype(BF)
            slope = cdf + u * (jnp.exp(-0.5 * (u * u)) * DENSITY)
            gu = (g_ref[at, :] * slope).astype(BF)
            gu_ref[at, pl.ds(offset(block, 256), 256)] = gu
            return total + jnp.sum(gu.astype(F32), axis=0, keepdims=True)

        total = lax.fori_loop(0, rows // 32, gelu, jnp.zeros((1, 256), F32))
        bias_ref[pl.ds(block, 1), :] = total
    for j in range(4):
        total = None
        for part in range(2):
            weight = jnp.concatenate(
                [one_rows(place, 128 * part, 128, slice(None)) for place in (2 * j, 2 * j + 1)], axis=0
            )
            term = dot_nt(gu_ref[:, 1024 * part : 1024 * part + 1024], weight)
            total = term if total is None else total + term
        gh_ref[:, pl.ds(offset(f ^ LY[2 * j], 128), 128)] = total[:, 0:128].astype(BF)
        gh_ref[:, pl.ds(offset(f ^ LY[2 * j + 1], 128), 128)] = total[:, 128:256].astype(BF)


def out_body(ids, e0_ref, o0_ref, e1_ref, o1_ref, two_a, two_b, keep_ref, send_ref, y_ref):
    half = ids[1] % 2
    for n in range(4):
        lanes = slice(256 * n, 256 * n + 256)
        weight = jnp.concatenate([two_a[:, lanes], two_b[:, lanes]], axis=0)
        start = 0
        for e_ref, o_ref in ((e0_ref, o0_ref), (e1_ref, o1_ref)):
            left = jnp.concatenate([e_ref[...], o_ref[...]], axis=1)
            y_ref[start : start + left.shape[0], lanes] = dot_nn(left, weight).astype(BF)
            start += left.shape[0]
    rows = keep_ref.shape[0]
    shift = y_ref.shape[0] - rows
    keep_ref[...] = y_ref[pl.ds(offset(half, shift), rows), :]
    send_ref[...] = y_ref[pl.ds(offset(1 - half, shift), rows), :]


def result_body(ids, par_ref, mid0_ref, mid1_ref, mine_ref, theirs_ref, out_ref, extra_ref):
    half = ids[1] % 2
    bias = natural(par_ref, 640)
    rows = out_ref.shape[0]
    shift = mid0_ref.shape[0] + mid1_ref.shape[0] - rows

    def step(i, carry):
        at = pl.ds(offset(i, 32), 32)
        place = half * shift + i * 32
        total = mine_ref[at, :].astype(F32) + theirs_ref[at, :].astype(F32) + bias
        size = mid0_ref.shape[0]

        @pl.when(place < size)
        def _():
            out_ref[at, :] = (total + mid0_ref[pl.ds(pl.multiple_of(place, 32), 32), :]).astype(BF)

        @pl.when(place >= size)
        def _():
            out_ref[at, :] = (total + mid1_ref[pl.ds(pl.multiple_of(place - size, 32), 32), :]).astype(BF)

        return carry

    lax.fori_loop(0, rows // 32, step, 0)
    spot = rows - shift
    extra_ref[...] = out_ref[spot : spot + extra_ref.shape[0], :]


def owner_rows_body(ids, valid_ref, full_ref, extra_ref, out_ref):
    half = ids[1] % 2
    pair = ids[1] // 2
    rows, cut = full_ref.shape[0], extra_ref.shape[0]
    tail = 2 * cut + 32 - rows
    shift = cut + tail
    spot = rows - shift
    width = full_ref.shape[1]

    def masked(at, values):
        valid = jnp.concatenate([valid_ref[at, :]] * (width // 128), axis=1)
        return jnp.where(valid > 0.0, values.astype(F32), 0.0).astype(out_ref.dtype)

    @pl.when(half == 0)
    def _():
        out_ref[...] = masked(slice(None), full_ref[...])

    @pl.when((half == 1) & (pair == 0))
    def _():
        top = slice(0, cut)
        out_ref[top, :] = masked(top, full_ref[spot : spot + cut, :])
        low = slice(cut, rows)
        border = full_ref[spot + cut : spot + cut + 1, :].astype(F32)
        first = lax.broadcasted_iota(jnp.int32, (cut, 1), 0) == 0
        out_ref[low, :] = masked(low, jnp.where(first, border, extra_ref[...].astype(F32)))

    @pl.when((half == 1) & (pair == 1))
    def _():
        top = slice(0, tail)
        out_ref[top, :] = masked(top, full_ref[spot + cut : spot + cut + tail, :])
        out_ref[tail:rows, :] = jnp.zeros((rows - tail, width), out_ref.dtype)


def rows_grad_body(step, ids, l0_ref, l1_ref, r0_ref, r1_ref, out_ref):
    rows = l0_ref.shape[0] + l1_ref.shape[0]
    left = jnp.concatenate([l0_ref[...], l1_ref[...]], axis=0)
    for n in range(out_ref.shape[1] // step):
        lanes = slice(step * n, step * n + step)
        if r0_ref.shape[0] == rows:
            right = r0_ref[:, lanes]
        else:
            right = jnp.concatenate([r0_ref[:, lanes], r1_ref[:, lanes]], axis=0)
        out_ref[:, lanes] = dot_tn(left, right).astype(BF)


def norm_back(values, grad, gain):
    center = values - jnp.mean(values, axis=-1, keepdims=True)
    scale = lax.rsqrt(jnp.mean(center * center, axis=-1, keepdims=True) + norm_eps)
    unit = center * scale
    scaled = grad * gain
    first = jnp.mean(scaled, axis=-1, keepdims=True)
    second = jnp.mean(scaled * unit, axis=-1, keepdims=True)
    return unit, scale * (scaled - first - unit * second)


def fold(values):
    total = values[0:8]
    for i in range(1, values.shape[0] // 8):
        total = total + values[8 * i : 8 * i + 8]
    return total


def spread(ref, start, partial_rows):
    row = jnp.sum(partial_rows, axis=0, keepdims=True)
    for i in range(8):
        ref[i : i + 1, start : start + 128] = row[:, 128 * i : 128 * i + 128]


def middle_back_body(base, ids, par_ref, mid_ref, gm_ref, mine_ref, theirs_ref, w_ref, gb_ref, go_ref, sums_ref):
    half = ids[1] % 2
    counts = jnp.where(half == 0, 1.0, 0.0)
    gain = natural(par_ref, 384)
    rows = mid_ref.shape[0]

    def step(i, carry):
        out_sum, gain_sum, shift_sum, last_sum = carry
        at = pl.ds(offset(i, 32), 32)
        mine = mine_ref[at, :].astype(F32)
        grad = mine + theirs_ref[at, :].astype(F32)
        unit, back = norm_back(mid_ref[at, :], grad, gain)
        gm = gm_ref[pl.ds(pl.multiple_of(base + i * 32, 32), 32), :].astype(F32)
        gb = (gm + back).astype(BF)
        gb_ref[at, :] = gb
        return (
            out_sum + fold(gb.astype(F32)),
            gain_sum + fold(mine * unit),
            shift_sum + fold(mine),
            last_sum + fold(gm),
        )

    zero = jnp.zeros((8, mid_ref.shape[1]), F32)
    sums = lax.fori_loop(0, rows // 32, step, (zero, zero, zero, zero))
    spread(sums_ref, 0, sums[0] * counts)
    spread(sums_ref, 128, sums[1])
    spread(sums_ref, 256, sums[2])
    spread(sums_ref, 384, sums[3] * counts)
    grad = gb_ref[...]
    for n in range(2):
        rows = slice(256 * n, 256 * n + 256)
        go_ref[:, rows] = dot_nt(grad, w_ref[rows, :]).astype(BF)


def out_grad_body(ids, o_ref, gb0_ref, gb1_ref, keep_ref, send_ref, grad_ref):
    f = ids[0]
    for n in range(4):
        lanes = slice(256 * n, 256 * n + 256)
        right = jnp.concatenate([gb0_ref[:, lanes], gb1_ref[:, lanes]], axis=0)
        grad_ref[:, lanes] = dot_tn(o_ref[...], right).astype(BF)
    for place, k in enumerate(LX):
        target = keep_ref if place < 4 else send_ref
        row = HD * (place % 4)
        target[row : row + HD, :] = grad_ref[pl.ds(offset(f ^ k, HD), HD), :]


def input_grad_body(ids, x_ref, par_ref, gq_ref, gk_ref, gv_ref, *refs):
    parts = parts_of(refs[:5])
    keep_ref, send_ref, sums_ref, wide_ref, gh_ref = refs[5:]
    f = ids[0]
    left = jnp.concatenate([gq_ref[...], gk_ref[...], gv_ref[...]], axis=1)
    for j in range(4):
        first, second = LY[2 * j], LY[2 * j + 1]
        weight = jnp.concatenate(
            [piece_tile(parts, first, slice(None)), piece_tile(parts, second, slice(None))], axis=0
        )
        total = dot_nt(left, weight)
        wide_ref[:, pl.ds(offset(f ^ first, 128), 128)] = total[:, 0:128]
        wide_ref[:, pl.ds(offset(f ^ second, 128), 128)] = total[:, 128:256]

    def step(i, carry):
        gain_sum, shift_sum = carry
        at = pl.ds(offset(i, 32), 32)
        grad = wide_ref[at, :]
        gh_ref[at, :] = grad.astype(BF)
        values = x_ref[at, :].astype(F32)
        center = values - jnp.mean(values, axis=-1, keepdims=True)
        unit = center * lax.rsqrt(jnp.mean(center * center, axis=-1, keepdims=True) + norm_eps)
        return gain_sum + fold(grad * unit), shift_sum + fold(grad)

    zero = jnp.zeros((8, x_ref.shape[1]), F32)
    gain_sum, shift_sum = lax.fori_loop(0, x_ref.shape[0] // 32, step, (zero, zero))
    half = ids[1] % 2
    rows = keep_ref.shape[0]
    shift = x_ref.shape[0] - rows
    keep_ref[...] = gh_ref[pl.ds(offset(half, shift), rows), :]
    send_ref[...] = gh_ref[pl.ds(offset(1 - half, shift), rows), :]
    spread(sums_ref, 0, gain_sum)
    spread(sums_ref, 128, shift_sum)


def qkv_grad_body(ids, even_ref, odd_ref, gq_ref, gk_ref, gv_ref, one_ref, mid0_ref, mid1_ref, fc0_ref, fc1_ref, *refs):
    keep_ref, send_ref, par_ref = refs
    f = ids[0]
    half = ids[1] % 2
    par_ref[:, 0:256] = one_ref[...]
    par_ref[:, 256:768] = mid0_ref[...] + mid1_ref[...]
    fc_sum = fc0_ref[...] + fc1_ref[...]
    low = lanes_low((1, 128))
    mine = low == (half == 0)
    for g_ref, place in ((gq_ref, 768), (gv_ref, 896)):
        row = jnp.sum(g_ref[...].astype(F32), axis=0, keepdims=True)
        for j in range(4):
            block = row[:, 128 * j : 128 * j + 128]
            turned = pltpu.roll(jnp.broadcast_to(block, (8, 128)), HD, 1)[0:1]
            first = jnp.where(half == 0, block, turned)
            second = jnp.where(half == 0, turned, block)
            par_ref[2 * j : 2 * j + 1, place : place + 128] = jnp.where(mine, first, 0.0)
            par_ref[2 * j + 1 : 2 * j + 2, place : place + 128] = jnp.where(mine, second, 0.0)
    zero = jnp.zeros((8, 256), F32)
    par_ref[:, 1024:1280] = jnp.where(half == 0, fc_sum, zero)
    par_ref[:, 1280:1536] = jnp.where(half == 1, fc_sum, zero)
    order_b = LY
    place_a = {k: i for i, k in enumerate(LX)}
    for j in range(4):
        source = even_ref if j < 2 else odd_ref
        left = source[:, 256 * (j % 2) : 256 * (j % 2) + 256]
        for n, g_ref in enumerate((gq_ref, gk_ref, gv_ref)):
            lanes = slice(512 * n, 512 * n + 512)
            total = dot_tn(left, g_ref[...]).astype(BF)
            for i in range(2):
                k = order_b[2 * j + i]
                target = keep_ref if place_a[k] < 4 else send_ref
                row = 64 * (place_a[k] % 4)
                target[row : row + 64, lanes] = total[128 * i : 128 * i + 64]
                row = 256 + 80 * ((2 * j + i) % 4)
                target[row : row + 64, lanes] = total[128 * i + 64 : 128 * i + 128]
    for place, k in enumerate(order_b):
        target = keep_ref if place < 4 else send_ref
        row = 320 + 80 * (place % 4)
        target[row : row + 16, :] = jnp.broadcast_to(par_ref[pl.ds(f ^ k, 1), :], (16, 1536)).astype(BF)


def input_back_body(ids, par_ref, x_ref, gb0_ref, gb1_ref, mine_ref, theirs_ref, out_ref, extra_ref, gb_ref):
    half = ids[1] % 2
    gain = natural(par_ref, 0)
    rows = out_ref.shape[0]
    shift = x_ref.shape[0] - rows
    size = gb0_ref.shape[0]
    gb_ref[0:size, :] = gb0_ref[...]
    gb_ref[size:, :] = gb1_ref[...]

    def step(i, carry):
        at = pl.ds(offset(i, 32), 32)
        place = pl.ds(pl.multiple_of(half * shift + i * 32, 32), 32)
        grad = mine_ref[at, :].astype(F32) + theirs_ref[at, :].astype(F32)
        back = norm_back(x_ref[place, :].astype(F32), grad, gain)[1]
        out_ref[at, :] = gb_ref[place, :].astype(F32) + back
        return carry

    lax.fori_loop(0, rows // 32, step, 0)
    spot = rows - shift
    extra_ref[...] = out_ref[spot : spot + extra_ref.shape[0], :].astype(BF)


def line_body(ids, ka_ref, ra_ref, kb_ref, rb_ref, ko_ref, ro_ref, *outs):
    s = ids[1]
    wide_a, wide_b, wide_o = outs[4:]
    wide_a[...] = halve(ka_ref[...], ra_ref[...])
    wide_b[...] = halve(kb_ref[...], rb_ref[...])
    for i in range(2):
        lanes = slice(512 * i, 512 * i + 512)
        wide_o[0:48, lanes] = halve(ko_ref[0:48, lanes], ro_ref[160:208, lanes])
        wide_o[48:64, lanes] = halve(ko_ref[48:64, lanes], ro_ref[160 + 16 * i : 176 + 16 * i, 1024:1536])
    for turn in range(4):
        t = s ^ turn
        lanes = pl.ds(offset(t, 384), 384)
        out_ref = outs[turn]
        out_ref[0:64, :] = wide_a[:, lanes]
        out_ref[64:128, :] = wide_b[0:64, lanes]
        block = jnp.concatenate([wide_b[64:65, 384 * i : 384 * i + 384].astype(F32) for i in range(4)], axis=0)
        block = jnp.concatenate([block, jnp.zeros((12, 384), F32)], axis=0)
        out_ref[128:144, :] = block.astype(BF)
        out_ref[144:192, 0:256] = wide_o[0:48, pl.ds(offset(t, 256), 256)]
        for i in range(2):
            out_ref[144 + 16 * i : 160 + 16 * i, 256:384] = wide_o[48:64, pl.ds(offset(2 * t + i, 128), 128)]
        out_ref[176:192, 256:384] = jnp.zeros((16, 128), BF)


def line_mlp_body(ids, k2_ref, r2_ref, k1_ref, r1_ref, *outs):
    s = ids[1]
    two, one = outs[4:]
    two[...] = halve(k2_ref[...], r2_ref[...])
    one[...] = halve(k1_ref[...], r1_ref[0:128, :])
    for turn in range(4):
        t = s ^ turn
        out_ref = outs[turn]
        out_ref[0:256, :] = two[:, pl.ds(offset(t, 256), 256)]
        for i in range(2):
            out_ref[256 + 128 * i : 384 + 128 * i, :] = one[:, pl.ds(offset(2 * t + i, 256), 256)]


def pack_out(target_ref, row, values):
    for i in range(2):
        lanes = slice(512 * i, 512 * i + 512)
        target_ref[row : row + 48, lanes] = values[0:48, lanes]
        target_ref[row + 16 * i : row + 16 * i + 16, 1024:1536] = values[48:64, lanes]
    target_ref[row + 32 : row + 48, 1024:1536] = jnp.zeros((16, 512), values.dtype)


def merge_body(ids, keep_ref, got_ref, stay_ref, send_ref):
    half = stay_ref.shape[0]
    stay_ref[...] = halve(keep_ref[0:half, :], got_ref[0:half, :])
    send_ref[...] = halve(keep_ref[half:, :], got_ref[half:, :])


def merge(ids, keep, got):
    shape = struct((keep.shape[0] // 2, keep.shape[1]), BF)
    return call(merge_body, [shape, shape], (ids, keep, got), micros=0.05)


def merge_one_body(ids, keep_ref, got_ref, ko_ref, ro_ref, stay_ref, send_ref, so_ref):
    stay_ref[...] = halve(keep_ref[0:128, :], got_ref[0:128, :])
    send_ref[0:128, :] = halve(keep_ref[128:256, :], got_ref[128:256, :])
    so_ref[...] = halve(ko_ref[0:128, :], ro_ref[0:128, :])
    for i in range(2):
        rows = slice(128 + 64 * i, 192 + 64 * i)
        send_ref[128:192, 1024 * i : 1024 * i + 1024] = halve(ko_ref[rows, :], ro_ref[rows, :])


def merge_qkv_body(ids, keep_ref, got_ref, ko_ref, ro_ref, stay_a, send_a, stay_b, send_b, stay_o):
    def total(start, size):
        return halve(keep_ref[start : start + size, :], got_ref[start : start + size, :])

    stay_a[...] = total(0, 128)
    send_a[...] = total(128, 128)
    stay_b[...] = total(256, 160)
    send_b[0:160, :] = total(416, 160)
    stay_o[...] = halve(ko_ref[0:64, :], ro_ref[128:192, 0:1024])
    pack_out(send_b, 160, halve(ko_ref[64:128, :], ro_ref[128:192, 1024:2048]))


def merge_last_body(ids, ka_ref, ra_ref, kb_ref, rb_ref, stay_a, send_a, stay_b, send_b):
    for keep_ref, got_ref, stay_ref, send_ref in ((ka_ref, ra_ref, stay_a, send_a), (kb_ref, rb_ref, stay_b, send_b)):
        half = stay_ref.shape[0]
        stay_ref[...] = halve(keep_ref[0:half, :], got_ref[0:half, :])
        send_ref[...] = halve(keep_ref[half : 2 * half, :], got_ref[half : 2 * half, :])


def join_mlp_body(ids, own_ref, pair_ref, far_ref, cross_ref, one_ref, two_ref):
    half = ids[1] % 2
    other = 1 - half

    def sums(at):
        same = own_ref[at, :].astype(F32) + far_ref[at, :].astype(F32)
        return same, pair_ref[at, :].astype(F32) + cross_ref[at, :].astype(F32)

    same, rest = sums(slice(0, 256))
    two_ref[pl.ds(offset(half, 256), 256), :] = same
    two_ref[pl.ds(offset(other, 256), 256), :] = rest
    for i in range(2):
        same, rest = sums(slice(256 + 128 * i, 384 + 128 * i))
        one_ref[:, pl.ds(offset(2 * i + half, 256), 256)] = same
        one_ref[:, pl.ds(offset(2 * i + other, 256), 256)] = rest


def join_body(ids, own_ref, pair_ref, far_ref, cross_ref, out_ref, wo_ref, sums_ref, wide_ref):
    s = ids[1]
    half = s % 2
    lower = half == 0
    low = lanes_low((128, 128))

    def sums(rows, lanes):
        same = own_ref[rows, lanes].astype(F32) + far_ref[rows, lanes].astype(F32)
        return same, pair_ref[rows, lanes].astype(F32) + cross_ref[rows, lanes].astype(F32)

    for j in range(3):
        same, other = sums(slice(0, 128), slice(128 * j, 128 * j + 128))
        first = jnp.where(lower, same, other)
        second = jnp.where(lower, other, same)
        out_ref[:, 256 * j : 256 * j + 128] = jnp.where(low, first, pltpu.roll(second, HD, 1))
        out_ref[:, 256 * j + 128 : 256 * j + 256] = jnp.where(low, pltpu.roll(first, HD, 1), second)
    places = [(slice(144, 192), slice(0, 256), 0, slice(0, 256))]
    places += [(slice(144 + 16 * i, 160 + 16 * i), slice(256, 384), 48, slice(128 * i, 128 * i + 128)) for i in range(2)]
    for rows, lanes, row, target in places:
        same, other = sums(rows, lanes)
        size = same.shape[0]
        wo_ref[pl.ds(pl.multiple_of(half * 64 + row, 16), size), target] = same
        wo_ref[pl.ds(pl.multiple_of((1 - half) * 64 + row, 16), size), target] = other
    same, other = sums(slice(128, 144), slice(0, 384))
    total = same + other
    for i in range(4):
        for n in range(3):
            spot = 3 * i + n
            block = total[i : i + 1, 128 * n : 128 * n + 128]
            if spot < 8:
                block = pltpu.roll(jnp.broadcast_to(block, (8, 128)), (128 - 32 * s) % 128, 1)[0:1]
                sums_ref[spot : spot + 1, :] = block
            else:
                wide_ref[spot - 8 : spot - 7, :] = block
    sums_ref[8:9, :] = wide_ref[pl.ds(s, 1), :]


def halve(keep, received):
    return (keep.astype(F32) + received.astype(F32)).astype(BF)


def paired_shards(
    tokens,
    segment_ids,
    ln1_gain,
    ln1_bias,
    w_qkv,
    q_bias,
    v_bias,
    w_out,
    out_bias,
    ln2_gain,
    ln2_bias,
    w_fc1,
    fc1_bias,
    w_fc2,
    fc2_bias,
    cotangent,
):
    own_rows, width = tokens.shape
    cut = own_rows // 2
    tail = 32
    rows = own_rows + cut + tail
    f = lax.axis_index("fsdp")
    s = lax.axis_index("seq")
    ids = jnp.where(lax.iota(jnp.int32, 2) == 0, f, s).astype(jnp.int32)

    def exchange(own, extra, name):
        extra = zshift(extra, ((1, 2),), name + "_extra")
        return zshift(own, PAIR, name), extra, zshift(extra, ((2, 3),), name + "_relay")

    hbm = partial(pltpu.with_memory_space_constraint, memory_space=pltpu.HBM)
    vectors = [ln1_gain, ln1_bias, out_bias, ln2_gain, ln2_bias, fc2_bias, q_bias, v_bias, fc1_bias]
    a, both, tokens_extra = call(
        pick_qkv,
        [struct((144, 1536), BF), struct((192, 1536), BF), struct((own_rows - cut, width), BF)],
        (ids, *[hbm(v) for v in (w_qkv, tokens, w_out, *vectors)]),
        scratch=[
            pltpu.VMEM(w_qkv.shape, BF),
            pltpu.VMEM((64, width), BF),
            *[pltpu.VMEM(v.shape, BF) for v in vectors],
            pltpu.SemaphoreType.DMA((12,)),
        ],
        space=pltpu.HBM, micros=2.2)
    moved_tokens = exchange(tokens, tokens_extra, "tokens")
    one, two = call(
        pick_mlp,
        [struct((320, 1024), BF), struct((320, 1024), BF)],
        (ids, hbm(after(w_fc1, a)), hbm(w_fc2), hbm(w_out)),
        scratch=[pltpu.SemaphoreType.DMA((11,))],
        space=pltpu.HBM, micros=1.9)
    pieces = [a, fshift(a, 2, "qkv_x"), fshift(a, 4, "qkv_y"), fshift(both, 6, "qkv_xy")]
    pieces.append(fshift(stack(ids, after(a, *moved_tokens, one), *pieces[1:], sizes=(144,) * 4), 1, "qkv_core"))

    one_x = fshift(after(one, moved_tokens[0]), 2, "one_x")
    two_y = fshift(after(two, moved_tokens[0]), 4, "two_y")

    one_two, two_two, outs_even = call(
        stack_mlp_body,
        [struct((512, 1024), BF), struct((512, 1024), BF), struct((256, 1024), BF)],
        (ids, one, one_x, two, two_y, pieces[3]), micros=60.0)
    outs_odd = fshift(outs_even, 1, "out_core")
    x, qkv, h1_e, h1_o, par = call(
        qkv_body,
        [
            struct((rows, width), BF),
            struct((rows, 1536), BF),
            struct((rows, 512), BF),
            struct((rows, 512), BF),
            struct((8, 1536), F32),
        ],
        (ids, after(tokens, one_two), *moved_tokens, *pieces),
        scratch=[pltpu.VMEM((rows, 1024), BF), pltpu.VMEM((1, 1536), F32)], micros=6.8)
    valid = segment_ids >= 0
    gm_own = jnp.where(valid[:, None], after(cotangent, *moved_tokens), jnp.zeros_like(cotangent))
    valid_lanes = jnp.broadcast_to(valid[:, None].astype(F32), (own_rows, 128))
    moved_gm = exchange(gm_own, gm_own[cut:], "cotangent")

    def columns(base, size=rows):
        return pl.BlockSpec((size, 128), lambda j: (0, base + j))

    heads_o = pl.pallas_call(
        partial(attend_body, own_rows, rows // 2),
        grid=(4,),
        out_shape=struct((rows, 512), BF),
        in_specs=[SMEM_SPEC, columns(0), columns(4), columns(8)],
        out_specs=columns(0),
        compiler_params=pltpu.CompilerParams(vmem_limit_bytes=20 * 2**20),
        cost_estimate=cost(7.1),
    )(ids, qkv, qkv, qkv)
    sizes = (320, rows - 320)

    mine_0, mine_1, w_out_full = call(
        mixed_body,
        [struct((sizes[0], width), BF), struct((sizes[1], width), BF), struct((512, width), BF)],
        (ids, heads_o, outs_even, outs_odd), micros=1.4)
    theirs_0 = zshift(mine_0, PAIR, "mixed")
    theirs_1 = zshift(after(mine_1, mine_0), PAIR, "mixed")
    gm = call(place_grad_body, struct((rows, width), BF), (ids, after(gm_own, mine_1), *moved_gm), micros=25.0)
    one_even = stack(ids, after(one_two, gm), fshift(one_two, 4, "one_y"))
    two_even = stack(ids, after(two_two, gm), fshift(two_two, 2, "two_x"))
    weights = (one_even, fshift(one_even, 1, "one_core"), two_even, fshift(two_even, 1, "two_core"))

    def middle(chunk, mine, theirs, micros):
        part = sizes[chunk]
        return call(
            partial(middle_body, chunk * sizes[0]),
            [struct((part, 1024), F32), struct((part, 512), BF), struct((part, 512), BF)],
            (ids, par, x, mine, theirs),
            scratch=[pltpu.VMEM((part, 1024), BF)],
            micros=micros,
        )

    def mlp(chunk, h2_e, h2_o):
        part = sizes[chunk]
        return call(
            partial(mlp_body, chunk * sizes[0]),
            [
                struct((part, 1024), BF),
                struct((part, 1024), BF),
                struct((part, 2048), BF),
                struct((part, 1024), BF),
                struct((8, 256), F32),
            ],
            (ids, par, h2_e, h2_o, gm, *weights),
            scratch=[pltpu.VMEM((part, 256), F32), pltpu.VMEM((part, 256), F32)],
            micros=9.5,
        )

    mid_0, h2_e0, h2_o0 = middle(0, mine_0, theirs_0, 60.0)
    act_e0, act_o0, gu_0, gh2_0, fc1_sums_0 = mlp(0, h2_e0, h2_o0)
    gh2_theirs_0 = zshift(gh2_0, PAIR, "mlp_grad")
    mid_1, h2_e1, h2_o1 = middle(1, after(mine_1, gh2_0), theirs_1, 2.0)
    act_e1, act_o1, gu_1, gh2_1, fc1_sums_1 = mlp(1, h2_e1, h2_o1)
    gh2_theirs_1 = zshift(gh2_1, PAIR, "mlp_grad")

    def row_grad(l0, l1, r0, r1, step):
        return call(
            partial(rows_grad_body, step),
            struct((l0.shape[1], r0.shape[1]), BF),
            (ids, l0, l1, r0, r1), micros=2.4)

    send_two = row_grad(after(act_o0, gh2_1), act_o1, gm, gm, 256)
    got_two = fshift(send_two, 1, "two_grad_core")
    keep_two = row_grad(after(act_e0, send_two), act_e1, gm, gm, 256)
    send_one = row_grad(after(h2_o0, keep_two), h2_o1, gu_0, gu_1, 512)
    got_one = fshift(send_one, 1, "one_grad_core")

    def middle_back(chunk, mid, mine, theirs, micros):
        part = sizes[chunk]
        return call(
            partial(middle_back_body, chunk * sizes[0]),
            [struct((part, 1024), BF), struct((part, 512), BF), struct((8, 512), F32)],
            (ids, par, mid, gm, mine, theirs, w_out_full),
            micros=micros,
        )

    gb_0, go_0, mid_sums_0 = middle_back(0, after(mid_0, send_one), gh2_0, gh2_theirs_0, 60.0)
    stay_two, send_two = merge(ids, after(keep_two, gb_0), got_two)
    got_two = fshift(send_two, 2, "two_grad_x")
    keep_one = row_grad(after(h2_e0, stay_two), h2_e1, gu_0, gu_1, 512)
    stay_one, send_one = merge(ids, keep_one, got_one)
    got_one = fshift(send_one, 4, "one_grad_y")
    y_keep, y_send = call(
        out_body,
        [struct((own_rows, width), BF)] * 2,
        (ids, after(act_e0, stay_one), act_o0, act_e1, act_o1, two_even, weights[3]),
        scratch=[pltpu.VMEM((rows, width), BF)],
        micros=0.18,
    )
    y_theirs = zshift(y_send, PAIR, "output")
    gb_1, go_1, mid_sums_1 = middle_back(1, after(mid_1, y_keep), gh2_1, gh2_theirs_1, 4.0)
    keep_o, send_o = call(
        out_grad_body,
        [struct((256, 1024), BF)] * 2,
        (ids, heads_o, gb_0, gb_1),
        scratch=[pltpu.VMEM((512, 1024), BF)],
        micros=0.085,
    )
    got_o = fshift(send_o, 1, "out_grad_core")
    gq, gk, gv = pl.pallas_call(
        partial(attend_back_body, own_rows, rows),
        grid=(4,),
        out_shape=[struct((rows, 512), BF)] * 3,
        in_specs=[SMEM_SPEC, columns(0), columns(4), columns(8), columns(0, sizes[0]), columns(0, sizes[1])],
        out_specs=[columns(0)] * 3,
        compiler_params=pltpu.CompilerParams(vmem_limit_bytes=24 * 2**20),
        cost_estimate=cost(0.7),
    )(ids, qkv, qkv, qkv, after(go_0, keep_o), go_1)
    result, result_extra = call(
        result_body,
        [struct((own_rows, width), BF), struct((cut, width), BF)],
        (ids, par, mid_0, mid_1, after(y_keep, gq), y_theirs),
        micros=0.055,
    )
    result_extra = zshift(result_extra, ((3, 1),), "output_rows")
    stay_two, send_two = merge(ids, after(stay_two, result), got_two)
    got_two = fshift(send_two, 4, "two_grad_y")
    stay_one, send_one, stay_o = call(
        merge_one_body,
        [struct((128, 2048), BF), struct((192, 2048), BF), struct((128, 1024), BF)],
        (ids, after(stay_one, stay_two), got_one, keep_o, got_o),
        micros=0.05,
    )
    got_one = fshift(send_one, 2, "one_grad_x")
    gh1_keep, gh1_send, one_sums = call(
        input_grad_body,
        [struct((own_rows, 1024), BF), struct((own_rows, 1024), BF), struct((8, 256), F32)],
        (ids, x, par, gq, gk, after(gv, stay_one), *pieces),
        scratch=[pltpu.VMEM((rows, 1024), F32), pltpu.VMEM((rows, 1024), BF)],
        micros=0.35,
    )
    gh1_theirs = zshift(gh1_send, PAIR, "input_grad")
    keep_q, send_q = call(
        qkv_grad_body,
        [struct((576, 1536), BF), struct((576, 1536), BF)],
        (ids, h1_e, h1_o, gq, gk, after(gv, gh1_send), one_sums, mid_sums_0, mid_sums_1, fc1_sums_0, fc1_sums_1),
        scratch=[pltpu.VMEM((8, 1536), F32)],
        micros=0.165,
    )
    got_q = fshift(send_q, 1, "qkv_grad_core")
    layer_output = call(
        owner_rows_body,
        struct((own_rows, width), BF),
        (ids, valid_lanes, after(result, keep_q), result_extra),
        micros=0.075,
    )
    stay_a, send_a, stay_b, send_b, last_o = call(
        merge_qkv_body,
        [struct((n, w), BF) for n, w in ((128, 1536), (128, 1536), (160, 1536), (208, 1536), (64, 1024))],
        (ids, after(keep_q, layer_output), got_q, stay_o, got_one),
        micros=0.05,
    )
    got_a = fshift(send_a, 2, "qkv_grad_x")
    got_b = fshift(send_b, 4, "qkv_grad_y")
    mlp_own, *mlp_sends = call(
        line_mlp_body,
        [struct((512, 256), BF)] * 4,
        (ids, after(stay_two, stay_a), got_two, stay_one, got_one),
        scratch=[pltpu.VMEM((256, 1024), BF), pltpu.VMEM((128, 2048), BF)],
        micros=0.06,
    )
    mlp_gots = [zshift(t, p, "mlp_grad_z") for t, p in zip(mlp_sends, (PAIR, FAR, CROSS))]
    back, back_extra = call(
        input_back_body,
        [struct((own_rows, width), F32), struct((cut, width), BF)],
        (ids, par, x, gb_0, gb_1, after(gh1_keep, mlp_own), gh1_theirs),
        scratch=[pltpu.VMEM((rows, width), BF)],
        micros=0.2,
    )
    back_extra = zshift(back_extra, ((3, 1),), "input_grad_rows")
    last_a, send_a, last_b, send_b = call(
        merge_last_body,
        [struct((n, 1536), BF) for n in (64, 64, 80, 80)],
        (ids, after(stay_a, back), got_a, stay_b, got_b),
        micros=0.05,
    )
    out_b = got_b
    got_a = fshift(send_a, 4, "qkv_grad_y")
    got_b = fshift(send_b, 2, "qkv_grad_x")
    w_fc1_grad, w_fc2_grad = call(
        join_mlp_body,
        [struct((128, 1024), F32), struct((512, 256), F32)],
        (ids, after(mlp_own, last_a), *mlp_gots),
        micros=0.085,
    )
    own, to_pair, to_far, to_cross = call(
        line_body,
        [struct((192, 384), BF)] * 4,
        (ids, after(last_a, w_fc1_grad), got_a, last_b, got_b, last_o, out_b),
        scratch=[pltpu.VMEM((64, 1536), BF), pltpu.VMEM((80, 1536), BF), pltpu.VMEM((64, 1024), BF)],
        micros=0.04,
    )
    got_pair = zshift(to_pair, PAIR, "qkv_grad_z")
    got_far = zshift(to_far, FAR, "qkv_grad_z")
    got_cross = zshift(to_cross, CROSS, "qkv_grad_z")
    tokens_grad = call(
        owner_rows_body,
        struct((own_rows, width), F32),
        (ids, valid_lanes, after(back, own), back_extra),
        micros=0.075,
    )
    w_qkv_grad, w_out_grad, sums = call(
        join_body,
        [struct((128, 768), F32), struct((128, 256), F32), struct((9, 128), F32)],
        (ids, own, got_pair, got_far, got_cross),
        scratch=[pltpu.VMEM((4, 128), F32)],
        micros=0.07,
    )

    def vector(spot):
        return sums[spot, 0:32]

    return (
        layer_output,
        tokens_grad,
        vector(0),
        vector(1),
        w_qkv_grad,
        vector(6),
        vector(7),
        w_out_grad,
        vector(2),
        vector(3),
        vector(4),
        w_fc1_grad,
        sums[8],
        w_fc2_grad,
        vector(5),
    )


def shards(*operands):
    tokens = operands[0]
    fits = (
        lax.axis_size("fsdp") == 8
        and lax.axis_size("seq") == 4
        and tokens.shape == (384, 1024)
        and operands[11].shape == (128, 4096)
    )
    return paired_shards(*operands) if fits else general_shards(*operands)


def solution(mesh):
    return jax.shard_map(
        shards,
        mesh=mesh,
        in_specs=(
            P(("fsdp", "seq"), None),
            P(("fsdp", "seq")),
            P("fsdp"),
            P("fsdp"),
            P("fsdp", None),
            P("fsdp"),
            P("fsdp"),
            P("fsdp", None),
            P("fsdp"),
            P("fsdp"),
            P("fsdp"),
            P("fsdp", None),
            P("fsdp"),
            P("fsdp", None),
            P("fsdp"),
            P(("fsdp", "seq"), None),
        ),
        out_specs=(
            P(("fsdp", "seq"), None),
            P(("fsdp", "seq"), None),
            P(("fsdp", "seq")),
            P(("fsdp", "seq")),
            P("fsdp", "seq"),
            P(("fsdp", "seq")),
            P(("fsdp", "seq")),
            P("fsdp", "seq"),
            P(("fsdp", "seq")),
            P(("fsdp", "seq")),
            P(("fsdp", "seq")),
            P("fsdp", "seq"),
            P(("fsdp", "seq")),
            P("fsdp", "seq"),
            P(("fsdp", "seq")),
        ),
        check_vma=False,
    )
```

```python
from functools import partial

import jax
import jax.numpy as jnp
from jax import lax
from jax.experimental import pallas as pl
from jax.experimental.pallas import tpu as pltpu
from jax.sharding import PartitionSpec as P

HD = 64
LEN = 577


norm_eps = 1e-06
masked_score = -1000000000.0


def normalize(values, gain, shift):
    row_mean = jnp.mean(values, axis=-1, keepdims=True)
    centered = values - row_mean
    variance = jnp.mean(centered * centered, axis=-1, keepdims=True)
    return centered * lax.rsqrt(variance + norm_eps) * gain + shift


def contract_rows(left, right):
    return lax.dot_general(
        left, right, (((0,), (0,)), ((), ())), preferred_element_type=jnp.float32
    )


def times_transposed(left, right):
    return lax.dot_general(
        left, right, (((1,), (1,)), ((), ())), preferred_element_type=jnp.float32
    )


def column_sum(values):
    return jnp.sum(values, axis=0, dtype=jnp.float32)


def shards_per_block(row_count, seq_count):
    for factor in range(1, seq_count + 1):
        if seq_count % factor == 0 and (row_count * factor >= 512 or factor == seq_count):
            return factor
    return seq_count


def add_window(total, delta, start):
    current = lax.dynamic_slice_in_dim(total, start, delta.shape[0], 0)
    return lax.dynamic_update_slice_in_dim(total, current + delta, start, 0)


def general_shards(
    tokens,
    segment_ids,
    ln1_gain,
    ln1_bias,
    w_qkv,
    q_bias,
    v_bias,
    w_out,
    out_bias,
    ln2_gain,
    ln2_bias,
    w_fc1,
    fc1_bias,
    w_fc2,
    fc2_bias,
    cotangent,
):
    row_count = tokens.shape[0]
    feature_width = tokens.shape[1]
    seq_count = lax.axis_size("seq")
    span_rows = row_count * seq_count
    local_heads = feature_width // seq_count // HD
    block_rows = row_count * shards_per_block(row_count, seq_count)
    block_count = span_rows // block_rows
    margin = LEN - 1
    window = block_rows + 2 * margin
    offsets = jnp.arange(block_count, dtype=jnp.int32) * block_rows
    scale = HD ** (-0.5)
    as_float = jnp.float32

    def weight_grad(left, right):
        return contract_rows(left, right)

    attn_set = (
        lax.all_gather(ln1_gain, "fsdp", axis=0, tiled=True),
        lax.all_gather(ln1_bias, "fsdp", axis=0, tiled=True),
        lax.all_gather(w_qkv, "fsdp", axis=0, tiled=True),
        lax.all_gather(q_bias, "fsdp", axis=0, tiled=True),
        lax.all_gather(v_bias, "fsdp", axis=0, tiled=True),
        lax.all_gather(w_out, "fsdp", axis=0, tiled=True),
        lax.all_gather(out_bias, "fsdp", axis=0, tiled=True),
    )
    span_labels = lax.all_gather(segment_ids, "seq", axis=0, tiled=True)
    inputs = tokens.astype(as_float)
    gain_one = attn_set[0].astype(as_float)
    shift_one = attn_set[1].astype(as_float)
    first_norm = normalize(inputs, gain_one, shift_one).astype(jnp.bfloat16)
    projected = jnp.dot(first_norm, attn_set[2], preferred_element_type=as_float)
    bias_all = jnp.concatenate(
        [
            attn_set[3].astype(as_float),
            jnp.zeros((feature_width,), as_float),
            attn_set[4].astype(as_float),
        ]
    )
    packed = (projected + bias_all).astype(jnp.bfloat16).reshape(row_count, 3, feature_width)
    head_rows = lax.all_to_all(packed, "seq", split_axis=2, concat_axis=0, tiled=True)
    query_heads = head_rows[:, 0, :].reshape(span_rows, local_heads, HD)
    key_heads = head_rows[:, 1, :].reshape(span_rows, local_heads, HD)
    value_heads = head_rows[:, 2, :].reshape(span_rows, local_heads, HD)
    key_padded = jnp.pad(key_heads, ((margin, margin), (0, 0), (0, 0)))
    value_padded = jnp.pad(value_heads, ((margin, margin), (0, 0), (0, 0)))
    label_padded = jnp.pad(span_labels, (margin, margin), constant_values=-2)

    def block_scores(offset):
        query_block = lax.dynamic_slice_in_dim(query_heads, offset, block_rows, 0)
        label_block = lax.dynamic_slice_in_dim(span_labels, offset, block_rows, 0)
        key_window = lax.dynamic_slice_in_dim(key_padded, offset, window, 0)
        value_window = lax.dynamic_slice_in_dim(value_padded, offset, window, 0)
        label_window = lax.dynamic_slice_in_dim(label_padded, offset, window, 0)
        scaled = (
            jnp.einsum("qhd,khd->hqk", query_block, key_window, preferred_element_type=as_float)
            * scale
        )
        same_image = label_block[:, None] == label_window[None, :]
        return (
            query_block,
            key_window,
            value_window,
            jnp.where(same_image[None], scaled, masked_score),
        )

    def block_forward(offset):
        unused_query, unused_key, value_window, scores = block_scores(offset)
        row_peak = jnp.max(scores, axis=-1, keepdims=True)
        lifted = jnp.exp(scores - row_peak)
        row_total = jnp.sum(lifted, axis=-1, keepdims=True)
        attn_probs = (lifted / row_total).astype(jnp.bfloat16)
        block_out = jnp.einsum(
            "hqk,khd->qhd", attn_probs, value_window, preferred_element_type=as_float
        ).astype(jnp.bfloat16)
        return (block_out, (row_peak + jnp.log(row_total))[..., 0])

    head_out, log_totals = lax.map(block_forward, offsets)
    head_flat = head_out.reshape(span_rows, local_heads * HD)
    attended = lax.all_to_all(head_flat, "seq", split_axis=0, concat_axis=1, tiled=True)
    mixed = jnp.dot(attended, attn_set[5], preferred_element_type=as_float) + attn_set[6].astype(
        as_float
    )
    middle = inputs + mixed
    mlp_set = (
        lax.all_gather(ln2_gain, "fsdp", axis=0, tiled=True),
        lax.all_gather(ln2_bias, "fsdp", axis=0, tiled=True),
        lax.all_gather(w_fc1, "fsdp", axis=0, tiled=True),
        lax.all_gather(fc1_bias, "fsdp", axis=0, tiled=True),
        lax.all_gather(w_fc2, "fsdp", axis=0, tiled=True),
        lax.all_gather(fc2_bias, "fsdp", axis=0, tiled=True),
    )
    gain_two = mlp_set[0].astype(as_float)
    shift_two = mlp_set[1].astype(as_float)
    second_norm = normalize(middle, gain_two, shift_two).astype(jnp.bfloat16)
    hidden = jnp.dot(second_norm, mlp_set[2], preferred_element_type=as_float) + mlp_set[3].astype(
        as_float
    )
    activated = jax.nn.gelu(hidden, approximate=False).astype(jnp.bfloat16)
    branch = jnp.dot(activated, mlp_set[4], preferred_element_type=as_float) + mlp_set[5].astype(
        as_float
    )
    valid = (segment_ids >= 0).astype(as_float)[:, None]
    layer_output = (valid * (middle + branch)).astype(jnp.bfloat16)
    grad_out = valid * cotangent.astype(as_float)
    grad_branch = grad_out.astype(jnp.bfloat16)
    fc2_bias_part = column_sum(grad_branch)
    w_fc2_part = weight_grad(activated, grad_branch)
    grad_act = times_transposed(grad_branch, mlp_set[4])
    unused_hidden, gelu_back = jax.vjp(partial(jax.nn.gelu, approximate=False), hidden)
    grad_hidden = gelu_back(grad_act)[0].astype(jnp.bfloat16)
    fc1_bias_part = column_sum(grad_hidden)
    w_fc1_part = weight_grad(second_norm, grad_hidden)
    grad_norm_two = times_transposed(grad_hidden, mlp_set[2])
    unused_two, norm_two_back = jax.vjp(
        normalize, middle, mlp_set[0].astype(as_float), mlp_set[1].astype(as_float)
    )
    grad_mid_norm, ln2_gain_part, ln2_bias_part = norm_two_back(grad_norm_two)
    grad_middle = grad_out + grad_mid_norm
    grad_mixed = grad_middle.astype(jnp.bfloat16)
    out_bias_part = column_sum(grad_mixed)
    w_out_part = weight_grad(attended, grad_mixed)
    grad_attended = times_transposed(grad_mixed, attn_set[5]).astype(jnp.bfloat16)
    grad_heads = lax.all_to_all(
        grad_attended, "seq", split_axis=1, concat_axis=0, tiled=True
    ).reshape(span_rows, local_heads, HD)

    def block_backward(running, inputs_block):
        key_total, value_total = running
        offset, log_block = inputs_block
        query_block, key_window, value_window, scores = block_scores(offset)
        grad_block = lax.dynamic_slice_in_dim(grad_heads, offset, block_rows, 0)
        probs_full = jnp.exp(scores - log_block[..., None])
        attn_probs = probs_full.astype(jnp.bfloat16)
        value_delta = jnp.einsum(
            "hqk,qhd->khd", attn_probs, grad_block, preferred_element_type=as_float
        )
        grad_probs = jnp.einsum(
            "qhd,khd->hqk", grad_block, value_window, preferred_element_type=as_float
        )
        row_inner = jnp.sum(grad_probs * probs_full, axis=-1, keepdims=True)
        grad_scores = (probs_full * (grad_probs - row_inner)).astype(jnp.bfloat16)
        grad_query = (
            jnp.einsum("hqk,khd->qhd", grad_scores, key_window, preferred_element_type=as_float)
            * scale
        )
        key_delta = (
            jnp.einsum("hqk,qhd->khd", grad_scores, query_block, preferred_element_type=as_float)
            * scale
        )
        return (
            (
                add_window(key_total, key_delta, offset),
                add_window(value_total, value_delta, offset),
            ),
            grad_query,
        )

    zero_heads = jnp.zeros((span_rows + 2 * margin, local_heads, HD), as_float)
    (key_padded_grad, value_padded_grad), query_grad = lax.scan(
        block_backward, (zero_heads, zero_heads), (offsets, log_totals)
    )
    key_grad = key_padded_grad[margin : margin + span_rows]
    value_grad = value_padded_grad[margin : margin + span_rows]
    head_grads = jnp.concatenate(
        [
            query_grad.reshape(span_rows, 1, local_heads * HD),
            key_grad.reshape(span_rows, 1, local_heads * HD),
            value_grad.reshape(span_rows, 1, local_heads * HD),
        ],
        axis=1,
    ).astype(jnp.bfloat16)
    token_grads = lax.all_to_all(
        head_grads, "seq", split_axis=0, concat_axis=2, tiled=True
    ).reshape(row_count, 3 * feature_width)
    q_bias_part = column_sum(token_grads[:, :feature_width])
    v_bias_part = column_sum(token_grads[:, 2 * feature_width :])
    w_qkv_part = weight_grad(first_norm, token_grads)
    grad_norm_one = times_transposed(token_grads, attn_set[2])
    unused_one, norm_one_back = jax.vjp(
        normalize, inputs, attn_set[0].astype(as_float), attn_set[1].astype(as_float)
    )
    grad_input_norm, ln1_gain_part, ln1_bias_part = norm_one_back(grad_norm_one)
    tokens_grad = grad_middle + grad_input_norm
    partial_sums = (
        lax.psum_scatter(
            ln1_gain_part.astype(jnp.bfloat16), "fsdp", scatter_dimension=0, tiled=True
        ).astype(jnp.float32),
        lax.psum_scatter(
            ln1_bias_part.astype(jnp.bfloat16), "fsdp", scatter_dimension=0, tiled=True
        ).astype(jnp.float32),
        lax.psum_scatter(
            w_qkv_part.astype(jnp.bfloat16), "fsdp", scatter_dimension=0, tiled=True
        ).astype(jnp.float32),
        lax.psum_scatter(
            q_bias_part.astype(jnp.bfloat16), "fsdp", scatter_dimension=0, tiled=True
        ).astype(jnp.float32),
        lax.psum_scatter(
            v_bias_part.astype(jnp.bfloat16), "fsdp", scatter_dimension=0, tiled=True
        ).astype(jnp.float32),
        lax.psum_scatter(
            w_out_part.astype(jnp.bfloat16), "fsdp", scatter_dimension=0, tiled=True
        ).astype(jnp.float32),
        lax.psum_scatter(
            out_bias_part.astype(jnp.bfloat16), "fsdp", scatter_dimension=0, tiled=True
        ).astype(jnp.float32),
        lax.psum_scatter(
            ln2_gain_part.astype(jnp.bfloat16), "fsdp", scatter_dimension=0, tiled=True
        ).astype(jnp.float32),
        lax.psum_scatter(
            ln2_bias_part.astype(jnp.bfloat16), "fsdp", scatter_dimension=0, tiled=True
        ).astype(jnp.float32),
        lax.psum_scatter(
            w_fc1_part.astype(jnp.bfloat16), "fsdp", scatter_dimension=0, tiled=True
        ).astype(jnp.float32),
        lax.psum_scatter(
            fc1_bias_part.astype(jnp.bfloat16), "fsdp", scatter_dimension=0, tiled=True
        ).astype(jnp.float32),
        lax.psum_scatter(
            w_fc2_part.astype(jnp.bfloat16), "fsdp", scatter_dimension=0, tiled=True
        ).astype(jnp.float32),
        lax.psum_scatter(
            fc2_bias_part.astype(jnp.bfloat16), "fsdp", scatter_dimension=0, tiled=True
        ).astype(jnp.float32),
    )
    summed = (
        lax.psum_scatter(
            partial_sums[0].astype(jnp.bfloat16), "seq", scatter_dimension=0, tiled=True
        ).astype(jnp.float32),
        lax.psum_scatter(
            partial_sums[1].astype(jnp.bfloat16), "seq", scatter_dimension=0, tiled=True
        ).astype(jnp.float32),
        lax.psum_scatter(
            partial_sums[2].astype(jnp.bfloat16), "seq", scatter_dimension=1, tiled=True
        ).astype(jnp.float32),
        lax.psum_scatter(
            partial_sums[3].astype(jnp.bfloat16), "seq", scatter_dimension=0, tiled=True
        ).astype(jnp.float32),
        lax.psum_scatter(
            partial_sums[4].astype(jnp.bfloat16), "seq", scatter_dimension=0, tiled=True
        ).astype(jnp.float32),
        lax.psum_scatter(
            partial_sums[5].astype(jnp.bfloat16), "seq", scatter_dimension=1, tiled=True
        ).astype(jnp.float32),
        lax.psum_scatter(
            partial_sums[6].astype(jnp.bfloat16), "seq", scatter_dimension=0, tiled=True
        ).astype(jnp.float32),
        lax.psum_scatter(
            partial_sums[7].astype(jnp.bfloat16), "seq", scatter_dimension=0, tiled=True
        ).astype(jnp.float32),
        lax.psum_scatter(
            partial_sums[8].astype(jnp.bfloat16), "seq", scatter_dimension=0, tiled=True
        ).astype(jnp.float32),
        lax.psum_scatter(
            partial_sums[9].astype(jnp.bfloat16), "seq", scatter_dimension=1, tiled=True
        ).astype(jnp.float32),
        lax.psum_scatter(
            partial_sums[10].astype(jnp.bfloat16), "seq", scatter_dimension=0, tiled=True
        ).astype(jnp.float32),
        lax.psum_scatter(
            partial_sums[11].astype(jnp.bfloat16), "seq", scatter_dimension=1, tiled=True
        ).astype(jnp.float32),
        lax.psum_scatter(
            partial_sums[12].astype(jnp.bfloat16), "seq", scatter_dimension=0, tiled=True
        ).astype(jnp.float32),
    )
    return (
        layer_output,
        tokens_grad,
        summed[0],
        summed[1],
        summed[2],
        summed[3],
        summed[4],
        summed[5],
        summed[6],
        summed[7],
        summed[8],
        summed[9],
        summed[10],
        summed[11],
        summed[12],
    )


LX = (0, 4, 2, 6, 1, 5, 3, 7)
LY = (0, 2, 4, 6, 1, 3, 5, 7)
PAIR = ((0, 1), (1, 0), (2, 3), (3, 2))
FAR = ((0, 2), (2, 0), (1, 3), (3, 1))
CROSS = ((0, 3), (3, 0), (1, 2), (2, 1))
BF = jnp.bfloat16
F32 = jnp.float32
RATE = 1.6e9
SMEM_SPEC = pl.BlockSpec(memory_space=pltpu.SMEM)
VMEM_SPEC = pl.BlockSpec(memory_space=pltpu.VMEM)
HALF_ROOT = 0.7071067811865476
DENSITY = 0.3989422804014327


def fshift(values, bit, name="move"):
    with jax.named_scope(name):
        return lax.ppermute(values, "fsdp", [(i, i ^ bit) for i in range(8)])


def zshift(values, pairs, name="move"):
    with jax.named_scope(name):
        return lax.ppermute(values, "seq", pairs)


def after(values, *earlier):
    return lax.optimization_barrier((values, *earlier))[0]


def cost(micros):
    return pl.CostEstimate(flops=int(micros * RATE) + 1, bytes_accessed=1, transcendentals=0)


def call(body, outs, args, scratch=(), micros=1.0, limit=12, space=pltpu.VMEM):
    single = not isinstance(outs, (list, tuple))
    shapes = [outs] if single else list(outs)
    result = pl.pallas_call(
        body,
        out_shape=shapes,
        in_specs=[SMEM_SPEC] + [pl.BlockSpec(memory_space=space)] * (len(args) - 1),
        out_specs=[VMEM_SPEC] * len(shapes),
        scratch_shapes=list(scratch),
        compiler_params=pltpu.CompilerParams(vmem_limit_bytes=limit * 2**20),
        cost_estimate=cost(micros),
    )(*args)
    return result[0] if single else result


def struct(shape, dtype):
    return jax.ShapeDtypeStruct(shape, dtype)


def lanes_low(shape):
    return lax.broadcasted_iota(jnp.int32, shape, 1) < HD


def dot_nn(a, b):
    return lax.dot_general(a, b, (((1,), (0,)), ((), ())), preferred_element_type=F32)


def dot_nt(a, b):
    return lax.dot_general(a, b, (((1,), (1,)), ((), ())), preferred_element_type=F32)


def dot_tn(a, b):
    return lax.dot_general(a, b, (((0,), (0,)), ((), ())), preferred_element_type=F32)


def offset(index, size):
    return pl.multiple_of(index * size, size)


def natural(ref, start):
    return jnp.concatenate([ref[i : i + 1, start : start + 128] for i in range(8)], axis=1)


def pick_qkv(ids, w_hbm, tokens_hbm, wo_hbm, *refs):
    count = (len(refs) - 6) // 2
    rows_hbm, rows, sems = refs[:count], refs[count + 5 : -1], refs[-1]
    out_ref, both_ref, extra_ref, w_ref, wo_ref = refs[count : count + 5]
    half = ids[1] % 2
    cut = tokens_hbm.shape[0] // 2
    copies = [(w_hbm, w_ref), (tokens_hbm.at[pl.ds(cut, cut)], extra_ref)]
    copies += [(wo_hbm.at[pl.ds(offset(half, 64), 64)], wo_ref), *zip(rows_hbm, rows)]
    copies = [pltpu.make_async_copy(source, target, sems.at[i]) for i, (source, target) in enumerate(copies)]
    for copy in copies:
        copy.start()
    for copy in copies:
        copy.wait()
    low = lanes_low((128, 128))
    for j in range(w_ref.shape[1] // 256):
        first = w_ref[:, 256 * j : 256 * j + 128].astype(F32)
        second = w_ref[:, 256 * j + 128 : 256 * j + 256].astype(F32)
        even = jnp.where(low, first, pltpu.roll(second, HD, 1))
        odd = jnp.where(low, pltpu.roll(first, HD, 1), second)
        out_ref[0:128, 128 * j : 128 * j + 128] = jnp.where(half == 0, even, odd).astype(BF)
    start = 0
    for row_ref in rows:
        size = row_ref.shape[0]
        row = row_ref[...].astype(F32)
        out_ref[128:144, start : start + size] = jnp.broadcast_to(row.reshape(1, size), (16, size)).astype(BF)
        start += size
    both_ref[0:144, :] = out_ref[...]
    pack_out(both_ref, 144, wo_ref[...])


def pick_mlp(ids, w1_hbm, w2_hbm, wo_hbm, one_ref, two_ref, sems):
    half = ids[1] % 2
    out_hbm = wo_hbm.at[pl.ds(offset(half, 64), 64)]
    copies = [
        (w2_hbm.at[pl.ds(offset(half, 256), 256)], two_ref.at[pl.ds(0, 256)]),
        (out_hbm, one_ref.at[pl.ds(256, 64)]),
        (out_hbm, two_ref.at[pl.ds(256, 64)]),
    ]
    for b in range(8):
        rows, lanes = pl.ds(128 * (b // 4), 128), pl.ds(256 * (b % 4), 256)
        copies.append((w1_hbm.at[:, pl.ds(offset(2 * b + half, 256), 256)], one_ref.at[rows, lanes]))
    copies = [pltpu.make_async_copy(source, target, sems.at[i]) for i, (source, target) in enumerate(copies)]
    for copy in copies:
        copy.start()
    for copy in copies:
        copy.wait()


def stack_mlp_body(ids, one_ref, one_x_ref, two_ref, two_y_ref, both_ref, one_out, two_out, outs):
    one_out[0:256, :] = one_ref[0:256, :]
    one_out[256:512, :] = one_x_ref[0:256, :]
    two_out[0:256, :] = two_ref[0:256, :]
    two_out[256:512, :] = two_y_ref[0:256, :]
    outs[0:64, :] = one_ref[256:320, :]
    outs[64:128, :] = one_x_ref[256:320, :]
    outs[128:192, :] = two_y_ref[256:320, :]
    for i in range(2):
        lanes = slice(512 * i, 512 * i + 512)
        outs[192:240, lanes] = both_ref[144:192, lanes]
        outs[240:256, lanes] = both_ref[144 + 16 * i : 160 + 16 * i, 1024:1536]


def stack_body(sizes, ids, *refs):
    out_ref = refs[-1]
    start = 0
    for ref, size in zip(refs[:-1], sizes):
        out_ref[start : start + size, :] = ref[0:size, :]
        start += size


def stack(ids, *arrays, sizes=None):
    sizes = sizes or tuple(a.shape[0] for a in arrays)
    shape = struct((sum(sizes), arrays[0].shape[1]), BF)
    return call(partial(stack_body, sizes), shape, (ids, *arrays), micros=0.7)


def place_rows(ids, own_ref, theirs_ref, two_ref, three_ref, out_ref):
    half = ids[1] % 2
    pair = ids[1] // 2
    own_rows = own_ref.shape[0]
    cut = two_ref.shape[0]
    tail = out_ref.shape[0] - own_rows - cut
    for value in range(2):
        first, second = (own_ref, theirs_ref) if value == 0 else (theirs_ref, own_ref)

        @pl.when(half == value)
        def _():
            out_ref[0:own_rows, :] = first[...]

        @pl.when((half == value) & (pair == 0))
        def _():
            out_ref[own_rows:, :] = second[0 : cut + tail, :]

        @pl.when((half == value) & (pair == 1))
        def _():
            out_ref[own_rows + cut :, :] = second[0:tail, :]

    @pl.when(pair == 1)
    def _():
        out_ref[own_rows : own_rows + cut, :] = two_ref[...] + three_ref[...]


def place_grad_body(ids, own_ref, theirs_ref, two_ref, three_ref, out_ref):
    place_rows(ids, own_ref, theirs_ref, two_ref, three_ref, out_ref)
    own_rows = own_ref.shape[0]
    rows = out_ref.shape[0]
    live = key_valid(ids, (rows - own_rows, 1), 0, own_rows, own_rows)
    tail = out_ref[own_rows:, :].astype(F32)
    out_ref[own_rows:, :] = jnp.where(live, tail, 0.0).astype(BF)


def parts_of(refs):
    a, x, y, d, other = refs
    parts = {0: (a, 0), 2: (x, 0), 4: (y, 0), 6: (d, 0)}
    parts.update({2 * i + 1: (other, 144 * i) for i in range(4)})
    return parts


def piece_tile(parts, k, lanes):
    ref, row = parts[k]
    return ref[row : row + 128, lanes]


def qkv_body(ids, own_ref, theirs_ref, two_ref, three_ref, *refs):
    parts = parts_of(refs[:5])
    x_ref, qkv_ref, even_ref, odd_ref, par_ref, norm_ref, bias_ref = refs[5:]
    place_rows(ids, own_ref, theirs_ref, two_ref, three_ref, x_ref)
    f = ids[0]
    half = ids[1] % 2
    rows = x_ref.shape[0]
    for k in range(8):
        ref, at = parts[k]
        par_ref[pl.ds(f ^ k, 1), :] = ref[at + 128 : at + 129, :].astype(F32)
    gain = natural(par_ref, 0)
    shift = natural(par_ref, 128)
    low = lanes_low((1, 128))
    bias_ref[...] = jnp.zeros_like(bias_ref)
    for start, place in ((768, 0), (896, 1024)):
        block = par_ref[:, start : start + 128]
        turned = pltpu.roll(block, HD, 1)
        lower = jnp.where(half == 0, block, turned)
        upper = jnp.where(half == 0, turned, block)
        for j in range(4):
            bias_ref[:, place + 128 * j : place + 128 * j + 128] = jnp.where(
                low, lower[2 * j : 2 * j + 1], upper[2 * j + 1 : 2 * j + 2]
            )

    def norm(i, carry):
        at = pl.ds(offset(i, 32), 32)
        values = x_ref[at, :].astype(F32)
        norm_ref[at, :] = normalize(values, gain, shift).astype(BF)
        return carry

    lax.fori_loop(0, rows // 32, norm, 0, unroll=True)
    for place, k in enumerate(LY):
        target = even_ref if place < 4 else odd_ref
        column = 128 * (place % 4)
        target[:, column : column + 128] = norm_ref[:, pl.ds(offset(f ^ k, 128), 128)]
    left = jnp.concatenate([even_ref[...], odd_ref[...]], axis=1)
    for n in range(6):
        lanes = slice(256 * n, 256 * n + 256)
        weight = jnp.concatenate([piece_tile(parts, k, lanes) for k in LY], axis=0)
        qkv_ref[:, lanes] = (dot_nn(left, weight) + bias_ref[:, lanes]).astype(BF)


def key_valid(ids, shape, axis, own_rows, first=0):
    pair = ids[1] // 2
    place = lax.broadcasted_iota(jnp.int32, shape, axis) + first
    return (place < LEN + pair) & ((place != own_rows) | (pair == 0))


def head_masked(block, head, factor=None):
    wide = block.astype(F32)
    low = lanes_low(wide.shape)
    keep = low if head == 0 else jnp.logical_not(low)
    if factor is not None:
        wide = wide * factor
    return jnp.where(keep, wide, 0.0).astype(BF)


def attend_body(own_rows, tile, ids, qkv_ref, o_ref):
    rows = qkv_ref.shape[0]
    live = key_valid(ids, (1, rows), 1, own_rows)
    low = lanes_low((tile, 128))
    for j in range(4):
        lanes = slice(128 * j, 128 * j + 128)
        key = qkv_ref[:, 512 + 128 * j : 640 + 128 * j]
        value = qkv_ref[:, 1024 + 128 * j : 1152 + 128 * j]
        keys = [head_masked(key, head, HD**-0.5) for head in range(2)]
        for t in range(rows // tile):
            at = slice(t * tile, t * tile + tile)
            outs = []
            for head in range(2):
                scores = jnp.where(live, dot_nt(qkv_ref[at, lanes], keys[head]), masked_score)
                peak = jnp.max(scores, axis=1, keepdims=True)
                lifted = jnp.exp(scores - peak)
                total = jnp.sum(lifted, axis=1, keepdims=True)
                outs.append(dot_nn(lifted.astype(BF), value) / total)
            o_ref[at, lanes] = jnp.where(low, outs[0], outs[1]).astype(BF)


def attend_back_body(own_rows, ids, qkv_ref, g0_ref, g1_ref, gq_ref, gk_ref, gv_ref):
    rows = qkv_ref.shape[0]
    scale = HD**-0.5
    live = key_valid(ids, (rows, 1), 0, own_rows)
    low = lanes_low((rows, 128))
    for j in range(4):
        lanes = slice(128 * j, 128 * j + 128)
        query = qkv_ref[:, lanes]
        key = qkv_ref[:, 512 + 128 * j : 640 + 128 * j]
        value = qkv_ref[:, 1024 + 128 * j : 1152 + 128 * j]
        grad = jnp.concatenate([g0_ref[:, lanes], g1_ref[:, lanes]], axis=0)
        grad_q, grads_k, grads_v = None, [], []
        for head in range(2):
            keys = head_masked(key, head, scale)
            values = head_masked(value, head)
            scores = jnp.where(live, dot_nt(keys, query), masked_score)
            peak = jnp.max(scores, axis=0, keepdims=True)
            lifted = jnp.exp(scores - peak)
            probs = lifted * (1.0 / jnp.sum(lifted, axis=0, keepdims=True))
            grad_p = dot_nt(values, grad)
            inner = jnp.sum(grad_p * probs, axis=0, keepdims=True)
            grad_s = (probs * (grad_p - inner)).astype(BF)
            grads_v.append(dot_nn(probs.astype(BF), grad))
            grads_k.append(dot_nn(grad_s, query) * scale)
            part = dot_tn(grad_s, keys)
            grad_q = part if grad_q is None else grad_q + part
        gq_ref[:, lanes] = grad_q.astype(BF)
        gk_ref[:, lanes] = jnp.where(low, grads_k[0], grads_k[1]).astype(BF)
        gv_ref[:, lanes] = jnp.where(low, grads_v[0], grads_v[1]).astype(BF)


def mixed_body(ids, o_ref, even_ref, odd_ref, first_ref, second_ref, w_ref):
    f = ids[0]
    for place, k in enumerate((0, 2, 4, 6)):
        row = HD * place
        w_ref[pl.ds(offset(f ^ k, HD), HD), :] = even_ref[row : row + HD, :]
        w_ref[pl.ds(offset(f ^ k ^ 1, HD), HD), :] = odd_ref[row : row + HD, :]
    size = first_ref.shape[0]
    for n in range(4):
        lanes = slice(256 * n, 256 * n + 256)
        first_ref[:, lanes] = dot_nn(o_ref[0:size, :], w_ref[:, lanes]).astype(BF)
    for n in range(4):
        lanes = slice(256 * n, 256 * n + 256)
        second_ref[:, lanes] = dot_nn(o_ref[size:, :], w_ref[:, lanes]).astype(BF)


def middle_body(base, ids, par_ref, x_ref, mine_ref, theirs_ref, mid_ref, even_ref, odd_ref, norm_ref):
    f = ids[0]
    rows = mid_ref.shape[0]
    gain = natural(par_ref, 384)
    shift = natural(par_ref, 512)
    bias = natural(par_ref, 256)

    def norm(i, carry):
        at = pl.ds(offset(i, 32), 32)
        middle = x_ref[pl.ds(pl.multiple_of(base + i * 32, 32), 32), :].astype(F32)
        middle = middle + (mine_ref[at, :].astype(F32) + theirs_ref[at, :].astype(F32) + bias)
        mid_ref[at, :] = middle
        norm_ref[at, :] = normalize(middle, gain, shift).astype(BF)
        return carry

    lax.fori_loop(0, rows // 32, norm, 0, unroll=True)
    for place, k in enumerate(LY):
        target = even_ref if place < 4 else odd_ref
        column = 128 * (place % 4)
        target[:, column : column + 128] = norm_ref[:, pl.ds(offset(f ^ k, 128), 128)]


def mlp_body(base, ids, par_ref, even_ref, odd_ref, gm_ref, one_a, one_b, two_a, two_b, *refs):
    act_e_ref, act_o_ref, gu_ref, gh_ref, bias_ref, u_ref, g_ref = refs
    f = ids[0]
    half = ids[1] % 2
    rows = even_ref.shape[0]

    def one_rows(place, start, size, lanes):
        ref = one_a if place < 4 else one_b
        return ref[pl.ds(256 * (place % 4) + start, size), lanes]

    left = jnp.concatenate([even_ref[...], odd_ref[...]], axis=1)
    grad = gm_ref[base : base + rows, :]
    for place, k in enumerate(LX):
        block = f ^ k
        at_lanes = pl.ds(offset(block % 4, 256), 256)
        weight = jnp.concatenate([one_rows(j, offset(block // 4, 128), 128, at_lanes) for j in range(8)], axis=0)
        u_ref[...] = dot_nn(left, weight)
        two_ref = two_a if place < 4 else two_b
        g_ref[...] = dot_nt(grad, two_ref[256 * (place % 4) : 256 * (place % 4) + 256, :])
        row = par_ref[pl.ds(block, 1), pl.ds(offset(4 + half, 256), 256)]
        act_ref = act_e_ref if place < 4 else act_o_ref
        column = 256 * (place % 4)

        def gelu(i, total):
            at = pl.ds(offset(i, 32), 32)
            u = u_ref[at, :] + row
            cdf = 0.5 + 0.5 * lax.erf(u * HALF_ROOT)
            act_ref[at, column : column + 256] = (u * cdf).astype(BF)
            slope = cdf + u * (jnp.exp(-0.5 * (u * u)) * DENSITY)
            gu = (g_ref[at, :] * slope).astype(BF)
            gu_ref[at, pl.ds(offset(block, 256), 256)] = gu
            return total + jnp.sum(gu.astype(F32), axis=0, keepdims=True)

        total = lax.fori_loop(0, rows // 32, gelu, jnp.zeros((1, 256), F32), unroll=True)
        bias_ref[pl.ds(block, 1), :] = total
    for j in range(4):
        total = None
        for part in range(2):
            weight = jnp.concatenate(
                [one_rows(place, 128 * part, 128, slice(None)) for place in (2 * j, 2 * j + 1)], axis=0
            )
            term = dot_nt(gu_ref[:, 1024 * part : 1024 * part + 1024], weight)
            total = term if total is None else total + term
        gh_ref[:, pl.ds(offset(f ^ LY[2 * j], 128), 128)] = total[:, 0:128].astype(BF)
        gh_ref[:, pl.ds(offset(f ^ LY[2 * j + 1], 128), 128)] = total[:, 128:256].astype(BF)


def out_first_body(ids, e_ref, o_ref, two_a, two_b, y_ref):
    left = jnp.concatenate([e_ref[...], o_ref[...]], axis=1)
    for n in range(4):
        lanes = slice(256 * n, 256 * n + 256)
        weight = jnp.concatenate([two_a[:, lanes], two_b[:, lanes]], axis=0)
        y_ref[:, lanes] = dot_nn(left, weight).astype(BF)


def out_body(ids, first_ref, e_ref, o_ref, two_a, two_b, keep_ref, send_ref, y_ref):
    half = ids[1] % 2
    start = first_ref.shape[0]
    y_ref[0:start, :] = first_ref[...]
    left = jnp.concatenate([e_ref[...], o_ref[...]], axis=1)
    for n in range(4):
        lanes = slice(256 * n, 256 * n + 256)
        weight = jnp.concatenate([two_a[:, lanes], two_b[:, lanes]], axis=0)
        y_ref[start:, lanes] = dot_nn(left, weight).astype(BF)
    rows = keep_ref.shape[0]
    shift = y_ref.shape[0] - rows
    keep_ref[...] = y_ref[pl.ds(offset(half, shift), rows), :]
    send_ref[...] = y_ref[pl.ds(offset(1 - half, shift), rows), :]


def result_body(ids, par_ref, mid0_ref, mid1_ref, mine_ref, theirs_ref, out_ref, extra_ref):
    half = ids[1] % 2
    bias = natural(par_ref, 640)
    rows = out_ref.shape[0]
    shift = mid0_ref.shape[0] + mid1_ref.shape[0] - rows

    def step(i, carry):
        at = pl.ds(offset(i, 32), 32)
        place = half * shift + i * 32
        total = mine_ref[at, :].astype(F32) + theirs_ref[at, :].astype(F32) + bias
        size = mid0_ref.shape[0]

        @pl.when(place < size)
        def _():
            out_ref[at, :] = (total + mid0_ref[pl.ds(pl.multiple_of(place, 32), 32), :]).astype(BF)

        @pl.when(place >= size)
        def _():
            out_ref[at, :] = (total + mid1_ref[pl.ds(pl.multiple_of(place - size, 32), 32), :]).astype(BF)

        return carry

    lax.fori_loop(0, rows // 32, step, 0, unroll=True)
    spot = rows - shift
    extra_ref[...] = out_ref[spot : spot + extra_ref.shape[0], :]


def owner_rows_body(ids, valid_ref, full_ref, extra_ref, out_ref):
    half = ids[1] % 2
    pair = ids[1] // 2
    rows, cut = full_ref.shape[0], extra_ref.shape[0]
    tail = 2 * cut + 32 - rows
    shift = cut + tail
    spot = rows - shift
    width = full_ref.shape[1]

    def masked(at, values):
        valid = jnp.concatenate([valid_ref[at, :]] * (width // 128), axis=1)
        return jnp.where(valid > 0.0, values.astype(F32), 0.0).astype(out_ref.dtype)

    @pl.when(half == 0)
    def _():
        out_ref[...] = masked(slice(None), full_ref[...])

    @pl.when((half == 1) & (pair == 0))
    def _():
        top = slice(0, cut)
        out_ref[top, :] = masked(top, full_ref[spot : spot + cut, :])
        low = slice(cut, rows)
        border = full_ref[spot + cut : spot + cut + 1, :].astype(F32)
        first = lax.broadcasted_iota(jnp.int32, (cut, 1), 0) == 0
        out_ref[low, :] = masked(low, jnp.where(first, border, extra_ref[...].astype(F32)))

    @pl.when((half == 1) & (pair == 1))
    def _():
        top = slice(0, tail)
        out_ref[top, :] = masked(top, full_ref[spot + cut : spot + cut + tail, :])
        out_ref[tail:rows, :] = jnp.zeros((rows - tail, width), out_ref.dtype)


def rows_grad_body(step, ids, l0_ref, l1_ref, r0_ref, r1_ref, out_ref):
    rows = l0_ref.shape[0] + l1_ref.shape[0]
    left = jnp.concatenate([l0_ref[...], l1_ref[...]], axis=0)
    for n in range(out_ref.shape[1] // step):
        lanes = slice(step * n, step * n + step)
        if r0_ref.shape[0] == rows:
            right = r0_ref[:, lanes]
        else:
            right = jnp.concatenate([r0_ref[:, lanes], r1_ref[:, lanes]], axis=0)
        out_ref[:, lanes] = dot_tn(left, right).astype(BF)


def norm_back(values, grad, gain):
    center = values - jnp.mean(values, axis=-1, keepdims=True)
    scale = lax.rsqrt(jnp.mean(center * center, axis=-1, keepdims=True) + norm_eps)
    unit = center * scale
    scaled = grad * gain
    first = jnp.mean(scaled, axis=-1, keepdims=True)
    second = jnp.mean(scaled * unit, axis=-1, keepdims=True)
    return unit, scale * (scaled - first - unit * second)


def fold(values):
    total = values[0:8]
    for i in range(1, values.shape[0] // 8):
        total = total + values[8 * i : 8 * i + 8]
    return total


def spread(ref, start, partial_rows):
    row = jnp.sum(partial_rows, axis=0, keepdims=True)
    for i in range(8):
        ref[i : i + 1, start : start + 128] = row[:, 128 * i : 128 * i + 128]


def middle_back_body(base, ids, par_ref, mid_ref, gm_ref, mine_ref, theirs_ref, w_ref, gb_ref, go_ref, sums_ref):
    half = ids[1] % 2
    counts = jnp.where(half == 0, 1.0, 0.0)
    gain = natural(par_ref, 384)
    rows = mid_ref.shape[0]

    def step(i, carry):
        out_sum, gain_sum, shift_sum, last_sum = carry
        at = pl.ds(offset(i, 32), 32)
        mine = mine_ref[at, :].astype(F32)
        grad = mine + theirs_ref[at, :].astype(F32)
        unit, back = norm_back(mid_ref[at, :], grad, gain)
        gm = gm_ref[pl.ds(pl.multiple_of(base + i * 32, 32), 32), :].astype(F32)
        gb = (gm + back).astype(BF)
        gb_ref[at, :] = gb
        return (
            out_sum + fold(gb.astype(F32)),
            gain_sum + fold(mine * unit),
            shift_sum + fold(mine),
            last_sum + fold(gm),
        )

    zero = jnp.zeros((8, mid_ref.shape[1]), F32)
    sums = lax.fori_loop(0, rows // 32, step, (zero, zero, zero, zero), unroll=True)
    spread(sums_ref, 0, sums[0] * counts)
    spread(sums_ref, 128, sums[1])
    spread(sums_ref, 256, sums[2])
    spread(sums_ref, 384, sums[3] * counts)
    grad = gb_ref[...]
    for n in range(2):
        rows = slice(256 * n, 256 * n + 256)
        go_ref[:, rows] = dot_nt(grad, w_ref[rows, :]).astype(BF)


def out_grad_body(ids, o_ref, gb0_ref, gb1_ref, keep_ref, send_ref, grad_ref):
    f = ids[0]
    for n in range(4):
        lanes = slice(256 * n, 256 * n + 256)
        right = jnp.concatenate([gb0_ref[:, lanes], gb1_ref[:, lanes]], axis=0)
        grad_ref[:, lanes] = dot_tn(o_ref[...], right).astype(BF)
    for place, k in enumerate(LX):
        target = keep_ref if place < 4 else send_ref
        row = HD * (place % 4)
        target[row : row + HD, :] = grad_ref[pl.ds(offset(f ^ k, HD), HD), :]


def input_grad_body(ids, x_ref, par_ref, gq_ref, gk_ref, gv_ref, *refs):
    parts = parts_of(refs[:5])
    keep_ref, send_ref, sums_ref, wide_ref, gh_ref = refs[5:]
    f = ids[0]
    left = jnp.concatenate([gq_ref[...], gk_ref[...], gv_ref[...]], axis=1)
    for j in range(4):
        first, second = LY[2 * j], LY[2 * j + 1]
        weight = jnp.concatenate(
            [piece_tile(parts, first, slice(None)), piece_tile(parts, second, slice(None))], axis=0
        )
        total = dot_nt(left, weight)
        wide_ref[:, pl.ds(offset(f ^ first, 128), 128)] = total[:, 0:128]
        wide_ref[:, pl.ds(offset(f ^ second, 128), 128)] = total[:, 128:256]

    def step(i, carry):
        gain_sum, shift_sum = carry
        at = pl.ds(offset(i, 32), 32)
        grad = wide_ref[at, :]
        gh_ref[at, :] = grad.astype(BF)
        values = x_ref[at, :].astype(F32)
        center = values - jnp.mean(values, axis=-1, keepdims=True)
        unit = center * lax.rsqrt(jnp.mean(center * center, axis=-1, keepdims=True) + norm_eps)
        return gain_sum + fold(grad * unit), shift_sum + fold(grad)

    zero = jnp.zeros((8, x_ref.shape[1]), F32)
    gain_sum, shift_sum = lax.fori_loop(0, x_ref.shape[0] // 32, step, (zero, zero), unroll=True)
    half = ids[1] % 2
    rows = keep_ref.shape[0]
    shift = x_ref.shape[0] - rows
    keep_ref[...] = gh_ref[pl.ds(offset(half, shift), rows), :]
    send_ref[...] = gh_ref[pl.ds(offset(1 - half, shift), rows), :]
    spread(sums_ref, 0, gain_sum)
    spread(sums_ref, 128, shift_sum)


def qkv_grad_body(ids, even_ref, odd_ref, gq_ref, gk_ref, gv_ref, one_ref, mid0_ref, mid1_ref, fc0_ref, fc1_ref, *refs):
    keep_ref, send_ref, par_ref = refs
    f = ids[0]
    half = ids[1] % 2
    par_ref[:, 0:256] = one_ref[...]
    par_ref[:, 256:768] = mid0_ref[...] + mid1_ref[...]
    fc_sum = fc0_ref[...] + fc1_ref[...]
    low = lanes_low((1, 128))
    mine = low == (half == 0)
    for g_ref, place in ((gq_ref, 768), (gv_ref, 896)):
        row = jnp.sum(g_ref[...].astype(F32), axis=0, keepdims=True)
        for j in range(4):
            block = row[:, 128 * j : 128 * j + 128]
            turned = pltpu.roll(jnp.broadcast_to(block, (8, 128)), HD, 1)[0:1]
            first = jnp.where(half == 0, block, turned)
            second = jnp.where(half == 0, turned, block)
            par_ref[2 * j : 2 * j + 1, place : place + 128] = jnp.where(mine, first, 0.0)
            par_ref[2 * j + 1 : 2 * j + 2, place : place + 128] = jnp.where(mine, second, 0.0)
    zero = jnp.zeros((8, 256), F32)
    par_ref[:, 1024:1280] = jnp.where(half == 0, fc_sum, zero)
    par_ref[:, 1280:1536] = jnp.where(half == 1, fc_sum, zero)
    order_b = LY
    place_a = {k: i for i, k in enumerate(LX)}
    for j in range(4):
        source = even_ref if j < 2 else odd_ref
        left = source[:, 256 * (j % 2) : 256 * (j % 2) + 256]
        for n, g_ref in enumerate((gq_ref, gk_ref, gv_ref)):
            lanes = slice(512 * n, 512 * n + 512)
            total = dot_tn(left, g_ref[...]).astype(BF)
            for i in range(2):
                k = order_b[2 * j + i]
                target = keep_ref if place_a[k] < 4 else send_ref
                row = 64 * (place_a[k] % 4)
                target[row : row + 64, lanes] = total[128 * i : 128 * i + 64]
                row = 256 + 80 * ((2 * j + i) % 4)
                target[row : row + 64, lanes] = total[128 * i + 64 : 128 * i + 128]
    for place, k in enumerate(order_b):
        target = keep_ref if place < 4 else send_ref
        row = 320 + 80 * (place % 4)
        target[row : row + 16, :] = jnp.broadcast_to(par_ref[pl.ds(f ^ k, 1), :], (16, 1536)).astype(BF)


def input_back_body(ids, par_ref, x_ref, gb0_ref, gb1_ref, mine_ref, theirs_ref, out_ref, extra_ref, gb_ref):
    half = ids[1] % 2
    gain = natural(par_ref, 0)
    rows = out_ref.shape[0]
    shift = x_ref.shape[0] - rows
    size = gb0_ref.shape[0]
    gb_ref[0:size, :] = gb0_ref[...]
    gb_ref[size:, :] = gb1_ref[...]

    def step(i, carry):
        at = pl.ds(offset(i, 32), 32)
        place = pl.ds(pl.multiple_of(half * shift + i * 32, 32), 32)
        grad = mine_ref[at, :].astype(F32) + theirs_ref[at, :].astype(F32)
        back = norm_back(x_ref[place, :].astype(F32), grad, gain)[1]
        out_ref[at, :] = gb_ref[place, :].astype(F32) + back
        return carry

    lax.fori_loop(0, rows // 32, step, 0, unroll=True)
    spot = rows - shift
    extra_ref[...] = out_ref[spot : spot + extra_ref.shape[0], :].astype(BF)


def line_body(ids, ka_ref, ra_ref, kb_ref, rb_ref, ko_ref, *outs):
    s = ids[1]
    wide_a, wide_b, wide_o = outs[4:]
    wide_a[...] = halve(ka_ref[...], ra_ref[0:64, :])
    wide_b[...] = halve(kb_ref[...], rb_ref[...])
    add_packed(wide_o, ko_ref, 0, ra_ref, 64)
    for turn in range(4):
        t = s ^ turn
        lanes = pl.ds(offset(t, 384), 384)
        out_ref = outs[turn]
        out_ref[0:64, :] = wide_a[:, lanes]
        out_ref[64:128, :] = wide_b[0:64, lanes]
        block = jnp.concatenate([wide_b[64:65, 384 * i : 384 * i + 384].astype(F32) for i in range(4)], axis=0)
        block = jnp.concatenate([block, jnp.zeros((12, 384), F32)], axis=0)
        out_ref[128:144, :] = block.astype(BF)
        out_ref[144:192, 0:256] = wide_o[0:48, pl.ds(offset(t, 256), 256)]
        for i in range(2):
            out_ref[144 + 16 * i : 160 + 16 * i, 256:384] = wide_o[48:64, pl.ds(offset(2 * t + i, 128), 128)]
        out_ref[176:192, 256:384] = jnp.zeros((16, 128), BF)


def line_mlp_body(ids, k2_ref, r2_ref, k1_ref, r1_ref, keep_ref, send_ref, two, one):
    s = ids[1]
    two[...] = halve(k2_ref[...], r2_ref[...])
    one[...] = halve(k1_ref[...], r1_ref[...])
    for turn in range(4):
        t = s ^ turn
        out_ref = keep_ref if turn < 2 else send_ref
        at = 512 * (turn % 2)
        out_ref[at : at + 256, :] = two[:, pl.ds(offset(t, 256), 256)]
        for i in range(2):
            row = at + 256 + 128 * i
            out_ref[row : row + 128, :] = one[:, pl.ds(offset(2 * t + i, 256), 256)]


def pack_out(target_ref, row, values):
    for i in range(2):
        lanes = slice(512 * i, 512 * i + 512)
        target_ref[row : row + 48, lanes] = values[0:48, lanes]
        target_ref[row + 16 * i : row + 16 * i + 16, 1024:1536] = values[48:64, lanes]
    target_ref[row + 32 : row + 48, 1024:1536] = jnp.zeros((16, 512), values.dtype)


def merge_body(ids, keep_ref, got_ref, stay_ref, send_ref):
    half = stay_ref.shape[0]
    stay_ref[...] = halve(keep_ref[0:half, :], got_ref[0:half, :])
    send_ref[...] = halve(keep_ref[half:, :], got_ref[half:, :])


def merge(ids, keep, got, micros=0.05):
    shape = struct((keep.shape[0] // 2, keep.shape[1]), BF)
    return call(merge_body, [shape, shape], (ids, keep, got), micros=micros)


def merge_qkv_body(ids, keep_ref, got_ref, ko_ref, ro_ref, stay_a, send_a, stay_b, send_b, stay_o):
    def total(start, size):
        return halve(keep_ref[start : start + size, :], got_ref[start : start + size, :])

    stay_a[...] = total(0, 128)
    send_a[0:128, :] = total(128, 128)
    stay_b[...] = total(256, 160)
    send_b[...] = total(416, 160)
    stay_o[...] = halve(ko_ref[0:128, :], ro_ref[0:128, :])
    for i in range(2):
        rows = slice(128 + 64 * i, 192 + 64 * i)
        pack_out(send_a, 128 + 48 * i, halve(ko_ref[rows, :], ro_ref[rows, :]))


def add_packed(target_ref, keep_ref, row, got_ref, at):
    for i in range(2):
        lanes = slice(512 * i, 512 * i + 512)
        target_ref[0:48, lanes] = halve(keep_ref[row : row + 48, lanes], got_ref[at : at + 48, lanes])
        target_ref[48:64, lanes] = halve(
            keep_ref[row + 48 : row + 64, lanes], got_ref[at + 16 * i : at + 16 * i + 16, 1024:1536]
        )


def merge_last_body(ids, ka_ref, ra_ref, kb_ref, rb_ref, ko_ref, stay_a, send_a, stay_b, send_b, stay_o, wide):
    stay_a[...] = halve(ka_ref[0:64, :], ra_ref[0:64, :])
    send_a[0:64, :] = halve(ka_ref[64:128, :], ra_ref[64:128, :])
    stay_b[...] = halve(kb_ref[0:80, :], rb_ref[0:80, :])
    send_b[...] = halve(kb_ref[80:160, :], rb_ref[80:160, :])
    add_packed(stay_o, ko_ref, 0, ra_ref, 128)
    add_packed(wide, ko_ref, 64, ra_ref, 176)
    pack_out(send_a, 64, wide[...])


def join_mlp_body(ids, own_ref, pair_ref, one_ref, two_ref):
    half = ids[1] % 2
    for ref, place in ((own_ref, half), (pair_ref, 1 - half)):
        two_ref[pl.ds(offset(place, 256), 256), :] = ref[0:256, :].astype(F32)
        for i in range(2):
            lanes = pl.ds(offset(2 * i + place, 256), 256)
            one_ref[:, lanes] = ref[256 + 128 * i : 384 + 128 * i, :].astype(F32)


def join_body(ids, own_ref, pair_ref, far_ref, cross_ref, out_ref, wo_ref, sums_ref, wide_ref):
    s = ids[1]
    half = s % 2
    lower = half == 0
    low = lanes_low((128, 128))

    def sums(rows, lanes):
        same = own_ref[rows, lanes].astype(F32) + far_ref[rows, lanes].astype(F32)
        return same, pair_ref[rows, lanes].astype(F32) + cross_ref[rows, lanes].astype(F32)

    for j in range(3):
        same, other = sums(slice(0, 128), slice(128 * j, 128 * j + 128))
        first = jnp.where(lower, same, other)
        second = jnp.where(lower, other, same)
        out_ref[:, 256 * j : 256 * j + 128] = jnp.where(low, first, pltpu.roll(second, HD, 1))
        out_ref[:, 256 * j + 128 : 256 * j + 256] = jnp.where(low, pltpu.roll(first, HD, 1), second)
    places = [(slice(144, 192), slice(0, 256), 0, slice(0, 256))]
    places += [(slice(144 + 16 * i, 160 + 16 * i), slice(256, 384), 48, slice(128 * i, 128 * i + 128)) for i in range(2)]
    for rows, lanes, row, target in places:
        same, other = sums(rows, lanes)
        size = same.shape[0]
        wo_ref[pl.ds(pl.multiple_of(half * 64 + row, 16), size), target] = same
        wo_ref[pl.ds(pl.multiple_of((1 - half) * 64 + row, 16), size), target] = other
    same, other = sums(slice(128, 144), slice(0, 384))
    total = same + other
    for i in range(4):
        for n in range(3):
            spot = 3 * i + n
            block = total[i : i + 1, 128 * n : 128 * n + 128]
            if spot < 8:
                block = pltpu.roll(jnp.broadcast_to(block, (8, 128)), (128 - 32 * s) % 128, 1)[0:1]
                sums_ref[spot : spot + 1, :] = block
            else:
                wide_ref[spot - 8 : spot - 7, :] = block
    sums_ref[8:9, :] = wide_ref[pl.ds(s, 1), :]


def halve(keep, received):
    return (keep.astype(F32) + received.astype(F32)).astype(BF)


def paired_shards(
    tokens,
    segment_ids,
    ln1_gain,
    ln1_bias,
    w_qkv,
    q_bias,
    v_bias,
    w_out,
    out_bias,
    ln2_gain,
    ln2_bias,
    w_fc1,
    fc1_bias,
    w_fc2,
    fc2_bias,
    cotangent,
):
    own_rows, width = tokens.shape
    cut = own_rows // 2
    tail = 32
    rows = own_rows + cut + tail
    f = lax.axis_index("fsdp")
    s = lax.axis_index("seq")
    ids = jnp.where(lax.iota(jnp.int32, 2) == 0, f, s).astype(jnp.int32)

    def exchange(own, extra, name):
        extra = zshift(extra, ((1, 2),), name + "_extra")
        return zshift(own, PAIR, name), extra, zshift(extra, ((2, 3),), name + "_relay")

    hbm = partial(pltpu.with_memory_space_constraint, memory_space=pltpu.HBM)
    vectors = [ln1_gain, ln1_bias, out_bias, ln2_gain, ln2_bias, fc2_bias, q_bias, v_bias, fc1_bias]
    a, both, tokens_extra = call(
        pick_qkv,
        [struct((144, 1536), BF), struct((192, 1536), BF), struct((own_rows - cut, width), BF)],
        (ids, *[hbm(v) for v in (w_qkv, tokens, w_out, *vectors)]),
        scratch=[
            pltpu.VMEM(w_qkv.shape, BF),
            pltpu.VMEM((64, width), BF),
            *[pltpu.VMEM(v.shape, BF) for v in vectors],
            pltpu.SemaphoreType.DMA((12,)),
        ],
        space=pltpu.HBM, micros=2.2)
    moved_tokens = exchange(tokens, tokens_extra, "tokens")
    one, two = call(
        pick_mlp,
        [struct((320, 1024), BF), struct((320, 1024), BF)],
        (ids, hbm(after(w_fc1, a)), hbm(w_fc2), hbm(w_out)),
        scratch=[pltpu.SemaphoreType.DMA((11,))],
        space=pltpu.HBM, micros=1.9)
    pieces = [a, fshift(a, 2, "qkv_x"), fshift(a, 4, "qkv_y"), fshift(both, 6, "qkv_xy")]
    pieces.append(fshift(stack(ids, after(a, *moved_tokens, one), *pieces[1:], sizes=(144,) * 4), 1, "qkv_core"))

    one_x = fshift(after(one, moved_tokens[0]), 2, "one_x")
    two_y = fshift(after(two, moved_tokens[0]), 4, "two_y")

    one_two, two_two, outs_even = call(
        stack_mlp_body,
        [struct((512, 1024), BF), struct((512, 1024), BF), struct((256, 1024), BF)],
        (ids, one, one_x, two, two_y, pieces[3]), micros=60.0)
    outs_odd = fshift(outs_even, 1, "out_core")
    x, qkv, h1_e, h1_o, par = call(
        qkv_body,
        [
            struct((rows, width), BF),
            struct((rows, 1536), BF),
            struct((rows, 512), BF),
            struct((rows, 512), BF),
            struct((8, 1536), F32),
        ],
        (ids, after(tokens, one_two), *moved_tokens, *pieces),
        scratch=[pltpu.VMEM((rows, 1024), BF), pltpu.VMEM((1, 1536), F32)], micros=6.8)
    valid = segment_ids >= 0
    gm_own = jnp.where(valid[:, None], after(cotangent, *moved_tokens), jnp.zeros_like(cotangent))
    valid_lanes = jnp.broadcast_to(valid[:, None].astype(F32), (own_rows, 128))
    moved_gm = exchange(gm_own, gm_own[cut:], "cotangent")

    heads_o = call(
        partial(attend_body, own_rows, rows // 2), struct((rows, 512), BF), (ids, qkv), micros=7.1, limit=16
    )
    sizes = (320, rows - 320)

    mine_0, mine_1, w_out_full = call(
        mixed_body,
        [struct((sizes[0], width), BF), struct((sizes[1], width), BF), struct((512, width), BF)],
        (ids, heads_o, outs_even, outs_odd), micros=1.4)
    theirs_0 = zshift(mine_0, PAIR, "mixed")
    theirs_1 = zshift(after(mine_1, mine_0), PAIR, "mixed")
    gm = call(place_grad_body, struct((rows, width), BF), (ids, after(gm_own, mine_1), *moved_gm), micros=25.0)
    one_even = stack(ids, after(one_two, gm), fshift(one_two, 4, "one_y"))
    two_even = stack(ids, after(two_two, gm), fshift(two_two, 2, "two_x"))
    weights = (one_even, fshift(one_even, 1, "one_core"), two_even, fshift(two_even, 1, "two_core"))

    def middle(chunk, mine, theirs, micros):
        part = sizes[chunk]
        return call(
            partial(middle_body, chunk * sizes[0]),
            [struct((part, 1024), F32), struct((part, 512), BF), struct((part, 512), BF)],
            (ids, par, x, mine, theirs),
            scratch=[pltpu.VMEM((part, 1024), BF)],
            micros=micros,
        )

    def mlp(chunk, h2_e, h2_o):
        part = sizes[chunk]
        return call(
            partial(mlp_body, chunk * sizes[0]),
            [
                struct((part, 1024), BF),
                struct((part, 1024), BF),
                struct((part, 2048), BF),
                struct((part, 1024), BF),
                struct((8, 256), F32),
            ],
            (ids, par, h2_e, h2_o, gm, *weights),
            scratch=[pltpu.VMEM((part, 256), F32), pltpu.VMEM((part, 256), F32)],
            micros=9.5,
        )

    mid_0, h2_e0, h2_o0 = middle(0, mine_0, theirs_0, 60.0)
    act_e0, act_o0, gu_0, gh2_0, fc1_sums_0 = mlp(0, h2_e0, h2_o0)
    gh2_theirs_0 = zshift(gh2_0, PAIR, "mlp_grad")
    mid_1, h2_e1, h2_o1 = middle(1, after(mine_1, gh2_0), theirs_1, 2.0)
    act_e1, act_o1, gu_1, gh2_1, fc1_sums_1 = mlp(1, h2_e1, h2_o1)
    gh2_theirs_1 = zshift(gh2_1, PAIR, "mlp_grad")

    def row_grad(l0, l1, r0, r1, step):
        return call(
            partial(rows_grad_body, step),
            struct((l0.shape[1], r0.shape[1]), BF),
            (ids, l0, l1, r0, r1), micros=2.4)

    send_two = row_grad(after(act_o0, gh2_1), act_o1, gm, gm, 256)
    got_two = fshift(send_two, 1, "two_grad_core")
    keep_two = row_grad(after(act_e0, send_two), act_e1, gm, gm, 256)
    send_one = row_grad(after(h2_o0, keep_two), h2_o1, gu_0, gu_1, 512)
    got_one = fshift(send_one, 1, "one_grad_core")

    def middle_back(chunk, mid, mine, theirs, micros):
        part = sizes[chunk]
        return call(
            partial(middle_back_body, chunk * sizes[0]),
            [struct((part, 1024), BF), struct((part, 512), BF), struct((8, 512), F32)],
            (ids, par, mid, gm, mine, theirs, w_out_full),
            micros=micros,
        )

    gb_0, go_0, mid_sums_0 = middle_back(0, after(mid_0, send_one), gh2_0, gh2_theirs_0, 60.0)
    stay_two, send_two = merge(ids, after(keep_two, gb_0), got_two)
    got_two = fshift(send_two, 2, "two_grad_x")
    keep_one = row_grad(after(h2_e0, stay_two), h2_e1, gu_0, gu_1, 512)
    stay_one, send_one = merge(ids, keep_one, got_one)
    got_one = fshift(send_one, 4, "one_grad_y")
    y_first = call(
        out_first_body,
        struct((sizes[0], width), BF),
        (ids, after(act_e0, stay_one), act_o0, two_even, weights[3]),
        micros=0.1,
    )
    gb_1, go_1, mid_sums_1 = middle_back(1, after(mid_1, y_first), gh2_1, gh2_theirs_1, 4.0)
    keep_o, send_o = call(
        out_grad_body,
        [struct((256, 1024), BF)] * 2,
        (ids, heads_o, gb_0, gb_1),
        scratch=[pltpu.VMEM((512, 1024), BF)],
        micros=0.085,
    )
    got_o = fshift(send_o, 1, "out_grad_core")
    y_keep, y_send = call(
        out_body,
        [struct((own_rows, width), BF)] * 2,
        (ids, y_first, after(act_e1, keep_o), act_o1, two_even, weights[3]),
        scratch=[pltpu.VMEM((rows, width), BF)],
        micros=0.18,
    )
    y_theirs = zshift(y_send, PAIR, "output")
    gq, gk, gv = call(
        partial(attend_back_body, own_rows),
        [struct((rows, 512), BF)] * 3,
        (ids, qkv, after(go_0, y_keep), go_1),
        micros=0.7,
        limit=20,
    )
    stay_two, send_two = merge(ids, after(stay_two, gq), got_two, micros=1.0)
    got_two = fshift(send_two, 4, "two_grad_y")
    stay_one, send_one = merge(ids, after(stay_one, stay_two), got_one)
    got_one = fshift(send_one, 2, "one_grad_x")
    result, result_extra = call(
        result_body,
        [struct((own_rows, width), BF), struct((cut, width), BF)],
        (ids, par, mid_0, mid_1, after(y_keep, stay_one), y_theirs),
        micros=0.05,
    )
    result_extra = zshift(result_extra, ((3, 1),), "output_rows")
    gh1_keep, gh1_send, one_sums = call(
        input_grad_body,
        [struct((own_rows, 1024), BF), struct((own_rows, 1024), BF), struct((8, 256), F32)],
        (ids, x, par, gq, gk, after(gv, result), *pieces),
        scratch=[pltpu.VMEM((rows, 1024), F32), pltpu.VMEM((rows, 1024), BF)],
        micros=0.2,
    )
    gh1_theirs = zshift(gh1_send, PAIR, "input_grad")
    keep_q, send_q = call(
        qkv_grad_body,
        [struct((576, 1536), BF), struct((576, 1536), BF)],
        (ids, h1_e, h1_o, gq, gk, after(gv, gh1_send), one_sums, mid_sums_0, mid_sums_1, fc1_sums_0, fc1_sums_1),
        scratch=[pltpu.VMEM((8, 1536), F32)],
        micros=0.2,
    )
    got_q = fshift(send_q, 1, "qkv_grad_core")
    mlp_own, mlp_send = call(
        line_mlp_body,
        [struct((1024, 256), BF)] * 2,
        (ids, after(stay_two, keep_q), got_two, stay_one, got_one),
        scratch=[pltpu.VMEM((256, 1024), BF), pltpu.VMEM((128, 2048), BF)],
        micros=0.06,
    )
    mlp_got = zshift(mlp_send, FAR, "mlp_grad_far")
    layer_output = call(
        owner_rows_body,
        struct((own_rows, width), BF),
        (ids, valid_lanes, after(result, mlp_own), result_extra),
        micros=90.0,
    )
    stay_a, send_a, stay_b, send_b, stay_o = call(
        merge_qkv_body,
        [struct((n, 1536), BF) for n in (128, 224, 160, 160)] + [struct((128, 1024), BF)],
        (ids, after(keep_q, layer_output), got_q, keep_o, got_o),
        micros=0.05,
    )
    got_a = fshift(send_a, 2, "qkv_grad_x")
    got_b = fshift(send_b, 4, "qkv_grad_y")
    last_a, send_a, last_b, send_b, last_o = call(
        merge_last_body,
        [struct((64, 1536), BF), struct((112, 1536), BF)] + [struct((80, 1536), BF)] * 2 + [struct((64, 1024), BF)],
        (ids, stay_a, got_a, stay_b, got_b, stay_o),
        scratch=[pltpu.VMEM((64, 1024), BF)],
        micros=0.05,
    )
    got_a = fshift(send_a, 4, "qkv_grad_y")
    got_b = fshift(send_b, 2, "qkv_grad_x")
    back, back_extra = call(
        input_back_body,
        [struct((own_rows, width), F32), struct((cut, width), BF)],
        (ids, par, x, gb_0, gb_1, after(gh1_keep, last_a), gh1_theirs),
        scratch=[pltpu.VMEM((rows, width), BF)],
        micros=0.1,
    )
    back_extra = zshift(back_extra, ((3, 1),), "input_grad_rows")
    own, to_pair, to_far, to_cross = call(
        line_body,
        [struct((192, 384), BF)] * 4,
        (ids, after(last_a, back), got_a, last_b, got_b, last_o),
        scratch=[pltpu.VMEM((64, 1536), BF), pltpu.VMEM((80, 1536), BF), pltpu.VMEM((64, 1024), BF)],
        micros=0.05,
    )
    got_pair = zshift(to_pair, PAIR, "qkv_grad_z")
    got_far = zshift(to_far, FAR, "qkv_grad_z")
    got_cross = zshift(to_cross, CROSS, "qkv_grad_z")
    mlp_own, mlp_send = merge(ids, after(mlp_own, own), mlp_got)
    mlp_got = zshift(mlp_send, PAIR, "mlp_grad_pair")
    tokens_grad = call(
        owner_rows_body,
        struct((own_rows, width), F32),
        (ids, valid_lanes, after(back, mlp_own), back_extra),
        micros=0.1,
    )
    w_qkv_grad, w_out_grad, sums = call(
        join_body,
        [struct((128, 768), F32), struct((128, 256), F32), struct((9, 128), F32)],
        (ids, after(own, tokens_grad), got_pair, got_far, got_cross),
        scratch=[pltpu.VMEM((4, 128), F32)],
        micros=0.1,
    )
    w_fc1_grad, w_fc2_grad = call(
        join_mlp_body,
        [struct((128, 1024), F32), struct((512, 256), F32)],
        (ids, after(mlp_own, w_qkv_grad), mlp_got),
        micros=0.1,
    )

    def vector(spot):
        return sums[spot, 0:32]

    return (
        layer_output,
        tokens_grad,
        vector(0),
        vector(1),
        w_qkv_grad,
        vector(6),
        vector(7),
        w_out_grad,
        vector(2),
        vector(3),
        vector(4),
        w_fc1_grad,
        sums[8],
        w_fc2_grad,
        vector(5),
    )


def shards(*operands):
    tokens = operands[0]
    fits = (
        lax.axis_size("fsdp") == 8
        and lax.axis_size("seq") == 4
        and tokens.shape == (384, 1024)
        and operands[11].shape == (128, 4096)
    )
    return paired_shards(*operands) if fits else general_shards(*operands)


def solution(mesh):
    return jax.shard_map(
        shards,
        mesh=mesh,
        in_specs=(
            P(("fsdp", "seq"), None),
            P(("fsdp", "seq")),
            P("fsdp"),
            P("fsdp"),
            P("fsdp", None),
            P("fsdp"),
            P("fsdp"),
            P("fsdp", None),
            P("fsdp"),
            P("fsdp"),
            P("fsdp"),
            P("fsdp", None),
            P("fsdp"),
            P("fsdp", None),
            P("fsdp"),
            P(("fsdp", "seq"), None),
        ),
        out_specs=(
            P(("fsdp", "seq"), None),
            P(("fsdp", "seq"), None),
            P(("fsdp", "seq")),
            P(("fsdp", "seq")),
            P("fsdp", "seq"),
            P(("fsdp", "seq")),
            P(("fsdp", "seq")),
            P("fsdp", "seq"),
            P(("fsdp", "seq")),
            P(("fsdp", "seq")),
            P(("fsdp", "seq")),
            P("fsdp", "seq"),
            P(("fsdp", "seq")),
            P("fsdp", "seq"),
            P(("fsdp", "seq")),
        ),
        check_vma=False,
    )
```

```python
from functools import partial

import jax
import jax.numpy as jnp
from jax import lax
from jax.experimental import pallas as pl
from jax.experimental.pallas import tpu as pltpu
from jax.sharding import PartitionSpec as P

HD = 64
LEN = 577


norm_eps = 1e-06
masked_score = -1000000000.0


def normalize(values, gain, shift):
    row_mean = jnp.mean(values, axis=-1, keepdims=True)
    centered = values - row_mean
    variance = jnp.mean(centered * centered, axis=-1, keepdims=True)
    return centered * lax.rsqrt(variance + norm_eps) * gain + shift


def contract_rows(left, right):
    return lax.dot_general(
        left, right, (((0,), (0,)), ((), ())), preferred_element_type=jnp.float32
    )


def times_transposed(left, right):
    return lax.dot_general(
        left, right, (((1,), (1,)), ((), ())), preferred_element_type=jnp.float32
    )


def column_sum(values):
    return jnp.sum(values, axis=0, dtype=jnp.float32)


def shards_per_block(row_count, seq_count):
    for factor in range(1, seq_count + 1):
        if seq_count % factor == 0 and (row_count * factor >= 512 or factor == seq_count):
            return factor
    return seq_count


def add_window(total, delta, start):
    current = lax.dynamic_slice_in_dim(total, start, delta.shape[0], 0)
    return lax.dynamic_update_slice_in_dim(total, current + delta, start, 0)


def general_shards(
    tokens,
    segment_ids,
    ln1_gain,
    ln1_bias,
    w_qkv,
    q_bias,
    v_bias,
    w_out,
    out_bias,
    ln2_gain,
    ln2_bias,
    w_fc1,
    fc1_bias,
    w_fc2,
    fc2_bias,
    cotangent,
):
    row_count = tokens.shape[0]
    feature_width = tokens.shape[1]
    seq_count = lax.axis_size("seq")
    span_rows = row_count * seq_count
    local_heads = feature_width // seq_count // HD
    block_rows = row_count * shards_per_block(row_count, seq_count)
    block_count = span_rows // block_rows
    margin = LEN - 1
    window = block_rows + 2 * margin
    offsets = jnp.arange(block_count, dtype=jnp.int32) * block_rows
    scale = HD ** (-0.5)
    as_float = jnp.float32

    def weight_grad(left, right):
        return contract_rows(left, right)

    attn_set = (
        lax.all_gather(ln1_gain, "fsdp", axis=0, tiled=True),
        lax.all_gather(ln1_bias, "fsdp", axis=0, tiled=True),
        lax.all_gather(w_qkv, "fsdp", axis=0, tiled=True),
        lax.all_gather(q_bias, "fsdp", axis=0, tiled=True),
        lax.all_gather(v_bias, "fsdp", axis=0, tiled=True),
        lax.all_gather(w_out, "fsdp", axis=0, tiled=True),
        lax.all_gather(out_bias, "fsdp", axis=0, tiled=True),
    )
    span_labels = lax.all_gather(segment_ids, "seq", axis=0, tiled=True)
    inputs = tokens.astype(as_float)
    gain_one = attn_set[0].astype(as_float)
    shift_one = attn_set[1].astype(as_float)
    first_norm = normalize(inputs, gain_one, shift_one).astype(jnp.bfloat16)
    projected = jnp.dot(first_norm, attn_set[2], preferred_element_type=as_float)
    bias_all = jnp.concatenate(
        [
            attn_set[3].astype(as_float),
            jnp.zeros((feature_width,), as_float),
            attn_set[4].astype(as_float),
        ]
    )
    packed = (projected + bias_all).astype(jnp.bfloat16).reshape(row_count, 3, feature_width)
    head_rows = lax.all_to_all(packed, "seq", split_axis=2, concat_axis=0, tiled=True)
    query_heads = head_rows[:, 0, :].reshape(span_rows, local_heads, HD)
    key_heads = head_rows[:, 1, :].reshape(span_rows, local_heads, HD)
    value_heads = head_rows[:, 2, :].reshape(span_rows, local_heads, HD)
    key_padded = jnp.pad(key_heads, ((margin, margin), (0, 0), (0, 0)))
    value_padded = jnp.pad(value_heads, ((margin, margin), (0, 0), (0, 0)))
    label_padded = jnp.pad(span_labels, (margin, margin), constant_values=-2)

    def block_scores(offset):
        query_block = lax.dynamic_slice_in_dim(query_heads, offset, block_rows, 0)
        label_block = lax.dynamic_slice_in_dim(span_labels, offset, block_rows, 0)
        key_window = lax.dynamic_slice_in_dim(key_padded, offset, window, 0)
        value_window = lax.dynamic_slice_in_dim(value_padded, offset, window, 0)
        label_window = lax.dynamic_slice_in_dim(label_padded, offset, window, 0)
        scaled = (
            jnp.einsum("qhd,khd->hqk", query_block, key_window, preferred_element_type=as_float)
            * scale
        )
        same_image = label_block[:, None] == label_window[None, :]
        return (
            query_block,
            key_window,
            value_window,
            jnp.where(same_image[None], scaled, masked_score),
        )

    def block_forward(offset):
        unused_query, unused_key, value_window, scores = block_scores(offset)
        row_peak = jnp.max(scores, axis=-1, keepdims=True)
        lifted = jnp.exp(scores - row_peak)
        row_total = jnp.sum(lifted, axis=-1, keepdims=True)
        attn_probs = (lifted / row_total).astype(jnp.bfloat16)
        block_out = jnp.einsum(
            "hqk,khd->qhd", attn_probs, value_window, preferred_element_type=as_float
        ).astype(jnp.bfloat16)
        return (block_out, (row_peak + jnp.log(row_total))[..., 0])

    head_out, log_totals = lax.map(block_forward, offsets)
    head_flat = head_out.reshape(span_rows, local_heads * HD)
    attended = lax.all_to_all(head_flat, "seq", split_axis=0, concat_axis=1, tiled=True)
    mixed = jnp.dot(attended, attn_set[5], preferred_element_type=as_float) + attn_set[6].astype(
        as_float
    )
    middle = inputs + mixed
    mlp_set = (
        lax.all_gather(ln2_gain, "fsdp", axis=0, tiled=True),
        lax.all_gather(ln2_bias, "fsdp", axis=0, tiled=True),
        lax.all_gather(w_fc1, "fsdp", axis=0, tiled=True),
        lax.all_gather(fc1_bias, "fsdp", axis=0, tiled=True),
        lax.all_gather(w_fc2, "fsdp", axis=0, tiled=True),
        lax.all_gather(fc2_bias, "fsdp", axis=0, tiled=True),
    )
    gain_two = mlp_set[0].astype(as_float)
    shift_two = mlp_set[1].astype(as_float)
    second_norm = normalize(middle, gain_two, shift_two).astype(jnp.bfloat16)
    hidden = jnp.dot(second_norm, mlp_set[2], preferred_element_type=as_float) + mlp_set[3].astype(
        as_float
    )
    activated = jax.nn.gelu(hidden, approximate=False).astype(jnp.bfloat16)
    branch = jnp.dot(activated, mlp_set[4], preferred_element_type=as_float) + mlp_set[5].astype(
        as_float
    )
    valid = (segment_ids >= 0).astype(as_float)[:, None]
    layer_output = (valid * (middle + branch)).astype(jnp.bfloat16)
    grad_out = valid * cotangent.astype(as_float)
    grad_branch = grad_out.astype(jnp.bfloat16)
    fc2_bias_part = column_sum(grad_branch)
    w_fc2_part = weight_grad(activated, grad_branch)
    grad_act = times_transposed(grad_branch, mlp_set[4])
    unused_hidden, gelu_back = jax.vjp(partial(jax.nn.gelu, approximate=False), hidden)
    grad_hidden = gelu_back(grad_act)[0].astype(jnp.bfloat16)
    fc1_bias_part = column_sum(grad_hidden)
    w_fc1_part = weight_grad(second_norm, grad_hidden)
    grad_norm_two = times_transposed(grad_hidden, mlp_set[2])
    unused_two, norm_two_back = jax.vjp(
        normalize, middle, mlp_set[0].astype(as_float), mlp_set[1].astype(as_float)
    )
    grad_mid_norm, ln2_gain_part, ln2_bias_part = norm_two_back(grad_norm_two)
    grad_middle = grad_out + grad_mid_norm
    grad_mixed = grad_middle.astype(jnp.bfloat16)
    out_bias_part = column_sum(grad_mixed)
    w_out_part = weight_grad(attended, grad_mixed)
    grad_attended = times_transposed(grad_mixed, attn_set[5]).astype(jnp.bfloat16)
    grad_heads = lax.all_to_all(
        grad_attended, "seq", split_axis=1, concat_axis=0, tiled=True
    ).reshape(span_rows, local_heads, HD)

    def block_backward(running, inputs_block):
        key_total, value_total = running
        offset, log_block = inputs_block
        query_block, key_window, value_window, scores = block_scores(offset)
        grad_block = lax.dynamic_slice_in_dim(grad_heads, offset, block_rows, 0)
        probs_full = jnp.exp(scores - log_block[..., None])
        attn_probs = probs_full.astype(jnp.bfloat16)
        value_delta = jnp.einsum(
            "hqk,qhd->khd", attn_probs, grad_block, preferred_element_type=as_float
        )
        grad_probs = jnp.einsum(
            "qhd,khd->hqk", grad_block, value_window, preferred_element_type=as_float
        )
        row_inner = jnp.sum(grad_probs * probs_full, axis=-1, keepdims=True)
        grad_scores = (probs_full * (grad_probs - row_inner)).astype(jnp.bfloat16)
        grad_query = (
            jnp.einsum("hqk,khd->qhd", grad_scores, key_window, preferred_element_type=as_float)
            * scale
        )
        key_delta = (
            jnp.einsum("hqk,qhd->khd", grad_scores, query_block, preferred_element_type=as_float)
            * scale
        )
        return (
            (
                add_window(key_total, key_delta, offset),
                add_window(value_total, value_delta, offset),
            ),
            grad_query,
        )

    zero_heads = jnp.zeros((span_rows + 2 * margin, local_heads, HD), as_float)
    (key_padded_grad, value_padded_grad), query_grad = lax.scan(
        block_backward, (zero_heads, zero_heads), (offsets, log_totals)
    )
    key_grad = key_padded_grad[margin : margin + span_rows]
    value_grad = value_padded_grad[margin : margin + span_rows]
    head_grads = jnp.concatenate(
        [
            query_grad.reshape(span_rows, 1, local_heads * HD),
            key_grad.reshape(span_rows, 1, local_heads * HD),
            value_grad.reshape(span_rows, 1, local_heads * HD),
        ],
        axis=1,
    ).astype(jnp.bfloat16)
    token_grads = lax.all_to_all(
        head_grads, "seq", split_axis=0, concat_axis=2, tiled=True
    ).reshape(row_count, 3 * feature_width)
    q_bias_part = column_sum(token_grads[:, :feature_width])
    v_bias_part = column_sum(token_grads[:, 2 * feature_width :])
    w_qkv_part = weight_grad(first_norm, token_grads)
    grad_norm_one = times_transposed(token_grads, attn_set[2])
    unused_one, norm_one_back = jax.vjp(
        normalize, inputs, attn_set[0].astype(as_float), attn_set[1].astype(as_float)
    )
    grad_input_norm, ln1_gain_part, ln1_bias_part = norm_one_back(grad_norm_one)
    tokens_grad = grad_middle + grad_input_norm
    partial_sums = (
        lax.psum_scatter(
            ln1_gain_part.astype(jnp.bfloat16), "fsdp", scatter_dimension=0, tiled=True
        ).astype(jnp.float32),
        lax.psum_scatter(
            ln1_bias_part.astype(jnp.bfloat16), "fsdp", scatter_dimension=0, tiled=True
        ).astype(jnp.float32),
        lax.psum_scatter(
            w_qkv_part.astype(jnp.bfloat16), "fsdp", scatter_dimension=0, tiled=True
        ).astype(jnp.float32),
        lax.psum_scatter(
            q_bias_part.astype(jnp.bfloat16), "fsdp", scatter_dimension=0, tiled=True
        ).astype(jnp.float32),
        lax.psum_scatter(
            v_bias_part.astype(jnp.bfloat16), "fsdp", scatter_dimension=0, tiled=True
        ).astype(jnp.float32),
        lax.psum_scatter(
            w_out_part.astype(jnp.bfloat16), "fsdp", scatter_dimension=0, tiled=True
        ).astype(jnp.float32),
        lax.psum_scatter(
            out_bias_part.astype(jnp.bfloat16), "fsdp", scatter_dimension=0, tiled=True
        ).astype(jnp.float32),
        lax.psum_scatter(
            ln2_gain_part.astype(jnp.bfloat16), "fsdp", scatter_dimension=0, tiled=True
        ).astype(jnp.float32),
        lax.psum_scatter(
            ln2_bias_part.astype(jnp.bfloat16), "fsdp", scatter_dimension=0, tiled=True
        ).astype(jnp.float32),
        lax.psum_scatter(
            w_fc1_part.astype(jnp.bfloat16), "fsdp", scatter_dimension=0, tiled=True
        ).astype(jnp.float32),
        lax.psum_scatter(
            fc1_bias_part.astype(jnp.bfloat16), "fsdp", scatter_dimension=0, tiled=True
        ).astype(jnp.float32),
        lax.psum_scatter(
            w_fc2_part.astype(jnp.bfloat16), "fsdp", scatter_dimension=0, tiled=True
        ).astype(jnp.float32),
        lax.psum_scatter(
            fc2_bias_part.astype(jnp.bfloat16), "fsdp", scatter_dimension=0, tiled=True
        ).astype(jnp.float32),
    )
    summed = (
        lax.psum_scatter(
            partial_sums[0].astype(jnp.bfloat16), "seq", scatter_dimension=0, tiled=True
        ).astype(jnp.float32),
        lax.psum_scatter(
            partial_sums[1].astype(jnp.bfloat16), "seq", scatter_dimension=0, tiled=True
        ).astype(jnp.float32),
        lax.psum_scatter(
            partial_sums[2].astype(jnp.bfloat16), "seq", scatter_dimension=1, tiled=True
        ).astype(jnp.float32),
        lax.psum_scatter(
            partial_sums[3].astype(jnp.bfloat16), "seq", scatter_dimension=0, tiled=True
        ).astype(jnp.float32),
        lax.psum_scatter(
            partial_sums[4].astype(jnp.bfloat16), "seq", scatter_dimension=0, tiled=True
        ).astype(jnp.float32),
        lax.psum_scatter(
            partial_sums[5].astype(jnp.bfloat16), "seq", scatter_dimension=1, tiled=True
        ).astype(jnp.float32),
        lax.psum_scatter(
            partial_sums[6].astype(jnp.bfloat16), "seq", scatter_dimension=0, tiled=True
        ).astype(jnp.float32),
        lax.psum_scatter(
            partial_sums[7].astype(jnp.bfloat16), "seq", scatter_dimension=0, tiled=True
        ).astype(jnp.float32),
        lax.psum_scatter(
            partial_sums[8].astype(jnp.bfloat16), "seq", scatter_dimension=0, tiled=True
        ).astype(jnp.float32),
        lax.psum_scatter(
            partial_sums[9].astype(jnp.bfloat16), "seq", scatter_dimension=1, tiled=True
        ).astype(jnp.float32),
        lax.psum_scatter(
            partial_sums[10].astype(jnp.bfloat16), "seq", scatter_dimension=0, tiled=True
        ).astype(jnp.float32),
        lax.psum_scatter(
            partial_sums[11].astype(jnp.bfloat16), "seq", scatter_dimension=1, tiled=True
        ).astype(jnp.float32),
        lax.psum_scatter(
            partial_sums[12].astype(jnp.bfloat16), "seq", scatter_dimension=0, tiled=True
        ).astype(jnp.float32),
    )
    return (
        layer_output,
        tokens_grad,
        summed[0],
        summed[1],
        summed[2],
        summed[3],
        summed[4],
        summed[5],
        summed[6],
        summed[7],
        summed[8],
        summed[9],
        summed[10],
        summed[11],
        summed[12],
    )


LX = (0, 4, 2, 6, 1, 5, 3, 7)
LY = (0, 2, 4, 6, 1, 3, 5, 7)
PAIR = ((0, 1), (1, 0), (2, 3), (3, 2))
FAR = ((0, 2), (2, 0), (1, 3), (3, 1))
CROSS = ((0, 3), (3, 0), (1, 2), (2, 1))
BF = jnp.bfloat16
F32 = jnp.float32
RATE = 1.6e9
SMEM_SPEC = pl.BlockSpec(memory_space=pltpu.SMEM)
VMEM_SPEC = pl.BlockSpec(memory_space=pltpu.VMEM)
HALF_ROOT = 0.7071067811865476
DENSITY = 0.3989422804014327


def fshift(values, bit, name="move"):
    with jax.named_scope(name):
        return lax.ppermute(values, "fsdp", [(i, i ^ bit) for i in range(8)])


def zshift(values, pairs, name="move"):
    with jax.named_scope(name):
        return lax.ppermute(values, "seq", pairs)


def after(values, *earlier):
    return lax.optimization_barrier((values, *earlier))[0]


def cost(micros):
    return pl.CostEstimate(flops=int(micros * RATE) + 1, bytes_accessed=1, transcendentals=0)


def call(body, outs, args, scratch=(), micros=1.0, limit=12, space=pltpu.VMEM):
    single = not isinstance(outs, (list, tuple))
    shapes = [outs] if single else list(outs)
    result = pl.pallas_call(
        body,
        out_shape=shapes,
        in_specs=[SMEM_SPEC] + [pl.BlockSpec(memory_space=space)] * (len(args) - 1),
        out_specs=[VMEM_SPEC] * len(shapes),
        scratch_shapes=list(scratch),
        compiler_params=pltpu.CompilerParams(vmem_limit_bytes=limit * 2**20),
        cost_estimate=cost(micros),
    )(*args)
    return result[0] if single else result


def struct(shape, dtype):
    return jax.ShapeDtypeStruct(shape, dtype)


def lanes_low(shape):
    return lax.broadcasted_iota(jnp.int32, shape, 1) < HD


def dot_nn(a, b):
    return lax.dot_general(a, b, (((1,), (0,)), ((), ())), preferred_element_type=F32)


def dot_nt(a, b):
    return lax.dot_general(a, b, (((1,), (1,)), ((), ())), preferred_element_type=F32)


def dot_tn(a, b):
    return lax.dot_general(a, b, (((0,), (0,)), ((), ())), preferred_element_type=F32)


def offset(index, size):
    return pl.multiple_of(index * size, size)


def natural(ref, start):
    return jnp.concatenate([ref[i : i + 1, start : start + 128] for i in range(8)], axis=1)


def pick_qkv(ids, w_hbm, tokens_hbm, wo_hbm, *refs):
    count = (len(refs) - 6) // 2
    rows_hbm, rows, sems = refs[:count], refs[count + 5 : -1], refs[-1]
    out_ref, both_ref, extra_ref, w_ref, wo_ref = refs[count : count + 5]
    half = ids[1] % 2
    cut = tokens_hbm.shape[0] // 2
    copies = [(w_hbm, w_ref), (tokens_hbm.at[pl.ds(cut, cut)], extra_ref)]
    copies += [(wo_hbm.at[pl.ds(offset(half, 64), 64)], wo_ref), *zip(rows_hbm, rows)]
    copies = [pltpu.make_async_copy(source, target, sems.at[i]) for i, (source, target) in enumerate(copies)]
    for copy in copies:
        copy.start()
    for copy in copies:
        copy.wait()
    low = lanes_low((128, 128))
    for j in range(w_ref.shape[1] // 256):
        first = w_ref[:, 256 * j : 256 * j + 128].astype(F32)
        second = w_ref[:, 256 * j + 128 : 256 * j + 256].astype(F32)
        even = jnp.where(low, first, pltpu.roll(second, HD, 1))
        odd = jnp.where(low, pltpu.roll(first, HD, 1), second)
        out_ref[0:128, 128 * j : 128 * j + 128] = jnp.where(half == 0, even, odd).astype(BF)
    start = 0
    for row_ref in rows:
        size = row_ref.shape[0]
        row = row_ref[...].astype(F32)
        out_ref[128:144, start : start + size] = jnp.broadcast_to(row.reshape(1, size), (16, size)).astype(BF)
        start += size
    both_ref[0:144, :] = out_ref[...]
    pack_out(both_ref, 144, wo_ref[...])


def pick_mlp(ids, w1_hbm, w2_hbm, wo_hbm, one_ref, two_ref, sems):
    half = ids[1] % 2
    out_hbm = wo_hbm.at[pl.ds(offset(half, 64), 64)]
    copies = [
        (w2_hbm.at[pl.ds(offset(half, 256), 256)], two_ref.at[pl.ds(0, 256)]),
        (out_hbm, one_ref.at[pl.ds(256, 64)]),
        (out_hbm, two_ref.at[pl.ds(256, 64)]),
    ]
    for b in range(8):
        rows, lanes = pl.ds(128 * (b // 4), 128), pl.ds(256 * (b % 4), 256)
        copies.append((w1_hbm.at[:, pl.ds(offset(2 * b + half, 256), 256)], one_ref.at[rows, lanes]))
    copies = [pltpu.make_async_copy(source, target, sems.at[i]) for i, (source, target) in enumerate(copies)]
    for copy in copies:
        copy.start()
    for copy in copies:
        copy.wait()


def stack_mlp_body(ids, one_ref, one_x_ref, two_ref, two_y_ref, both_ref, one_out, two_out, outs):
    one_out[0:256, :] = one_ref[0:256, :]
    one_out[256:512, :] = one_x_ref[0:256, :]
    two_out[0:256, :] = two_ref[0:256, :]
    two_out[256:512, :] = two_y_ref[0:256, :]
    outs[0:64, :] = one_ref[256:320, :]
    outs[64:128, :] = one_x_ref[256:320, :]
    outs[128:192, :] = two_y_ref[256:320, :]
    for i in range(2):
        lanes = slice(512 * i, 512 * i + 512)
        outs[192:240, lanes] = both_ref[144:192, lanes]
        outs[240:256, lanes] = both_ref[144 + 16 * i : 160 + 16 * i, 1024:1536]


def stack_body(sizes, ids, *refs):
    out_ref = refs[-1]
    start = 0
    for ref, size in zip(refs[:-1], sizes):
        out_ref[start : start + size, :] = ref[0:size, :]
        start += size


def stack(ids, *arrays, sizes=None):
    sizes = sizes or tuple(a.shape[0] for a in arrays)
    shape = struct((sum(sizes), arrays[0].shape[1]), BF)
    return call(partial(stack_body, sizes), shape, (ids, *arrays), micros=0.7)


def place_rows(ids, own_ref, theirs_ref, two_ref, three_ref, out_ref):
    half = ids[1] % 2
    pair = ids[1] // 2
    own_rows = own_ref.shape[0]
    cut = two_ref.shape[0]
    tail = out_ref.shape[0] - own_rows - cut
    for value in range(2):
        first, second = (own_ref, theirs_ref) if value == 0 else (theirs_ref, own_ref)

        @pl.when(half == value)
        def _():
            out_ref[0:own_rows, :] = first[...]

        @pl.when((half == value) & (pair == 0))
        def _():
            out_ref[own_rows:, :] = second[0 : cut + tail, :]

        @pl.when((half == value) & (pair == 1))
        def _():
            out_ref[own_rows + cut :, :] = second[0:tail, :]

    @pl.when(pair == 1)
    def _():
        out_ref[own_rows : own_rows + cut, :] = two_ref[...] + three_ref[...]


def place_grad_body(ids, own_ref, theirs_ref, two_ref, three_ref, out_ref):
    place_rows(ids, own_ref, theirs_ref, two_ref, three_ref, out_ref)
    own_rows = own_ref.shape[0]
    rows = out_ref.shape[0]
    live = key_valid(ids, (rows - own_rows, 1), 0, own_rows, own_rows)
    tail = out_ref[own_rows:, :].astype(F32)
    out_ref[own_rows:, :] = jnp.where(live, tail, 0.0).astype(BF)


def parts_of(refs):
    a, x, y, d, other = refs
    parts = {0: (a, 0), 2: (x, 0), 4: (y, 0), 6: (d, 0)}
    parts.update({2 * i + 1: (other, 144 * i) for i in range(4)})
    return parts


def piece_tile(parts, k, lanes):
    ref, row = parts[k]
    return ref[row : row + 128, lanes]


def qkv_body(ids, own_ref, theirs_ref, two_ref, three_ref, *refs):
    parts = parts_of(refs[:5])
    x_ref, qkv_ref, even_ref, odd_ref, par_ref, norm_ref, bias_ref = refs[5:]
    place_rows(ids, own_ref, theirs_ref, two_ref, three_ref, x_ref)
    f = ids[0]
    half = ids[1] % 2
    rows = x_ref.shape[0]
    for k in range(8):
        ref, at = parts[k]
        par_ref[pl.ds(f ^ k, 1), :] = ref[at + 128 : at + 129, :].astype(F32)
    gain = natural(par_ref, 0)
    shift = natural(par_ref, 128)
    low = lanes_low((1, 128))
    bias_ref[...] = jnp.zeros_like(bias_ref)
    for start, place in ((768, 0), (896, 1024)):
        block = par_ref[:, start : start + 128]
        turned = pltpu.roll(block, HD, 1)
        lower = jnp.where(half == 0, block, turned)
        upper = jnp.where(half == 0, turned, block)
        for j in range(4):
            bias_ref[:, place + 128 * j : place + 128 * j + 128] = jnp.where(
                low, lower[2 * j : 2 * j + 1], upper[2 * j + 1 : 2 * j + 2]
            )

    def norm(i, carry):
        at = pl.ds(offset(i, 32), 32)
        values = x_ref[at, :].astype(F32)
        norm_ref[at, :] = normalize(values, gain, shift).astype(BF)
        return carry

    lax.fori_loop(0, rows // 32, norm, 0, unroll=True)
    for place, k in enumerate(LY):
        target = even_ref if place < 4 else odd_ref
        column = 128 * (place % 4)
        target[:, column : column + 128] = norm_ref[:, pl.ds(offset(f ^ k, 128), 128)]
    left = jnp.concatenate([even_ref[...], odd_ref[...]], axis=1)
    for n in range(6):
        lanes = slice(256 * n, 256 * n + 256)
        weight = jnp.concatenate([piece_tile(parts, k, lanes) for k in LY], axis=0)
        qkv_ref[:, lanes] = (dot_nn(left, weight) + bias_ref[:, lanes]).astype(BF)


def key_valid(ids, shape, axis, own_rows, first=0):
    pair = ids[1] // 2
    place = lax.broadcasted_iota(jnp.int32, shape, axis) + first
    return (place < LEN + pair) & ((place != own_rows) | (pair == 0))


def head_masked(block, head, factor=None):
    wide = block.astype(F32)
    low = lanes_low(wide.shape)
    keep = low if head == 0 else jnp.logical_not(low)
    if factor is not None:
        wide = wide * factor
    return jnp.where(keep, wide, 0.0).astype(BF)


def attend_body(own_rows, tile, ids, qkv_ref, o_ref):
    rows = qkv_ref.shape[0]
    live = key_valid(ids, (1, rows), 1, own_rows)
    low = lanes_low((tile, 128))
    for j in range(4):
        lanes = slice(128 * j, 128 * j + 128)
        key = qkv_ref[:, 512 + 128 * j : 640 + 128 * j]
        value = qkv_ref[:, 1024 + 128 * j : 1152 + 128 * j]
        keys = [head_masked(key, head, HD**-0.5) for head in range(2)]
        for t in range(rows // tile):
            at = slice(t * tile, t * tile + tile)
            outs = []
            for head in range(2):
                scores = jnp.where(live, dot_nt(qkv_ref[at, lanes], keys[head]), masked_score)
                peak = jnp.max(scores, axis=1, keepdims=True)
                lifted = jnp.exp(scores - peak)
                total = jnp.sum(lifted, axis=1, keepdims=True)
                outs.append(dot_nn(lifted.astype(BF), value) / total)
            o_ref[at, lanes] = jnp.where(low, outs[0], outs[1]).astype(BF)


def attend_back_body(own_rows, ids, qkv_ref, g0_ref, g1_ref, gq_ref, gk_ref, gv_ref):
    rows = qkv_ref.shape[0]
    scale = HD**-0.5
    live = key_valid(ids, (rows, 1), 0, own_rows)
    low = lanes_low((rows, 128))
    for j in range(4):
        lanes = slice(128 * j, 128 * j + 128)
        query = qkv_ref[:, lanes]
        key = qkv_ref[:, 512 + 128 * j : 640 + 128 * j]
        value = qkv_ref[:, 1024 + 128 * j : 1152 + 128 * j]
        grad = jnp.concatenate([g0_ref[:, lanes], g1_ref[:, lanes]], axis=0)
        grad_q, grads_k, grads_v = None, [], []
        for head in range(2):
            keys = head_masked(key, head, scale)
            values = head_masked(value, head)
            scores = jnp.where(live, dot_nt(keys, query), masked_score)
            peak = jnp.max(scores, axis=0, keepdims=True)
            lifted = jnp.exp(scores - peak)
            probs = lifted * (1.0 / jnp.sum(lifted, axis=0, keepdims=True))
            grad_p = dot_nt(values, grad)
            inner = jnp.sum(grad_p * probs, axis=0, keepdims=True)
            grad_s = (probs * (grad_p - inner)).astype(BF)
            grads_v.append(dot_nn(probs.astype(BF), grad))
            grads_k.append(dot_nn(grad_s, query) * scale)
            part = dot_tn(grad_s, keys)
            grad_q = part if grad_q is None else grad_q + part
        gq_ref[:, lanes] = grad_q.astype(BF)
        gk_ref[:, lanes] = jnp.where(low, grads_k[0], grads_k[1]).astype(BF)
        gv_ref[:, lanes] = jnp.where(low, grads_v[0], grads_v[1]).astype(BF)


def mixed_body(ids, o_ref, even_ref, odd_ref, first_ref, second_ref, w_ref):
    f = ids[0]
    for place, k in enumerate((0, 2, 4, 6)):
        row = HD * place
        w_ref[pl.ds(offset(f ^ k, HD), HD), :] = even_ref[row : row + HD, :]
        w_ref[pl.ds(offset(f ^ k ^ 1, HD), HD), :] = odd_ref[row : row + HD, :]
    size = first_ref.shape[0]
    for n in range(4):
        lanes = slice(256 * n, 256 * n + 256)
        first_ref[:, lanes] = dot_nn(o_ref[0:size, :], w_ref[:, lanes]).astype(BF)
    for n in range(4):
        lanes = slice(256 * n, 256 * n + 256)
        second_ref[:, lanes] = dot_nn(o_ref[size:, :], w_ref[:, lanes]).astype(BF)


def middle_body(base, ids, par_ref, x_ref, mine_ref, theirs_ref, mid_ref, even_ref, odd_ref, norm_ref):
    f = ids[0]
    rows = mid_ref.shape[0]
    gain = natural(par_ref, 384)
    shift = natural(par_ref, 512)
    bias = natural(par_ref, 256)

    def norm(i, carry):
        at = pl.ds(offset(i, 32), 32)
        middle = x_ref[pl.ds(pl.multiple_of(base + i * 32, 32), 32), :].astype(F32)
        middle = middle + (mine_ref[at, :].astype(F32) + theirs_ref[at, :].astype(F32) + bias)
        mid_ref[at, :] = middle
        norm_ref[at, :] = normalize(middle, gain, shift).astype(BF)
        return carry

    lax.fori_loop(0, rows // 32, norm, 0, unroll=True)
    for place, k in enumerate(LY):
        target = even_ref if place < 4 else odd_ref
        column = 128 * (place % 4)
        target[:, column : column + 128] = norm_ref[:, pl.ds(offset(f ^ k, 128), 128)]


def mlp_body(base, ids, par_ref, even_ref, odd_ref, gm_ref, one_a, one_b, two_a, two_b, *refs):
    act_e_ref, act_o_ref, gu_ref, gh_ref, bias_ref, u_ref, g_ref = refs
    f = ids[0]
    half = ids[1] % 2
    rows = even_ref.shape[0]

    def one_rows(place, start, size, lanes):
        ref = one_a if place < 4 else one_b
        return ref[pl.ds(256 * (place % 4) + start, size), lanes]

    left = jnp.concatenate([even_ref[...], odd_ref[...]], axis=1)
    grad = gm_ref[base : base + rows, :]
    for place, k in enumerate(LX):
        block = f ^ k
        at_lanes = pl.ds(offset(block % 4, 256), 256)
        weight = jnp.concatenate([one_rows(j, offset(block // 4, 128), 128, at_lanes) for j in range(8)], axis=0)
        u_ref[...] = dot_nn(left, weight)
        two_ref = two_a if place < 4 else two_b
        g_ref[...] = dot_nt(grad, two_ref[256 * (place % 4) : 256 * (place % 4) + 256, :])
        row = par_ref[pl.ds(block, 1), pl.ds(offset(4 + half, 256), 256)]
        act_ref = act_e_ref if place < 4 else act_o_ref
        column = 256 * (place % 4)

        def gelu(i, total):
            at = pl.ds(offset(i, 32), 32)
            u = u_ref[at, :] + row
            cdf = 0.5 + 0.5 * lax.erf(u * HALF_ROOT)
            act_ref[at, column : column + 256] = (u * cdf).astype(BF)
            slope = cdf + u * (jnp.exp(-0.5 * (u * u)) * DENSITY)
            gu = (g_ref[at, :] * slope).astype(BF)
            gu_ref[at, pl.ds(offset(block, 256), 256)] = gu
            return total + jnp.sum(gu.astype(F32), axis=0, keepdims=True)

        total = lax.fori_loop(0, rows // 32, gelu, jnp.zeros((1, 256), F32), unroll=True)
        bias_ref[pl.ds(block, 1), :] = total
    for j in range(4):
        total = None
        for part in range(2):
            weight = jnp.concatenate(
                [one_rows(place, 128 * part, 128, slice(None)) for place in (2 * j, 2 * j + 1)], axis=0
            )
            term = dot_nt(gu_ref[:, 1024 * part : 1024 * part + 1024], weight)
            total = term if total is None else total + term
        gh_ref[:, pl.ds(offset(f ^ LY[2 * j], 128), 128)] = total[:, 0:128].astype(BF)
        gh_ref[:, pl.ds(offset(f ^ LY[2 * j + 1], 128), 128)] = total[:, 128:256].astype(BF)


def out_first_body(ids, e_ref, o_ref, two_a, two_b, y_ref):
    left = jnp.concatenate([e_ref[...], o_ref[...]], axis=1)
    for n in range(4):
        lanes = slice(256 * n, 256 * n + 256)
        weight = jnp.concatenate([two_a[:, lanes], two_b[:, lanes]], axis=0)
        y_ref[:, lanes] = dot_nn(left, weight).astype(BF)


def out_body(ids, first_ref, e_ref, o_ref, two_a, two_b, keep_ref, send_ref, y_ref):
    half = ids[1] % 2
    start = first_ref.shape[0]
    y_ref[0:start, :] = first_ref[...]
    left = jnp.concatenate([e_ref[...], o_ref[...]], axis=1)
    for n in range(4):
        lanes = slice(256 * n, 256 * n + 256)
        weight = jnp.concatenate([two_a[:, lanes], two_b[:, lanes]], axis=0)
        y_ref[start:, lanes] = dot_nn(left, weight).astype(BF)
    rows = keep_ref.shape[0]
    shift = y_ref.shape[0] - rows
    keep_ref[...] = y_ref[pl.ds(offset(half, shift), rows), :]
    send_ref[...] = y_ref[pl.ds(offset(1 - half, shift), rows), :]


def result_body(ids, par_ref, mid0_ref, mid1_ref, mine_ref, theirs_ref, out_ref, extra_ref):
    half = ids[1] % 2
    bias = natural(par_ref, 640)
    rows = out_ref.shape[0]
    shift = mid0_ref.shape[0] + mid1_ref.shape[0] - rows

    def step(i, carry):
        at = pl.ds(offset(i, 32), 32)
        place = half * shift + i * 32
        total = mine_ref[at, :].astype(F32) + theirs_ref[at, :].astype(F32) + bias
        size = mid0_ref.shape[0]

        @pl.when(place < size)
        def _():
            out_ref[at, :] = (total + mid0_ref[pl.ds(pl.multiple_of(place, 32), 32), :]).astype(BF)

        @pl.when(place >= size)
        def _():
            out_ref[at, :] = (total + mid1_ref[pl.ds(pl.multiple_of(place - size, 32), 32), :]).astype(BF)

        return carry

    lax.fori_loop(0, rows // 32, step, 0, unroll=True)
    spot = rows - shift
    extra_ref[...] = out_ref[spot : spot + extra_ref.shape[0], :]


def owner_rows_body(ids, valid_ref, full_ref, extra_ref, out_ref):
    half = ids[1] % 2
    pair = ids[1] // 2
    rows, cut = full_ref.shape[0], extra_ref.shape[0]
    tail = 2 * cut + 32 - rows
    shift = cut + tail
    spot = rows - shift
    width = full_ref.shape[1]

    def masked(at, values):
        valid = jnp.concatenate([valid_ref[at, :]] * (width // 128), axis=1)
        return jnp.where(valid > 0.0, values.astype(F32), 0.0).astype(out_ref.dtype)

    @pl.when(half == 0)
    def _():
        out_ref[...] = masked(slice(None), full_ref[...])

    @pl.when((half == 1) & (pair == 0))
    def _():
        top = slice(0, cut)
        out_ref[top, :] = masked(top, full_ref[spot : spot + cut, :])
        low = slice(cut, rows)
        border = full_ref[spot + cut : spot + cut + 1, :].astype(F32)
        first = lax.broadcasted_iota(jnp.int32, (cut, 1), 0) == 0
        out_ref[low, :] = masked(low, jnp.where(first, border, extra_ref[...].astype(F32)))

    @pl.when((half == 1) & (pair == 1))
    def _():
        top = slice(0, tail)
        out_ref[top, :] = masked(top, full_ref[spot + cut : spot + cut + tail, :])
        out_ref[tail:rows, :] = jnp.zeros((rows - tail, width), out_ref.dtype)


def rows_grad_body(step, ids, l0_ref, l1_ref, r0_ref, r1_ref, out_ref):
    rows = l0_ref.shape[0] + l1_ref.shape[0]
    left = jnp.concatenate([l0_ref[...], l1_ref[...]], axis=0)
    for n in range(out_ref.shape[1] // step):
        lanes = slice(step * n, step * n + step)
        if r0_ref.shape[0] == rows:
            right = r0_ref[:, lanes]
        else:
            right = jnp.concatenate([r0_ref[:, lanes], r1_ref[:, lanes]], axis=0)
        out_ref[:, lanes] = dot_tn(left, right).astype(BF)


def norm_back(values, grad, gain):
    center = values - jnp.mean(values, axis=-1, keepdims=True)
    scale = lax.rsqrt(jnp.mean(center * center, axis=-1, keepdims=True) + norm_eps)
    unit = center * scale
    scaled = grad * gain
    first = jnp.mean(scaled, axis=-1, keepdims=True)
    second = jnp.mean(scaled * unit, axis=-1, keepdims=True)
    return unit, scale * (scaled - first - unit * second)


def fold(values):
    total = values[0:8]
    for i in range(1, values.shape[0] // 8):
        total = total + values[8 * i : 8 * i + 8]
    return total


def spread(ref, start, partial_rows):
    row = jnp.sum(partial_rows, axis=0, keepdims=True)
    for i in range(8):
        ref[i : i + 1, start : start + 128] = row[:, 128 * i : 128 * i + 128]


def middle_back_body(base, ids, par_ref, mid_ref, gm_ref, mine_ref, theirs_ref, w_ref, gb_ref, go_ref, sums_ref):
    half = ids[1] % 2
    counts = jnp.where(half == 0, 1.0, 0.0)
    gain = natural(par_ref, 384)
    rows = mid_ref.shape[0]

    def step(i, carry):
        out_sum, gain_sum, shift_sum, last_sum = carry
        at = pl.ds(offset(i, 32), 32)
        mine = mine_ref[at, :].astype(F32)
        grad = mine + theirs_ref[at, :].astype(F32)
        unit, back = norm_back(mid_ref[at, :], grad, gain)
        gm = gm_ref[pl.ds(pl.multiple_of(base + i * 32, 32), 32), :].astype(F32)
        gb = (gm + back).astype(BF)
        gb_ref[at, :] = gb
        return (
            out_sum + fold(gb.astype(F32)),
            gain_sum + fold(mine * unit),
            shift_sum + fold(mine),
            last_sum + fold(gm),
        )

    zero = jnp.zeros((8, mid_ref.shape[1]), F32)
    sums = lax.fori_loop(0, rows // 32, step, (zero, zero, zero, zero), unroll=True)
    spread(sums_ref, 0, sums[0] * counts)
    spread(sums_ref, 128, sums[1])
    spread(sums_ref, 256, sums[2])
    spread(sums_ref, 384, sums[3] * counts)
    grad = gb_ref[...]
    for n in range(2):
        rows = slice(256 * n, 256 * n + 256)
        go_ref[:, rows] = dot_nt(grad, w_ref[rows, :]).astype(BF)


def out_grad_body(ids, o_ref, gb0_ref, gb1_ref, keep_ref, send_ref, grad_ref):
    f = ids[0]
    for n in range(4):
        lanes = slice(256 * n, 256 * n + 256)
        right = jnp.concatenate([gb0_ref[:, lanes], gb1_ref[:, lanes]], axis=0)
        grad_ref[:, lanes] = dot_tn(o_ref[...], right).astype(BF)
    for place, k in enumerate(LX):
        target = keep_ref if place < 4 else send_ref
        row = HD * (place % 4)
        target[row : row + HD, :] = grad_ref[pl.ds(offset(f ^ k, HD), HD), :]


def input_grad_body(ids, x_ref, par_ref, gq_ref, gk_ref, gv_ref, *refs):
    parts = parts_of(refs[:5])
    keep_ref, send_ref, sums_ref, wide_ref, gh_ref = refs[5:]
    f = ids[0]
    left = jnp.concatenate([gq_ref[...], gk_ref[...], gv_ref[...]], axis=1)
    for j in range(4):
        first, second = LY[2 * j], LY[2 * j + 1]
        weight = jnp.concatenate(
            [piece_tile(parts, first, slice(None)), piece_tile(parts, second, slice(None))], axis=0
        )
        total = dot_nt(left, weight)
        wide_ref[:, pl.ds(offset(f ^ first, 128), 128)] = total[:, 0:128]
        wide_ref[:, pl.ds(offset(f ^ second, 128), 128)] = total[:, 128:256]

    def step(i, carry):
        gain_sum, shift_sum = carry
        at = pl.ds(offset(i, 32), 32)
        grad = wide_ref[at, :]
        gh_ref[at, :] = grad.astype(BF)
        values = x_ref[at, :].astype(F32)
        center = values - jnp.mean(values, axis=-1, keepdims=True)
        unit = center * lax.rsqrt(jnp.mean(center * center, axis=-1, keepdims=True) + norm_eps)
        return gain_sum + fold(grad * unit), shift_sum + fold(grad)

    zero = jnp.zeros((8, x_ref.shape[1]), F32)
    gain_sum, shift_sum = lax.fori_loop(0, x_ref.shape[0] // 32, step, (zero, zero), unroll=True)
    half = ids[1] % 2
    rows = keep_ref.shape[0]
    shift = x_ref.shape[0] - rows
    keep_ref[...] = gh_ref[pl.ds(offset(half, shift), rows), :]
    send_ref[...] = gh_ref[pl.ds(offset(1 - half, shift), rows), :]
    spread(sums_ref, 0, gain_sum)
    spread(sums_ref, 128, shift_sum)


def qkv_grad_body(ids, even_ref, odd_ref, gq_ref, gk_ref, gv_ref, one_ref, mid0_ref, mid1_ref, fc0_ref, fc1_ref, *refs):
    keep_ref, send_ref, par_ref = refs
    f = ids[0]
    half = ids[1] % 2
    par_ref[:, 0:256] = one_ref[...]
    par_ref[:, 256:768] = mid0_ref[...] + mid1_ref[...]
    fc_sum = fc0_ref[...] + fc1_ref[...]
    low = lanes_low((1, 128))
    mine = low == (half == 0)
    for g_ref, place in ((gq_ref, 768), (gv_ref, 896)):
        row = jnp.sum(g_ref[...].astype(F32), axis=0, keepdims=True)
        for j in range(4):
            block = row[:, 128 * j : 128 * j + 128]
            turned = pltpu.roll(jnp.broadcast_to(block, (8, 128)), HD, 1)[0:1]
            first = jnp.where(half == 0, block, turned)
            second = jnp.where(half == 0, turned, block)
            par_ref[2 * j : 2 * j + 1, place : place + 128] = jnp.where(mine, first, 0.0)
            par_ref[2 * j + 1 : 2 * j + 2, place : place + 128] = jnp.where(mine, second, 0.0)
    zero = jnp.zeros((8, 256), F32)
    par_ref[:, 1024:1280] = jnp.where(half == 0, fc_sum, zero)
    par_ref[:, 1280:1536] = jnp.where(half == 1, fc_sum, zero)
    order_b = LY
    place_a = {k: i for i, k in enumerate(LX)}
    for j in range(4):
        source = even_ref if j < 2 else odd_ref
        left = source[:, 256 * (j % 2) : 256 * (j % 2) + 256]
        for n, g_ref in enumerate((gq_ref, gk_ref, gv_ref)):
            lanes = slice(512 * n, 512 * n + 512)
            total = dot_tn(left, g_ref[...]).astype(BF)
            for i in range(2):
                k = order_b[2 * j + i]
                target = keep_ref if place_a[k] < 4 else send_ref
                row = 64 * (place_a[k] % 4)
                target[row : row + 64, lanes] = total[128 * i : 128 * i + 64]
                row = 256 + 80 * ((2 * j + i) % 4)
                target[row : row + 64, lanes] = total[128 * i + 64 : 128 * i + 128]
    for place, k in enumerate(order_b):
        target = keep_ref if place < 4 else send_ref
        row = 320 + 80 * (place % 4)
        target[row : row + 16, :] = jnp.broadcast_to(par_ref[pl.ds(f ^ k, 1), :], (16, 1536)).astype(BF)


def input_back_body(ids, par_ref, x_ref, gb0_ref, gb1_ref, mine_ref, theirs_ref, out_ref, extra_ref, gb_ref):
    half = ids[1] % 2
    gain = natural(par_ref, 0)
    rows = out_ref.shape[0]
    shift = x_ref.shape[0] - rows
    size = gb0_ref.shape[0]
    gb_ref[0:size, :] = gb0_ref[...]
    gb_ref[size:, :] = gb1_ref[...]

    def step(i, carry):
        at = pl.ds(offset(i, 32), 32)
        place = pl.ds(pl.multiple_of(half * shift + i * 32, 32), 32)
        grad = mine_ref[at, :].astype(F32) + theirs_ref[at, :].astype(F32)
        back = norm_back(x_ref[place, :].astype(F32), grad, gain)[1]
        out_ref[at, :] = gb_ref[place, :].astype(F32) + back
        return carry

    lax.fori_loop(0, rows // 32, step, 0, unroll=True)
    spot = rows - shift
    extra_ref[...] = out_ref[spot : spot + extra_ref.shape[0], :].astype(BF)


def line_body(ids, ka_ref, ra_ref, kb_ref, rb_ref, ko_ref, *outs):
    s = ids[1]
    wide_a, wide_b, wide_o = outs[4:]
    wide_a[...] = halve(ka_ref[...], ra_ref[0:64, :])
    wide_b[...] = halve(kb_ref[...], rb_ref[...])
    add_packed(wide_o, ko_ref, 0, ra_ref, 64)
    for turn in range(4):
        t = s ^ turn
        lanes = pl.ds(offset(t, 384), 384)
        out_ref = outs[turn]
        out_ref[0:64, :] = wide_a[:, lanes]
        out_ref[64:128, :] = wide_b[0:64, lanes]
        block = jnp.concatenate([wide_b[64:65, 384 * i : 384 * i + 384].astype(F32) for i in range(4)], axis=0)
        block = jnp.concatenate([block, jnp.zeros((12, 384), F32)], axis=0)
        out_ref[128:144, :] = block.astype(BF)
        out_ref[144:192, 0:256] = wide_o[0:48, pl.ds(offset(t, 256), 256)]
        for i in range(2):
            out_ref[144 + 16 * i : 160 + 16 * i, 256:384] = wide_o[48:64, pl.ds(offset(2 * t + i, 128), 128)]
        out_ref[176:192, 256:384] = jnp.zeros((16, 128), BF)


def line_mlp_body(ids, k2_ref, r2_ref, k1_ref, r1_ref, keep_ref, send_ref, two, one):
    s = ids[1]
    two[...] = halve(k2_ref[...], r2_ref[...])
    one[...] = halve(k1_ref[...], r1_ref[...])
    for turn in range(4):
        t = s ^ turn
        out_ref = keep_ref if turn < 2 else send_ref
        at = 512 * (turn % 2)
        out_ref[at : at + 256, :] = two[:, pl.ds(offset(t, 256), 256)]
        for i in range(2):
            row = at + 256 + 128 * i
            out_ref[row : row + 128, :] = one[:, pl.ds(offset(2 * t + i, 256), 256)]


def pack_out(target_ref, row, values):
    for i in range(2):
        lanes = slice(512 * i, 512 * i + 512)
        target_ref[row : row + 48, lanes] = values[0:48, lanes]
        target_ref[row + 16 * i : row + 16 * i + 16, 1024:1536] = values[48:64, lanes]
    target_ref[row + 32 : row + 48, 1024:1536] = jnp.zeros((16, 512), values.dtype)


def merge_body(ids, keep_ref, got_ref, stay_ref, send_ref):
    half = stay_ref.shape[0]
    stay_ref[...] = halve(keep_ref[0:half, :], got_ref[0:half, :])
    send_ref[...] = halve(keep_ref[half:, :], got_ref[half:, :])


def merge(ids, keep, got, micros=0.0):
    shape = struct((keep.shape[0] // 2, keep.shape[1]), BF)
    return call(merge_body, [shape, shape], (ids, keep, got), micros=micros)


def merge_qkv_body(ids, keep_ref, got_ref, ko_ref, ro_ref, stay_a, send_a, stay_b, send_b, stay_o):
    def total(start, size):
        return halve(keep_ref[start : start + size, :], got_ref[start : start + size, :])

    stay_a[...] = total(0, 128)
    send_a[0:128, :] = total(128, 128)
    stay_b[...] = total(256, 160)
    send_b[...] = total(416, 160)
    stay_o[...] = halve(ko_ref[0:128, :], ro_ref[0:128, :])
    for i in range(2):
        rows = slice(128 + 64 * i, 192 + 64 * i)
        pack_out(send_a, 128 + 48 * i, halve(ko_ref[rows, :], ro_ref[rows, :]))


def add_packed(target_ref, keep_ref, row, got_ref, at):
    for i in range(2):
        lanes = slice(512 * i, 512 * i + 512)
        target_ref[0:48, lanes] = halve(keep_ref[row : row + 48, lanes], got_ref[at : at + 48, lanes])
        target_ref[48:64, lanes] = halve(
            keep_ref[row + 48 : row + 64, lanes], got_ref[at + 16 * i : at + 16 * i + 16, 1024:1536]
        )


def merge_last_body(ids, ka_ref, ra_ref, kb_ref, rb_ref, ko_ref, stay_a, send_a, stay_b, send_b, stay_o, wide):
    stay_a[...] = halve(ka_ref[0:64, :], ra_ref[0:64, :])
    send_a[0:64, :] = halve(ka_ref[64:128, :], ra_ref[64:128, :])
    stay_b[...] = halve(kb_ref[0:80, :], rb_ref[0:80, :])
    send_b[...] = halve(kb_ref[80:160, :], rb_ref[80:160, :])
    add_packed(stay_o, ko_ref, 0, ra_ref, 128)
    add_packed(wide, ko_ref, 64, ra_ref, 176)
    pack_out(send_a, 64, wide[...])


def join_mlp_body(ids, own_ref, pair_ref, one_ref, two_ref):
    half = ids[1] % 2
    for ref, place in ((own_ref, half), (pair_ref, 1 - half)):
        two_ref[pl.ds(offset(place, 256), 256), :] = ref[0:256, :].astype(F32)
        for i in range(2):
            lanes = pl.ds(offset(2 * i + place, 256), 256)
            one_ref[:, lanes] = ref[256 + 128 * i : 384 + 128 * i, :].astype(F32)


def join_body(ids, own_ref, pair_ref, far_ref, cross_ref, out_ref, wo_ref, sums_ref, wide_ref):
    s = ids[1]
    half = s % 2
    lower = half == 0
    low = lanes_low((128, 128))

    def sums(rows, lanes):
        same = own_ref[rows, lanes].astype(F32) + far_ref[rows, lanes].astype(F32)
        return same, pair_ref[rows, lanes].astype(F32) + cross_ref[rows, lanes].astype(F32)

    for j in range(3):
        same, other = sums(slice(0, 128), slice(128 * j, 128 * j + 128))
        first = jnp.where(lower, same, other)
        second = jnp.where(lower, other, same)
        out_ref[:, 256 * j : 256 * j + 128] = jnp.where(low, first, pltpu.roll(second, HD, 1))
        out_ref[:, 256 * j + 128 : 256 * j + 256] = jnp.where(low, pltpu.roll(first, HD, 1), second)
    places = [(slice(144, 192), slice(0, 256), 0, slice(0, 256))]
    places += [(slice(144 + 16 * i, 160 + 16 * i), slice(256, 384), 48, slice(128 * i, 128 * i + 128)) for i in range(2)]
    for rows, lanes, row, target in places:
        same, other = sums(rows, lanes)
        size = same.shape[0]
        wo_ref[pl.ds(pl.multiple_of(half * 64 + row, 16), size), target] = same
        wo_ref[pl.ds(pl.multiple_of((1 - half) * 64 + row, 16), size), target] = other
    same, other = sums(slice(128, 144), slice(0, 384))
    total = same + other
    for i in range(4):
        for n in range(3):
            spot = 3 * i + n
            block = total[i : i + 1, 128 * n : 128 * n + 128]
            if spot < 8:
                block = pltpu.roll(jnp.broadcast_to(block, (8, 128)), (128 - 32 * s) % 128, 1)[0:1]
                sums_ref[spot : spot + 1, :] = block
            else:
                wide_ref[spot - 8 : spot - 7, :] = block
    sums_ref[8:9, :] = wide_ref[pl.ds(s, 1), :]


def halve(keep, received):
    return (keep.astype(F32) + received.astype(F32)).astype(BF)


def paired_shards(
    tokens,
    segment_ids,
    ln1_gain,
    ln1_bias,
    w_qkv,
    q_bias,
    v_bias,
    w_out,
    out_bias,
    ln2_gain,
    ln2_bias,
    w_fc1,
    fc1_bias,
    w_fc2,
    fc2_bias,
    cotangent,
):
    own_rows, width = tokens.shape
    cut = own_rows // 2
    tail = 32
    rows = own_rows + cut + tail
    f = lax.axis_index("fsdp")
    s = lax.axis_index("seq")
    ids = jnp.where(lax.iota(jnp.int32, 2) == 0, f, s).astype(jnp.int32)

    def exchange(own, extra, name):
        extra = zshift(extra, ((1, 2),), name + "_extra")
        return zshift(own, PAIR, name), extra, zshift(extra, ((2, 3),), name + "_relay")

    hbm = partial(pltpu.with_memory_space_constraint, memory_space=pltpu.HBM)
    vectors = [ln1_gain, ln1_bias, out_bias, ln2_gain, ln2_bias, fc2_bias, q_bias, v_bias, fc1_bias]
    a, both, tokens_extra = call(
        pick_qkv,
        [struct((144, 1536), BF), struct((192, 1536), BF), struct((own_rows - cut, width), BF)],
        (ids, *[hbm(v) for v in (w_qkv, tokens, w_out, *vectors)]),
        scratch=[
            pltpu.VMEM(w_qkv.shape, BF),
            pltpu.VMEM((64, width), BF),
            *[pltpu.VMEM(v.shape, BF) for v in vectors],
            pltpu.SemaphoreType.DMA((12,)),
        ],
        space=pltpu.HBM, micros=2.2)
    moved_tokens = exchange(tokens, tokens_extra, "tokens")
    one, two = call(
        pick_mlp,
        [struct((320, 1024), BF), struct((320, 1024), BF)],
        (ids, hbm(after(w_fc1, a)), hbm(w_fc2), hbm(w_out)),
        scratch=[pltpu.SemaphoreType.DMA((11,))],
        space=pltpu.HBM, micros=1.9)
    pieces = [a, fshift(a, 2, "qkv_x"), fshift(a, 4, "qkv_y"), fshift(both, 6, "qkv_xy")]
    pieces.append(fshift(stack(ids, after(a, *moved_tokens, one), *pieces[1:], sizes=(144,) * 4), 1, "qkv_core"))

    one_x = fshift(after(one, moved_tokens[0]), 2, "one_x")
    two_y = fshift(after(two, moved_tokens[0]), 4, "two_y")

    one_two, two_two, outs_even = call(
        stack_mlp_body,
        [struct((512, 1024), BF), struct((512, 1024), BF), struct((256, 1024), BF)],
        (ids, one, one_x, two, two_y, pieces[3]), micros=60.0)
    outs_odd = fshift(outs_even, 1, "out_core")
    x, qkv, h1_e, h1_o, par = call(
        qkv_body,
        [
            struct((rows, width), BF),
            struct((rows, 1536), BF),
            struct((rows, 512), BF),
            struct((rows, 512), BF),
            struct((8, 1536), F32),
        ],
        (ids, after(tokens, one_two), *moved_tokens, *pieces),
        scratch=[pltpu.VMEM((rows, 1024), BF), pltpu.VMEM((1, 1536), F32)], micros=6.8)
    valid = segment_ids >= 0
    gm_own = jnp.where(valid[:, None], after(cotangent, *moved_tokens), jnp.zeros_like(cotangent))
    valid_lanes = jnp.broadcast_to(valid[:, None].astype(F32), (own_rows, 128))
    moved_gm = exchange(gm_own, gm_own[cut:], "cotangent")

    heads_o = call(
        partial(attend_body, own_rows, rows // 2), struct((rows, 512), BF), (ids, qkv), micros=7.1, limit=16
    )
    sizes = (320, rows - 320)

    mine_0, mine_1, w_out_full = call(
        mixed_body,
        [struct((sizes[0], width), BF), struct((sizes[1], width), BF), struct((512, width), BF)],
        (ids, heads_o, outs_even, outs_odd), micros=1.4)
    theirs_0 = zshift(mine_0, PAIR, "mixed")
    theirs_1 = zshift(after(mine_1, mine_0), PAIR, "mixed")
    gm = call(place_grad_body, struct((rows, width), BF), (ids, after(gm_own, mine_1), *moved_gm), micros=25.0)
    one_even = stack(ids, after(one_two, gm), fshift(one_two, 4, "one_y"))
    two_even = stack(ids, after(two_two, gm), fshift(two_two, 2, "two_x"))
    weights = (one_even, fshift(one_even, 1, "one_core"), two_even, fshift(two_even, 1, "two_core"))

    def middle(chunk, mine, theirs, micros):
        part = sizes[chunk]
        return call(
            partial(middle_body, chunk * sizes[0]),
            [struct((part, 1024), F32), struct((part, 512), BF), struct((part, 512), BF)],
            (ids, par, x, mine, theirs),
            scratch=[pltpu.VMEM((part, 1024), BF)],
            micros=micros,
        )

    def mlp(chunk, h2_e, h2_o):
        part = sizes[chunk]
        return call(
            partial(mlp_body, chunk * sizes[0]),
            [
                struct((part, 1024), BF),
                struct((part, 1024), BF),
                struct((part, 2048), BF),
                struct((part, 1024), BF),
                struct((8, 256), F32),
            ],
            (ids, par, h2_e, h2_o, gm, *weights),
            scratch=[pltpu.VMEM((part, 256), F32), pltpu.VMEM((part, 256), F32)],
            micros=9.5,
        )

    mid_0, h2_e0, h2_o0 = middle(0, mine_0, theirs_0, 60.0)
    act_e0, act_o0, gu_0, gh2_0, fc1_sums_0 = mlp(0, h2_e0, h2_o0)
    gh2_theirs_0 = zshift(gh2_0, PAIR, "mlp_grad")
    mid_1, h2_e1, h2_o1 = middle(1, after(mine_1, gh2_0), theirs_1, 2.0)
    act_e1, act_o1, gu_1, gh2_1, fc1_sums_1 = mlp(1, h2_e1, h2_o1)
    gh2_theirs_1 = zshift(gh2_1, PAIR, "mlp_grad")

    def row_grad(l0, l1, r0, r1, step):
        return call(
            partial(rows_grad_body, step),
            struct((l0.shape[1], r0.shape[1]), BF),
            (ids, l0, l1, r0, r1), micros=0.0)

    send_two = row_grad(after(act_o0, gh2_1), act_o1, gm, gm, 256)
    got_two = fshift(send_two, 1, "two_grad_core")
    keep_two = row_grad(after(act_e0, send_two), act_e1, gm, gm, 256)
    send_one = row_grad(after(h2_o0, keep_two), h2_o1, gu_0, gu_1, 512)
    got_one = fshift(send_one, 1, "one_grad_core")

    def middle_back(chunk, mid, mine, theirs, micros):
        part = sizes[chunk]
        return call(
            partial(middle_back_body, chunk * sizes[0]),
            [struct((part, 1024), BF), struct((part, 512), BF), struct((8, 512), F32)],
            (ids, par, mid, gm, mine, theirs, w_out_full),
            micros=micros,
        )

    gb_0, go_0, mid_sums_0 = middle_back(0, after(mid_0, send_one), gh2_0, gh2_theirs_0, 60.0)
    stay_two, send_two = merge(ids, after(keep_two, gb_0), got_two)
    got_two = fshift(send_two, 2, "two_grad_x")
    keep_one = row_grad(after(h2_e0, stay_two), h2_e1, gu_0, gu_1, 512)
    stay_one, send_one = merge(ids, keep_one, got_one)
    got_one = fshift(send_one, 4, "one_grad_y")
    y_first = call(
        out_first_body,
        struct((sizes[0], width), BF),
        (ids, after(act_e0, stay_one), act_o0, two_even, weights[3]),
        micros=0.0,
    )
    gb_1, go_1, mid_sums_1 = middle_back(1, after(mid_1, y_first), gh2_1, gh2_theirs_1, 0.0)
    keep_o, send_o = call(
        out_grad_body,
        [struct((256, 1024), BF)] * 2,
        (ids, heads_o, gb_0, gb_1),
        scratch=[pltpu.VMEM((512, 1024), BF)],
        micros=0.0,
    )
    got_o = fshift(send_o, 1, "out_grad_core")
    y_keep, y_send = call(
        out_body,
        [struct((own_rows, width), BF)] * 2,
        (ids, y_first, after(act_e1, keep_o), act_o1, two_even, weights[3]),
        scratch=[pltpu.VMEM((rows, width), BF)],
        micros=0.0,
    )
    y_theirs = zshift(y_send, PAIR, "output")
    gq, gk, gv = call(
        partial(attend_back_body, own_rows),
        [struct((rows, 512), BF)] * 3,
        (ids, qkv, after(go_0, y_keep), go_1),
        micros=0.0,
        limit=20,
    )
    stay_two, send_two = merge(ids, after(stay_two, gq), got_two, micros=1.0)
    got_two = fshift(send_two, 4, "two_grad_y")
    stay_one, send_one = merge(ids, after(stay_one, stay_two), got_one)
    got_one = fshift(send_one, 2, "one_grad_x")
    result, result_extra = call(
        result_body,
        [struct((own_rows, width), BF), struct((cut, width), BF)],
        (ids, par, mid_0, mid_1, after(y_keep, stay_one), y_theirs),
        micros=0.05,
    )
    result_extra = zshift(result_extra, ((3, 1),), "output_rows")
    gh1_keep, gh1_send, one_sums = call(
        input_grad_body,
        [struct((own_rows, 1024), BF), struct((own_rows, 1024), BF), struct((8, 256), F32)],
        (ids, x, par, gq, gk, after(gv, result), *pieces),
        scratch=[pltpu.VMEM((rows, 1024), F32), pltpu.VMEM((rows, 1024), BF)],
        micros=0.2,
    )
    gh1_theirs = zshift(gh1_send, PAIR, "input_grad")
    keep_q, send_q = call(
        qkv_grad_body,
        [struct((576, 1536), BF), struct((576, 1536), BF)],
        (ids, h1_e, h1_o, gq, gk, after(gv, gh1_send), one_sums, mid_sums_0, mid_sums_1, fc1_sums_0, fc1_sums_1),
        scratch=[pltpu.VMEM((8, 1536), F32)],
        micros=0.2,
    )
    got_q = fshift(send_q, 1, "qkv_grad_core")
    mlp_own, mlp_send = call(
        line_mlp_body,
        [struct((1024, 256), BF)] * 2,
        (ids, after(stay_two, keep_q), got_two, stay_one, got_one),
        scratch=[pltpu.VMEM((256, 1024), BF), pltpu.VMEM((128, 2048), BF)],
        micros=0.06,
    )
    mlp_got = zshift(mlp_send, FAR, "mlp_grad_far")
    layer_output = call(
        owner_rows_body,
        struct((own_rows, width), BF),
        (ids, valid_lanes, after(result, mlp_own), result_extra),
        micros=90.0,
    )
    stay_a, send_a, stay_b, send_b, stay_o = call(
        merge_qkv_body,
        [struct((n, 1536), BF) for n in (128, 224, 160, 160)] + [struct((128, 1024), BF)],
        (ids, after(keep_q, layer_output), got_q, keep_o, got_o),
        micros=0.05,
    )
    got_a = fshift(send_a, 2, "qkv_grad_x")
    got_b = fshift(send_b, 4, "qkv_grad_y")
    back, back_extra = call(
        input_back_body,
        [struct((own_rows, width), F32), struct((cut, width), BF)],
        (ids, par, x, gb_0, gb_1, after(gh1_keep, stay_a), gh1_theirs),
        scratch=[pltpu.VMEM((rows, width), BF)],
        micros=0.1,
    )
    back_extra = zshift(back_extra, ((3, 1),), "input_grad_rows")
    last_a, send_a, last_b, send_b, last_o = call(
        merge_last_body,
        [struct((64, 1536), BF), struct((112, 1536), BF)] + [struct((80, 1536), BF)] * 2 + [struct((64, 1024), BF)],
        (ids, after(stay_a, back), got_a, stay_b, got_b, stay_o),
        scratch=[pltpu.VMEM((64, 1024), BF)],
        micros=0.05,
    )
    got_a = fshift(send_a, 4, "qkv_grad_y")
    got_b = fshift(send_b, 2, "qkv_grad_x")
    own, to_pair, to_far, to_cross = call(
        line_body,
        [struct((192, 384), BF)] * 4,
        (ids, last_a, got_a, last_b, got_b, last_o),
        scratch=[pltpu.VMEM((64, 1536), BF), pltpu.VMEM((80, 1536), BF), pltpu.VMEM((64, 1024), BF)],
        micros=0.05,
    )
    got_pair = zshift(to_pair, PAIR, "qkv_grad_z")
    got_far = zshift(to_far, FAR, "qkv_grad_z")
    got_cross = zshift(to_cross, CROSS, "qkv_grad_z")
    mlp_own, mlp_send = merge(ids, after(mlp_own, own), mlp_got, micros=2.0)
    mlp_got = zshift(mlp_send, PAIR, "mlp_grad_pair")
    tokens_grad = call(
        owner_rows_body,
        struct((own_rows, width), F32),
        (ids, valid_lanes, after(back, mlp_own), back_extra),
        micros=0.1,
    )
    w_qkv_grad, w_out_grad, sums = call(
        join_body,
        [struct((128, 768), F32), struct((128, 256), F32), struct((9, 128), F32)],
        (ids, after(own, tokens_grad), got_pair, got_far, got_cross),
        scratch=[pltpu.VMEM((4, 128), F32)],
        micros=0.1,
    )
    w_fc1_grad, w_fc2_grad = call(
        join_mlp_body,
        [struct((128, 1024), F32), struct((512, 256), F32)],
        (ids, after(mlp_own, w_qkv_grad), mlp_got),
        micros=0.1,
    )

    def vector(spot):
        return sums[spot, 0:32]

    return (
        layer_output,
        tokens_grad,
        vector(0),
        vector(1),
        w_qkv_grad,
        vector(6),
        vector(7),
        w_out_grad,
        vector(2),
        vector(3),
        vector(4),
        w_fc1_grad,
        sums[8],
        w_fc2_grad,
        vector(5),
    )


def shards(*operands):
    tokens = operands[0]
    fits = (
        lax.axis_size("fsdp") == 8
        and lax.axis_size("seq") == 4
        and tokens.shape == (384, 1024)
        and operands[11].shape == (128, 4096)
    )
    return paired_shards(*operands) if fits else general_shards(*operands)


def solution(mesh):
    return jax.shard_map(
        shards,
        mesh=mesh,
        in_specs=(
            P(("fsdp", "seq"), None),
            P(("fsdp", "seq")),
            P("fsdp"),
            P("fsdp"),
            P("fsdp", None),
            P("fsdp"),
            P("fsdp"),
            P("fsdp", None),
            P("fsdp"),
            P("fsdp"),
            P("fsdp"),
            P("fsdp", None),
            P("fsdp"),
            P("fsdp", None),
            P("fsdp"),
            P(("fsdp", "seq"), None),
        ),
        out_specs=(
            P(("fsdp", "seq"), None),
            P(("fsdp", "seq"), None),
            P(("fsdp", "seq")),
            P(("fsdp", "seq")),
            P("fsdp", "seq"),
            P(("fsdp", "seq")),
            P(("fsdp", "seq")),
            P("fsdp", "seq"),
            P(("fsdp", "seq")),
            P(("fsdp", "seq")),
            P(("fsdp", "seq")),
            P("fsdp", "seq"),
            P(("fsdp", "seq")),
            P("fsdp", "seq"),
            P(("fsdp", "seq")),
        ),
        check_vma=False,
    )
```
